32 devices in a mesh: chan: 16 (over z, x, core), tm: 2 (over y).
Axes of the slice: x: 2, y: 2, z: 4, core: 2. Of those that a mesh axis runs over, the one named last changes fastest.
Arguments:
- samples: bfloat16 [2, 256, 32, 1024], P(None, 'chan', 'tm'), may hold values from -64 to 64
- steer_index: int32 [256, 256], replicated, may hold values from 0 to 255
Outputs:
- beams: bfloat16 [2, 128, 256, 32], P(None, 'chan', None, 'tm')
The draws below stay inside these ranges and needn't reach their ends.
All inputs are finite; a program needn't handle non-finite values.
Results may differ from the reference program's by a relative error of at most 0.0081.
Values may be sent and summed in bfloat16 or wider, within the bound.
A program may use at most 128 MiB of HBM per device.

```python
import math
import jax
import jax.numpy as jnp
from jax import lax

A = 256
C = 1024
B = 256
PHASES = 256
ITERS = 3
BAND = 128
SNAPS = 32


def draw_samples(key, part):
    keys = jax.random.split(key, 4)
    sources = 8
    phase_angle = jax.random.uniform(keys[0], (sources, A), jnp.float32, -math.pi, math.pi)
    strength = jnp.exp(jax.random.uniform(keys[1], (sources,), jnp.float32, math.log(0.3), math.log(1.0)))
    noise_scale = jnp.exp(jax.random.uniform(keys[2], (A,), jnp.float32, math.log(0.5), math.log(2.0)))
    signal = jax.random.normal(keys[3], (2, sources, SNAPS * C), jnp.float32)
    mix_real = strength[:, None] * jnp.cos(phase_angle)
    mix_imag = strength[:, None] * jnp.sin(phase_angle)

    def one_antenna(antenna):
        noise_key = jax.random.fold_in(key, antenna + 17)
        column_real = mix_real[:, antenna]
        column_imag = mix_imag[:, antenna]
        real_part = jnp.dot(column_real, signal[0]) - jnp.dot(column_imag, signal[1])
        imag_part = jnp.dot(column_real, signal[1]) + jnp.dot(column_imag, signal[0])
        noise = jax.random.normal(noise_key, (2, SNAPS * C), jnp.float32)
        mixed = jnp.stack([real_part, imag_part], 0) + noise_scale[antenna] * noise
        return jnp.clip(mixed, -64.0, 64.0).astype(jnp.bfloat16)
    drawn = lax.map(one_antenna, jnp.arange(A, dtype=jnp.int32))
    return jnp.transpose(drawn, (1, 0, 2)).reshape(2, A, SNAPS, C)


def set_ends(values, stream_key, low, high):
    dims = values.shape
    place = [jax.random.randint(jax.random.fold_in(stream_key, axis), (), 0, dims[axis]) for axis in range(len(dims))]
    values = values.at[tuple(place)].set(low)
    longest = dims.index(max(dims))
    place[longest] = (place[longest] + 1) % dims[longest]
    return values.at[tuple(place)].set(high)


def setup_inputs(seed: int = 0) -> dict:
    splits = jax.random.split(jax.random.key(seed), 3)
    return {
        "samples": draw_samples(jax.random.fold_in(splits[2], 71), 0),
        "steer_index": set_ends(jax.random.randint(splits[1], (B, A), 0, PHASES), jax.random.fold_in(splits[1], 1), 0, PHASES - 1).astype(jnp.int32),
    }


HIGHEST = lax.Precision.HIGHEST

def transform_table(channels_all):
    offset = (C - channels_all) // 2
    channel_number = jnp.arange(channels_all, dtype=jnp.int32) + offset
    sample_number = jnp.arange(C, dtype=jnp.int32)
    phase_turns = channel_number[:, None] * sample_number[None, :] % C
    phase_angle = 2.0 * math.pi / C * phase_turns.astype(jnp.float32)
    window_taper = (0.5 - 0.5 * jnp.cos(2.0 * math.pi / C * sample_number.astype(jnp.float32))) / math.sqrt(C)
    cosine = window_taper[None, :] * jnp.cos(phase_angle)
    sine_part = window_taper[None, :] * jnp.sin(phase_angle)
    coefficients = jnp.stack([jnp.stack([cosine, sine_part], 1), jnp.stack([-sine_part, cosine], 1)], 0)
    return coefficients.astype(jnp.bfloat16)

def complex_product(left_real, left_imag, right_real, right_imag):
    real_part = jnp.dot(left_real, right_real, precision=HIGHEST) - jnp.dot(left_imag, right_imag, precision=HIGHEST)
    imag_part = jnp.dot(left_real, right_imag, precision=HIGHEST) + jnp.dot(left_imag, right_real, precision=HIGHEST)
    return (real_part, imag_part)

def invert_loaded(covariance_real, covariance_imag):
    matrix_order = covariance_real.shape[0]
    loading = 0.1 * jnp.mean(jnp.diagonal(covariance_real))
    identity = jnp.eye(matrix_order, dtype=jnp.float32)
    loaded = covariance_real + loading * identity
    magnitude = jnp.sqrt(loaded * loaded + covariance_imag * covariance_imag)
    largest = jnp.max(lax.optimization_barrier(jnp.sum(magnitude, axis=1)))

    def iterate(counter, state):
        approx_real, approx_imag = state
        image_real, image_imag = complex_product(loaded, covariance_imag, approx_real, approx_imag)
        square_real, square_imag = complex_product(approx_real, approx_imag, image_real, image_imag)
        return (2.0 * approx_real - square_real, 2.0 * approx_imag - square_imag)
    start_state = (identity / largest, jnp.zeros_like(identity))
    return lax.fori_loop(0, ITERS, iterate, start_state)

def form_weights(covariance_real, covariance_imag, steer_real, steer_imag):
    inverse_real, inverse_imag = invert_loaded(covariance_real, covariance_imag)
    gain_real, gain_imag = complex_product(inverse_real, inverse_imag, steer_real, steer_imag)
    response = lax.optimization_barrier(jnp.sum(steer_real * gain_real + steer_imag * gain_imag, axis=0))
    factor = lax.rsqrt(response)
    return ((gain_real * factor).astype(jnp.bfloat16), (gain_imag * factor).astype(jnp.bfloat16))

def steering(steer_index):
    phase_angle = 2.0 * math.pi / PHASES * steer_index.astype(jnp.float32)
    return (jnp.cos(phase_angle).T, jnp.sin(phase_angle).T)

def channel_beams(spectrum, steer_real, steer_imag):
    values = spectrum.astype(jnp.float32)
    outer_sums = jnp.einsum('ins,jms->injm', values, values, precision=HIGHEST)
    covariance_real = (outer_sums[0, :, 0, :] + outer_sums[1, :, 1, :]) / SNAPS
    covariance_imag = (outer_sums[1, :, 0, :] - outer_sums[0, :, 1, :]) / SNAPS
    weight_real, weight_imag = form_weights(covariance_real, covariance_imag, steer_real, steer_imag)
    real_weight = weight_real.astype(jnp.float32)
    imag_weight = weight_imag.astype(jnp.float32)
    beam_real = jnp.einsum('nb,ns->bs', real_weight, values[0], precision=HIGHEST) + jnp.einsum('nb,ns->bs', imag_weight, values[1], precision=HIGHEST)
    beam_imag = jnp.einsum('nb,ns->bs', real_weight, values[1], precision=HIGHEST) - jnp.einsum('nb,ns->bs', imag_weight, values[0], precision=HIGHEST)
    return jnp.stack([beam_real, beam_imag], 0).astype(jnp.bfloat16)

def reference(samples, steer_index):
    coefficients = transform_table(BAND).astype(jnp.float32)

    def antenna_spectra(antenna_samples):
        spectrum = lax.dot_general(coefficients, antenna_samples.astype(jnp.float32), (((2, 3), (0, 2)), ((), ())), precision=HIGHEST)
        return spectrum.astype(jnp.bfloat16)
    per_antenna = lax.map(antenna_spectra, jnp.transpose(samples, (1, 0, 2, 3)))
    by_channel = jnp.transpose(per_antenna, (2, 1, 0, 3))
    steer_real, steer_imag = steering(steer_index)
    beams = lax.map(lambda spectrum: channel_beams(spectrum, steer_real, steer_imag), by_channel)
    return jnp.transpose(beams, (1, 0, 2, 3))
```

```python
import functools
import itertools
import math

import jax
import jax.numpy as jnp
import numpy as np
from jax import lax
from jax.experimental import pallas as pl
from jax.experimental.pallas import tpu as pltpu
from jax.sharding import PartitionSpec as P

C = 1024
PHASES = 256
CH_DEV = 8
ITERS = 3
TERMS = 2**ITERS
LANES = 128


HIGHEST = lax.Precision.HIGHEST
F32 = jnp.float32
BF16 = jnp.bfloat16
NT = (((1,), (1,)), ((), ()))


def transform_table(channels_all):
    offset = (C - channels_all) // 2
    channel_number = jnp.arange(channels_all, dtype=jnp.int32) + offset
    sample_number = jnp.arange(C, dtype=jnp.int32)
    phase_turns = channel_number[:, None] * sample_number[None, :] % C
    phase_angle = 2.0 * math.pi / C * phase_turns.astype(jnp.float32)
    window_taper = (
        0.5 - 0.5 * jnp.cos(2.0 * math.pi / C * sample_number.astype(jnp.float32))
    ) / math.sqrt(C)
    cosine = window_taper[None, :] * jnp.cos(phase_angle)
    sine_part = window_taper[None, :] * jnp.sin(phase_angle)
    coefficients = jnp.stack(
        [jnp.stack([cosine, sine_part], 1), jnp.stack([-sine_part, cosine], 1)], 0
    )
    return coefficients.astype(jnp.bfloat16)


def complex_product(left_real, left_imag, right_real, right_imag):
    real_part = jnp.dot(left_real, right_real, precision=HIGHEST) - jnp.dot(
        left_imag, right_imag, precision=HIGHEST
    )
    imag_part = jnp.dot(left_real, right_imag, precision=HIGHEST) + jnp.dot(
        left_imag, right_real, precision=HIGHEST
    )
    return (real_part, imag_part)


def invert_loaded(covariance_real, covariance_imag):
    matrix_order = covariance_real.shape[0]
    loading = 0.1 * jnp.mean(jnp.diagonal(covariance_real))
    identity = jnp.eye(matrix_order, dtype=jnp.float32)
    loaded = covariance_real + loading * identity
    magnitude = jnp.sqrt(loaded * loaded + covariance_imag * covariance_imag)
    largest = jnp.max(jnp.sum(magnitude, axis=1))

    def iterate(counter, state):
        approx_real, approx_imag = state
        image_real, image_imag = complex_product(loaded, covariance_imag, approx_real, approx_imag)
        square_real, square_imag = complex_product(approx_real, approx_imag, image_real, image_imag)
        return (2.0 * approx_real - square_real, 2.0 * approx_imag - square_imag)

    start_state = (identity / largest, jnp.zeros_like(identity))
    return lax.fori_loop(0, ITERS, iterate, start_state)


def form_weights(covariance_real, covariance_imag, steer_real, steer_imag):
    inverse_real, inverse_imag = invert_loaded(covariance_real, covariance_imag)
    gain_real, gain_imag = complex_product(inverse_real, inverse_imag, steer_real, steer_imag)
    response = jnp.sum(steer_real * gain_real + steer_imag * gain_imag, axis=0)
    factor = lax.rsqrt(response)
    return ((gain_real * factor).astype(jnp.bfloat16), (gain_imag * factor).astype(jnp.bfloat16))


def weights_stacked(covariance_real, covariance_imag, steer_real, steer_imag):
    weight_real, weight_imag = jax.vmap(form_weights, in_axes=(0, 0, None, None))(
        covariance_real, covariance_imag, steer_real, steer_imag
    )
    return jnp.stack([weight_real, weight_imag], 1)


def steering(steer_index):
    phase_angle = 2.0 * math.pi / PHASES * steer_index.astype(jnp.float32)
    return (jnp.cos(phase_angle).T, jnp.sin(phase_angle).T)


def apply_beams(weight_pair, spectrum):
    real_weight = weight_pair[:, 0]
    imag_weight = weight_pair[:, 1]
    beam_real = jnp.einsum(
        "knb,kns->kbs", real_weight, spectrum[0], preferred_element_type=jnp.float32
    ) + jnp.einsum("knb,kns->kbs", imag_weight, spectrum[1], preferred_element_type=jnp.float32)
    beam_imag = jnp.einsum(
        "knb,kns->kbs", real_weight, spectrum[1], preferred_element_type=jnp.float32
    ) - jnp.einsum("knb,kns->kbs", imag_weight, spectrum[0], preferred_element_type=jnp.float32)
    return jnp.stack([beam_real, beam_imag], 0).astype(jnp.bfloat16)


def local(samples, steer_index):
    channels_all = CH_DEV * lax.axis_size("chan")
    coefficients = transform_table(channels_all)
    spectra = lax.dot_general(
        coefficients, samples, (((2, 3), (0, 3)), ((), ())), preferred_element_type=jnp.float32
    ).astype(jnp.bfloat16)
    steer_real, steer_imag = steering(steer_index)
    turned = lax.all_to_all(
        lax.all_to_all(spectra, "chan", split_axis=1, concat_axis=2, tiled=True),
        "tm",
        split_axis=1,
        concat_axis=3,
        tiled=True,
    )
    outer_sums = jnp.einsum("ikns,jkms->kinjm", turned, turned, preferred_element_type=jnp.float32)
    snapshots = turned.shape[3]
    covariance_real = (outer_sums[:, 0, :, 0, :] + outer_sums[:, 1, :, 1, :]) / snapshots
    covariance_imag = (outer_sums[:, 1, :, 0, :] - outer_sums[:, 0, :, 1, :]) / snapshots
    weight_pair = weights_stacked(covariance_real, covariance_imag, steer_real, steer_imag)
    local_beams = apply_beams(weight_pair, turned)
    return lax.all_to_all(local_beams, "tm", split_axis=3, concat_axis=1, tiled=True)


def taper_table(channels_all):
    offset = (C - channels_all) // 2
    channel = np.arange(channels_all) + offset
    sample = np.arange(C)
    angle = 2.0 * math.pi / C * (channel[None, :] * sample[:, None] % C)
    taper = (0.5 - 0.5 * np.cos(2.0 * math.pi / C * sample)) / math.sqrt(C)
    both = np.concatenate([taper[:, None] * np.cos(angle), taper[:, None] * np.sin(angle)], 1)
    return both.astype(np.float32).astype(BF16)


def iota(shape, axis):
    return lax.broadcasted_iota(jnp.int32, shape, axis)


def dot(a, b, dims=(((1,), (0,)), ((), ()))):
    return lax.dot_general(a, b, dims, preferred_element_type=F32)


def split(x):
    high = x.astype(BF16)
    return high, (x - high.astype(F32)).astype(BF16)


def exchange_blocks(rows, count, width):
    lane = iota(rows[0].shape, 1)
    total = count * width
    step = count // 2
    while step:
        low = (lane // width) & step == 0
        done = list(rows)
        for a in range(count):
            if a & step:
                continue
            b = a + step
            up = pltpu.roll(rows[b], step * width, 1)
            down = pltpu.roll(rows[a], total - step * width, 1)
            done[a] = jnp.where(low, rows[a], up)
            done[b] = jnp.where(low, down, rows[b])
        rows = done
        step //= 2
    return rows


def steering_parts(index):
    turn = index & (PHASES - 1)
    quarter = PHASES // 4
    quadrant = (turn + quarter // 2) // quarter
    x = (turn - quarter * quadrant).astype(F32) * (2.0 * math.pi / PHASES)
    y = x * x
    s = x * (1.0 + y * (-1.0 / 6 + y * (1.0 / 120 + y * (-1.0 / 5040 + y * (1.0 / 362880)))))
    c = 1.0 + y * (-0.5 + y * (1.0 / 24 + y * (-1.0 / 720 + y * (1.0 / 40320 - y * (1.0 / 3628800)))))
    odd = quadrant & 1 == 1
    flip_c = (quadrant + 1) & 2 == 2
    flip_s = quadrant & 2 == 2
    cosine = jnp.where(odd, s, c)
    sine = jnp.where(odd, c, s)
    return jnp.where(flip_c, -cosine, cosine), jnp.where(flip_s, -sine, sine)


def fused(ni, nj, samples_hbm, table_hbm, index_hbm, out_ref, samples_ref, table_ref, index_ref, re_ref,
          im_ref, send_ref, recv_ref, steer_ref, load_sem, send_sem, recv_sem):
    nl, t_loc, q = 16, 16, 2 * CH_DEV
    antennas = ni * nl
    size = q * t_loc
    my_i, my_j = lax.axis_index("chan"), lax.axis_index("tm")
    other_j = 1 - my_j

    loads = [pltpu.make_async_copy(src, dst, load_sem.at[i]) for i, (src, dst) in enumerate(
        [(table_hbm, table_ref), (samples_hbm.at[0], samples_ref.at[0]),
         (samples_hbm.at[1], samples_ref.at[1]), (index_hbm, index_ref)])]
    for load in loads:
        load.start()

    barrier = pltpu.get_barrier_semaphore()

    def after(step):
        ahead = my_i + step
        return jnp.where(ahead >= ni, ahead - ni, ahead)

    def around(body):
        lax.fori_loop(1, ni, lambda step, carry: (body(step), carry)[1], 0)

    def greet(peer_i, peer_j):
        pl.semaphore_signal(barrier, inc=1, device_id=(peer_i, peer_j),
                            device_id_type=pl.DeviceIdType.MESH)

    greet(my_i, other_j)

    def greet_both(step):
        greet(after(step), my_j)
        greet(after(step), other_j)

    around(greet_both)

    loads[0].wait()
    table = table_ref[...]
    half = table.shape[1] // 2
    loads[1].wait()
    first = dot(samples_ref[0], table)
    loads[2].wait()
    second = dot(samples_ref[1], table)
    re_ref[...] = first[:, :half] + second[:, half:]
    im_ref[...] = second[:, :half] - first[:, half:]
    parts = []
    for ref in (re_ref, im_ref):
        rows = [ref[pl.ds(t, nl, stride=t_loc), :] for t in range(t_loc)]
        parts.append(exchange_blocks(rows, ni, CH_DEV))
    blocks = jnp.concatenate(
        [jnp.concatenate([a, b], 1) for a, b in zip(*parts)], 0
    ).astype(BF16)
    src, dst = iota((size, size), 0), iota((size, size), 1)
    want = (dst // t_loc % 2) * (t_loc * CH_DEV) + (dst % t_loc) * CH_DEV + dst // (2 * t_loc)
    order = jnp.where(src == want, 1.0, 0.0).astype(BF16)
    send_ref[...] = dot(blocks, order).astype(BF16)

    pl.semaphore_wait(barrier, ni * nj - 1)

    rows_of = lambda i: pl.ds(pl.multiple_of(i * nl, nl), nl)
    mine = rows_of(my_i)

    def block_copy(step, origin, plane):
        peer = after(step)
        return pltpu.make_async_remote_copy(
            src_ref=send_ref.at[rows_of(peer), :],
            dst_ref=recv_ref.at[plane, rows_of(origin), :],
            send_sem=send_sem,
            recv_sem=recv_sem.at[plane],
            device_id=(peer, other_j if plane else my_j),
            device_id_type=pl.DeviceIdType.MESH,
        )

    def send(step):
        block_copy(step, my_i, 0).start()
        block_copy(step, my_i, 1).start()

    block_copy(0, my_i, 1).start()
    around(send)
    recv_ref[0, mine, :] = send_ref[mine, :]

    loads[3].wait()
    cosine, sine = steering_parts(index_ref[...])
    steer_ref[0] = cosine.astype(BF16)
    steer_ref[1] = sine.astype(BF16)

    span = 2 * t_loc
    row_id, col_id = iota((size, size), 0), iota((size, size), 1)
    on_diag = row_id == col_id
    unit = jnp.where(on_diag, 1.0, 0.0).astype(BF16)
    turn_j = jnp.where(row_id == (col_id ^ t_loc), jnp.where(col_id & t_loc == 0, 1.0, -1.0), 0.0).astype(BF16)

    def prepare(plane):
        z = recv_ref[plane]
        zt = dot(unit, z, NT).astype(BF16)
        zj = dot(z, turn_j).astype(BF16)
        zjt = jnp.concatenate(
            [b for i in range(size // span) for b in
             (zt[i * span + t_loc : (i + 1) * span], -zt[i * span : i * span + t_loc])], 0)
        pt = dot(zt, steer_ref[0], NT) + dot(zjt, steer_ref[1], NT)
        return z, zt, zj, zjt, pt

    def sized(ref, plane):
        return pltpu.make_async_remote_copy(
            src_ref=ref, dst_ref=ref, send_sem=send_sem, recv_sem=recv_sem.at[plane],
            device_id=(my_i, other_j), device_id_type=pl.DeviceIdType.MESH)

    sized(recv_ref.at[0, : antennas - nl], 0).wait_recv()
    planes = [prepare(0)]
    sized(recv_ref.at[1], 1).wait_recv()
    planes.append(prepare(1))

    groups = size // LANES
    per = CH_DEV // groups
    cols = nj * LANES
    chan_of = lambda x: x // span % per
    same = chan_of(row_id) == chan_of(col_id)
    lane_chan = chan_of(iota((1, cols), 1))

    def by_channel(values):
        return jnp.concatenate([jnp.broadcast_to(values[i % per], (span, cols)) for i in range(cols // span)], 0)

    half_ants = antennas // 2

    def magnitude(re, im):
        power = re * re + im * im
        return power * lax.rsqrt(jnp.maximum(power, 1e-37))

    def group_steps(g):
        cut = slice(g * LANES, (g + 1) * LANES)
        z = jnp.concatenate([p[0][:, cut] for p in planes], 1)
        zj = jnp.concatenate([p[2][:, cut] for p in planes], 1)
        zt, zjt, pt = (jnp.concatenate([p[i][cut] for p in planes], 0) for i in (1, 3, 4))
        gram = dot(zt, z) + dot(zjt, zj)
        low_t = jnp.concatenate([zt[:, half_ants:], zjt[:, half_ants:]], 1)
        yield
        bounds, rhos = [], []
        for k in range(per):
            yield
            keep = jnp.where(lane_chan == k, 1.0, 0.0).astype(BF16)
            zk = z * keep
            top = magnitude(dot(zk[:half_ants], zt), dot(zj[:half_ants] * keep, zt))
            low = dot(zk[half_ants:], low_t)
            low = magnitude(low[:, :half_ants], low[:, half_ants:])
            rows = jnp.max(jnp.sum(top, axis=1, keepdims=True), axis=0, keepdims=True)
            columns = jnp.sum(top[:, half_ants:], axis=0, keepdims=True) + jnp.sum(low, axis=0, keepdims=True)
            largest = jnp.maximum(rows, jnp.max(columns, axis=1, keepdims=True))
            trace = 0.0
            for j in range(nj):
                at = j * LANES + k * span
                piece = (slice(at, at + span), slice(j * LANES, (j + 1) * LANES))
                trace += jnp.sum(jnp.sum(jnp.where(on_diag[piece], gram[piece], 0.0), axis=0, keepdims=True), axis=1, keepdims=True)
            load = (0.1 / antennas * 0.5) * trace
            bound = largest + load
            bounds.append(bound)
            rhos.append(1.0 - load / bound)
        yield
        sums, fourth = [], []
        for k in range(per):
            s, total = [], 1.0 + 0.0 * rhos[k]
            for m in range(TERMS):
                s.append(total)
                total = 1.0 + rhos[k] * total
            sums.append(s)
            fourth.append(rhos[k] * rhos[k] * rhos[k] * rhos[k])
        each = range(per)
        of = lambda values: by_channel(values)
        rho = of(rhos)
        rho2 = of([r * r for r in rhos])
        inverse = [1.0 / b for b in bounds]
        x1 = jnp.where(same, gram, 0.0) * of(inverse)
        b1 = x1.astype(BF16)
        yield
        x2 = (2.0 * rho) * x1 - dot(b1, b1)
        b2 = x2.astype(BF16)
        yield
        both = dot(jnp.concatenate([b1, b2], 0), b2)
        x3 = rho * x2 + rho2 * x1 - both[:cols]
        x4 = (2.0 * rho2) * x2 - both[cols:]
        b4 = x4.astype(BF16)
        coef = lambda i: [sums[k][TERMS - 2 - i] for k in each]
        tail = of(coef(5)) * x1 + of(coef(6)) * x2
        own = (x1 + x2 + x3)[:LANES]
        yield
        both = dot(jnp.concatenate([tail.astype(BF16), own.astype(BF16)], 0), b4)
        tail0 = [coef(4)[k] + rhos[k] * (coef(5)[k] + rhos[k] * coef(6)[k]) for k in each]
        head0 = [coef(0)[k] + rhos[k] * (coef(1)[k] + rhos[k] * (coef(2)[k] + rhos[k] * coef(3)[k])) for k in each]
        poly0 = [head0[k] + fourth[k] * tail0[k] for k in each]
        poly = (of([coef(1)[k] + fourth[k] * coef(5)[k] for k in each]) * x1
                + of([coef(2)[k] + fourth[k] * coef(6)[k] for k in each]) * x2
                + of(coef(3)) * x3 + of(tail0) * x4 - both[:cols])
        out = (of([1.0 + f for f in fourth])[:LANES] * own + of([s[3] for s in sums])[:LANES] * x4[:LANES] - both[cols:])
        yield
        pth, ptl = split(pt)
        oh, ol = split(out)
        ends = dot(jnp.concatenate([poly.astype(BF16), oh, ol], 0), pth)
        back = (ends[cols : cols + LANES] + ends[cols + LANES :]) + dot(oh, ptl)
        product = pt * (of(poly0) * pt - ends[:cols])
        yield
        for k in range(per):
            at = k * span
            energy = 0.0
            for j in range(nj):
                low = j * LANES + at
                energy += jnp.sum(product[low : low + span], axis=0, keepdims=True)
            whole = sums[k][TERMS - 1]
            response = antennas * whole - energy * inverse[k]
            factor = lax.rsqrt(response) * lax.rsqrt(bounds[k] * (1.0 / (nj * t_loc)))
            beam = (whole * pt[at : at + span] - back[at : at + span]) * factor
            beam = beam.astype(BF16)
            out_ref[0, g * per + k] = beam[:t_loc]
            out_ref[1, g * per + k] = beam[t_loc:]

    for _ in itertools.zip_longest(*[group_steps(g) for g in range(groups)]):
        pass

    sized(send_ref.at[: antennas - nl], 0).wait_send()
    sized(send_ref, 1).wait_send()


def fused_local(ni, nj, samples, steer_index):
    _, nl, t_loc, _ = samples.shape
    beams, antennas = steer_index.shape
    size = 2 * CH_DEV * t_loc
    vmem = pl.BlockSpec(memory_space=pltpu.VMEM)
    table = jnp.asarray(taper_table(CH_DEV * ni))
    out = pl.pallas_call(
        functools.partial(fused, ni, nj),
        out_shape=pltpu.VMEM((2, CH_DEV, t_loc, beams), BF16),
        in_specs=[pl.BlockSpec(memory_space=pl.ANY)] * 3,
        out_specs=vmem,
        scratch_shapes=[
            pltpu.VMEM((2, nl * t_loc, C), BF16),
            pltpu.VMEM(table.shape, BF16),
            pltpu.VMEM((beams, antennas), jnp.int32),
            pltpu.VMEM((nl * t_loc, CH_DEV * ni), F32),
            pltpu.VMEM((nl * t_loc, CH_DEV * ni), F32),
            pltpu.VMEM((antennas, size), BF16),
            pltpu.VMEM((nj, antennas, size), BF16),
            pltpu.VMEM((2, beams, antennas), BF16),
            pltpu.SemaphoreType.DMA((4,)),
            pltpu.SemaphoreType.DMA,
            pltpu.SemaphoreType.DMA((nj,)),
        ],
        compiler_params=pltpu.CompilerParams(collective_id=0, has_side_effects=True),
    )(samples.reshape(2, nl * t_loc, C), table, steer_index)
    return jnp.transpose(out, (0, 1, 3, 2))


def choose(ni, nj, samples, steer_index):
    _, nl, t_loc, _ = samples.shape
    beams, antennas = steer_index.shape
    tiled = nl == 16 and t_loc == 16 and CH_DEV * ni == LANES and antennas == nl * ni
    if tiled and nj == 2:
        return fused_local(ni, nj, samples, steer_index)
    return local(samples, steer_index)


def solution(mesh):
    return jax.shard_map(
        functools.partial(choose, mesh.shape["chan"], mesh.shape["tm"]),
        mesh=mesh,
        in_specs=(P(None, "chan", "tm", None), P()),
        out_specs=P(None, "chan", None, "tm"),
        check_vma=False,
    )
```

```python
import functools
import itertools
import math

import jax
import jax.numpy as jnp
import numpy as np
from jax import lax
from jax.experimental import pallas as pl
from jax.experimental.pallas import tpu as pltpu
from jax.sharding import PartitionSpec as P

C = 1024
PHASES = 256
CH_DEV = 8
ITERS = 3
TERMS = 2**ITERS
LANES = 128


HIGHEST = lax.Precision.HIGHEST
F32 = jnp.float32
BF16 = jnp.bfloat16
NT = (((1,), (1,)), ((), ()))


def transform_table(channels_all):
    offset = (C - channels_all) // 2
    channel_number = jnp.arange(channels_all, dtype=jnp.int32) + offset
    sample_number = jnp.arange(C, dtype=jnp.int32)
    phase_turns = channel_number[:, None] * sample_number[None, :] % C
    phase_angle = 2.0 * math.pi / C * phase_turns.astype(jnp.float32)
    window_taper = (
        0.5 - 0.5 * jnp.cos(2.0 * math.pi / C * sample_number.astype(jnp.float32))
    ) / math.sqrt(C)
    cosine = window_taper[None, :] * jnp.cos(phase_angle)
    sine_part = window_taper[None, :] * jnp.sin(phase_angle)
    coefficients = jnp.stack(
        [jnp.stack([cosine, sine_part], 1), jnp.stack([-sine_part, cosine], 1)], 0
    )
    return coefficients.astype(jnp.bfloat16)


def complex_product(left_real, left_imag, right_real, right_imag):
    real_part = jnp.dot(left_real, right_real, precision=HIGHEST) - jnp.dot(
        left_imag, right_imag, precision=HIGHEST
    )
    imag_part = jnp.dot(left_real, right_imag, precision=HIGHEST) + jnp.dot(
        left_imag, right_real, precision=HIGHEST
    )
    return (real_part, imag_part)


def invert_loaded(covariance_real, covariance_imag):
    matrix_order = covariance_real.shape[0]
    loading = 0.1 * jnp.mean(jnp.diagonal(covariance_real))
    identity = jnp.eye(matrix_order, dtype=jnp.float32)
    loaded = covariance_real + loading * identity
    magnitude = jnp.sqrt(loaded * loaded + covariance_imag * covariance_imag)
    largest = jnp.max(jnp.sum(magnitude, axis=1))

    def iterate(counter, state):
        approx_real, approx_imag = state
        image_real, image_imag = complex_product(loaded, covariance_imag, approx_real, approx_imag)
        square_real, square_imag = complex_product(approx_real, approx_imag, image_real, image_imag)
        return (2.0 * approx_real - square_real, 2.0 * approx_imag - square_imag)

    start_state = (identity / largest, jnp.zeros_like(identity))
    return lax.fori_loop(0, ITERS, iterate, start_state)


def form_weights(covariance_real, covariance_imag, steer_real, steer_imag):
    inverse_real, inverse_imag = invert_loaded(covariance_real, covariance_imag)
    gain_real, gain_imag = complex_product(inverse_real, inverse_imag, steer_real, steer_imag)
    response = jnp.sum(steer_real * gain_real + steer_imag * gain_imag, axis=0)
    factor = lax.rsqrt(response)
    return ((gain_real * factor).astype(jnp.bfloat16), (gain_imag * factor).astype(jnp.bfloat16))


def weights_stacked(covariance_real, covariance_imag, steer_real, steer_imag):
    weight_real, weight_imag = jax.vmap(form_weights, in_axes=(0, 0, None, None))(
        covariance_real, covariance_imag, steer_real, steer_imag
    )
    return jnp.stack([weight_real, weight_imag], 1)


def steering(steer_index):
    phase_angle = 2.0 * math.pi / PHASES * steer_index.astype(jnp.float32)
    return (jnp.cos(phase_angle).T, jnp.sin(phase_angle).T)


def apply_beams(weight_pair, spectrum):
    real_weight = weight_pair[:, 0]
    imag_weight = weight_pair[:, 1]
    beam_real = jnp.einsum(
        "knb,kns->kbs", real_weight, spectrum[0], preferred_element_type=jnp.float32
    ) + jnp.einsum("knb,kns->kbs", imag_weight, spectrum[1], preferred_element_type=jnp.float32)
    beam_imag = jnp.einsum(
        "knb,kns->kbs", real_weight, spectrum[1], preferred_element_type=jnp.float32
    ) - jnp.einsum("knb,kns->kbs", imag_weight, spectrum[0], preferred_element_type=jnp.float32)
    return jnp.stack([beam_real, beam_imag], 0).astype(jnp.bfloat16)


def local(samples, steer_index):
    channels_all = CH_DEV * lax.axis_size("chan")
    coefficients = transform_table(channels_all)
    spectra = lax.dot_general(
        coefficients, samples, (((2, 3), (0, 3)), ((), ())), preferred_element_type=jnp.float32
    ).astype(jnp.bfloat16)
    steer_real, steer_imag = steering(steer_index)
    turned = lax.all_to_all(
        lax.all_to_all(spectra, "chan", split_axis=1, concat_axis=2, tiled=True),
        "tm",
        split_axis=1,
        concat_axis=3,
        tiled=True,
    )
    outer_sums = jnp.einsum("ikns,jkms->kinjm", turned, turned, preferred_element_type=jnp.float32)
    snapshots = turned.shape[3]
    covariance_real = (outer_sums[:, 0, :, 0, :] + outer_sums[:, 1, :, 1, :]) / snapshots
    covariance_imag = (outer_sums[:, 1, :, 0, :] - outer_sums[:, 0, :, 1, :]) / snapshots
    weight_pair = weights_stacked(covariance_real, covariance_imag, steer_real, steer_imag)
    local_beams = apply_beams(weight_pair, turned)
    return lax.all_to_all(local_beams, "tm", split_axis=3, concat_axis=1, tiled=True)


def taper_table(channels_all):
    offset = (C - channels_all) // 2
    channel = np.arange(channels_all) + offset
    sample = np.arange(C)
    angle = 2.0 * math.pi / C * (channel[None, :] * sample[:, None] % C)
    taper = (0.5 - 0.5 * np.cos(2.0 * math.pi / C * sample)) / math.sqrt(C)
    both = np.concatenate([taper[:, None] * np.cos(angle), taper[:, None] * np.sin(angle)], 1)
    return both.astype(np.float32).astype(BF16)


def iota(shape, axis):
    return lax.broadcasted_iota(jnp.int32, shape, axis)


def dot(a, b, dims=(((1,), (0,)), ((), ()))):
    return lax.dot_general(a, b, dims, preferred_element_type=F32)


def split(x):
    high = x.astype(BF16)
    return high, (x - high.astype(F32)).astype(BF16)


def exchange_blocks(rows, count, width):
    lane = iota(rows[0].shape, 1)
    total = count * width
    step = count // 2
    while step:
        low = (lane // width) & step == 0
        done = list(rows)
        for a in range(count):
            if a & step:
                continue
            b = a + step
            up = pltpu.roll(rows[b], step * width, 1)
            down = pltpu.roll(rows[a], total - step * width, 1)
            done[a] = jnp.where(low, rows[a], up)
            done[b] = jnp.where(low, down, rows[b])
        rows = done
        step //= 2
    return rows


def steering_parts(index):
    turn = index & (PHASES - 1)
    quarter = PHASES // 4
    quadrant = (turn + quarter // 2) // quarter
    x = (turn - quarter * quadrant).astype(F32) * (2.0 * math.pi / PHASES)
    y = x * x
    s = x * (1.0 + y * (-1.0 / 6 + y * (1.0 / 120 + y * (-1.0 / 5040 + y * (1.0 / 362880)))))
    c = 1.0 + y * (-0.5 + y * (1.0 / 24 + y * (-1.0 / 720 + y * (1.0 / 40320 - y * (1.0 / 3628800)))))
    odd = quadrant & 1 == 1
    flip_c = (quadrant + 1) & 2 == 2
    flip_s = quadrant & 2 == 2
    cosine = jnp.where(odd, s, c)
    sine = jnp.where(odd, c, s)
    return jnp.where(flip_c, -cosine, cosine), jnp.where(flip_s, -sine, sine)


def fused(ni, nj, samples_hbm, table_hbm, index_hbm, out_ref, samples_ref, table_ref, index_ref, re_ref,
          im_ref, send_ref, recv_ref, steer_ref, load_sem, send_sem, recv_sem):
    nl, t_loc, q = 16, 16, 2 * CH_DEV
    antennas = ni * nl
    size = q * t_loc
    my_i, my_j = lax.axis_index("chan"), lax.axis_index("tm")
    other_j = 1 - my_j

    loads = [pltpu.make_async_copy(src, dst, load_sem.at[i]) for i, (src, dst) in enumerate(
        [(table_hbm, table_ref), (samples_hbm.at[0], samples_ref.at[0]),
         (samples_hbm.at[1], samples_ref.at[1]), (index_hbm, index_ref)])]
    for load in loads:
        load.start()

    barrier = pltpu.get_barrier_semaphore()

    def after(step):
        ahead = my_i + step
        return jnp.where(ahead >= ni, ahead - ni, ahead)

    def around(body):
        lax.fori_loop(1, ni, lambda step, carry: (body(step), carry)[1], 0)

    def greet(peer_i, peer_j):
        pl.semaphore_signal(barrier, inc=1, device_id=(peer_i, peer_j),
                            device_id_type=pl.DeviceIdType.MESH)

    greet(my_i, other_j)

    def greet_both(step):
        greet(after(step), my_j)
        greet(after(step), other_j)

    around(greet_both)

    loads[0].wait()
    table = table_ref[...]
    half = table.shape[1] // 2
    loads[1].wait()
    first = dot(samples_ref[0], table)
    loads[2].wait()
    second = dot(samples_ref[1], table)
    re_ref[...] = first[:, :half] + second[:, half:]
    im_ref[...] = second[:, :half] - first[:, half:]
    parts = []
    for ref in (re_ref, im_ref):
        rows = [ref[pl.ds(t, nl, stride=t_loc), :] for t in range(t_loc)]
        parts.append(exchange_blocks(rows, ni, CH_DEV))
    blocks = jnp.concatenate(
        [jnp.concatenate([a, b], 1) for a, b in zip(*parts)], 0
    ).astype(BF16)
    src, dst = iota((size, size), 0), iota((size, size), 1)
    want = (dst // t_loc % 2) * (t_loc * CH_DEV) + (dst % t_loc) * CH_DEV + dst // (2 * t_loc)
    order = jnp.where(src == want, 1.0, 0.0).astype(BF16)
    send_ref[...] = dot(blocks, order).astype(BF16)

    pl.semaphore_wait(barrier, ni * nj - 1)

    rows_of = lambda i: pl.ds(pl.multiple_of(i * nl, nl), nl)
    mine = rows_of(my_i)

    def block_copy(step, origin, plane):
        peer = after(step)
        return pltpu.make_async_remote_copy(
            src_ref=send_ref.at[rows_of(peer), :],
            dst_ref=recv_ref.at[plane, rows_of(origin), :],
            send_sem=send_sem,
            recv_sem=recv_sem.at[plane],
            device_id=(peer, other_j if plane else my_j),
            device_id_type=pl.DeviceIdType.MESH,
        )

    def send(step):
        block_copy(step, my_i, 0).start()
        block_copy(step, my_i, 1).start()

    block_copy(0, my_i, 1).start()
    around(send)
    recv_ref[0, mine, :] = send_ref[mine, :]

    loads[3].wait()
    cosine, sine = steering_parts(index_ref[...])
    steer_ref[0] = cosine.astype(BF16)
    steer_ref[1] = sine.astype(BF16)

    span = 2 * t_loc
    row_id, col_id = iota((size, size), 0), iota((size, size), 1)
    on_diag = row_id == col_id
    unit = jnp.where(on_diag, 1.0, 0.0).astype(BF16)
    turn_j = jnp.where(row_id == (col_id ^ t_loc), jnp.where(col_id & t_loc == 0, 1.0, -1.0), 0.0).astype(BF16)

    def prepare(plane):
        z = recv_ref[plane]
        zt = dot(unit, z, NT).astype(BF16)
        zj = dot(z, turn_j).astype(BF16)
        zjt = jnp.concatenate(
            [b for i in range(size // span) for b in
             (zt[i * span + t_loc : (i + 1) * span], -zt[i * span : i * span + t_loc])], 0)
        pt = dot(zt, steer_ref[0], NT) + dot(zjt, steer_ref[1], NT)
        return z, zt, zj, zjt, pt

    def sized(ref, plane):
        return pltpu.make_async_remote_copy(
            src_ref=ref, dst_ref=ref, send_sem=send_sem, recv_sem=recv_sem.at[plane],
            device_id=(my_i, other_j), device_id_type=pl.DeviceIdType.MESH)

    sized(recv_ref.at[0, : antennas - nl], 0).wait_recv()
    planes = [prepare(0)]
    sized(recv_ref.at[1], 1).wait_recv()
    planes.append(prepare(1))

    groups = size // LANES
    per = CH_DEV // groups
    cols = nj * LANES
    wide = nj * span
    chan_of = lambda x: x // span % per
    lane_chan = chan_of(iota((1, cols), 1))
    half_ants = antennas // 2
    blocks = range(cols // span)
    rows_at = lambda i: slice(i * span, (i + 1) * span)
    lane = iota((span, LANES), 1)
    slot = lane // span
    packed_slot = iota((span, LANES), 1) // span
    first = iota((cols, LANES), 1) < wide

    def shifted(x, amount):
        return x if amount % LANES == 0 else pltpu.roll(x, amount % LANES, 1)

    def pack(grams):
        done = []
        for i in blocks:
            kept = None
            for g in range(groups):
                for j in range(nj):
                    to = g * nj + j
                    moved = shifted(grams[g][rows_at(i), j * LANES : (j + 1) * LANES], (to - i % per) * span)
                    kept = moved if kept is None else jnp.where(slot == to, moved, kept)
            done.append(kept)
        return jnp.concatenate(done, 0)

    def spread(x, g):
        done = []
        for i in range(x.shape[0] // span):
            k = i % per
            done.append(jnp.concatenate(
                [jnp.where(packed_slot == k, shifted(x[rows_at(i)], (k - g * nj - j) * span), 0.0).astype(BF16)
                 for j in range(nj)], 1))
        return jnp.concatenate(done, 0)

    def spread_all(x):
        return jnp.concatenate([spread(x, g) for g in range(groups)], 0)

    def pick(out):
        return jnp.where(first, out[:cols], out[cols:])

    def magnitude(re, im):
        power = re * re + im * im
        return power * lax.rsqrt(jnp.maximum(power, 1e-37))

    def group_steps(g, keepers):
        cut = slice(g * LANES, (g + 1) * LANES)
        z = jnp.concatenate([p[0][:, cut] for p in planes], 1)
        zj = jnp.concatenate([p[2][:, cut] for p in planes], 1)
        zt, zjt, pt = (jnp.concatenate([p[i][cut] for p in planes], 0) for i in (1, 3, 4))
        keepers["gram"][g] = dot(zt, z) + dot(zjt, zj)
        keepers["pt"][g] = pt
        low_t = jnp.concatenate([zt[:, half_ants:], zjt[:, half_ants:]], 1)
        yield
        for k in range(per):
            yield
            keep = jnp.where(lane_chan == k, 1.0, 0.0).astype(BF16)
            zk = z * keep
            top = magnitude(dot(zk[:half_ants], zt), dot(zj[:half_ants] * keep, zt))
            low = dot(zk[half_ants:], low_t)
            low = magnitude(low[:, :half_ants], low[:, half_ants:])
            rows = jnp.max(jnp.sum(top, axis=1, keepdims=True), axis=0, keepdims=True)
            columns = jnp.sum(top[:, half_ants:], axis=0, keepdims=True) + jnp.sum(low, axis=0, keepdims=True)
            keepers["largest"][g][k] = jnp.maximum(rows, jnp.max(columns, axis=1, keepdims=True))

    kept = {"gram": {}, "pt": {}, "largest": [{}, {}]}
    for _ in itertools.zip_longest(*[group_steps(g, kept) for g in range(groups)]):
        pass

    gram = pack(kept["gram"])
    gram_b = gram.astype(BF16)
    square = pick(dot(spread_all(gram), gram_b))

    lane_row = iota((1, LANES), 1)
    on_diag = iota((cols, LANES), 1) % wide == iota((cols, LANES), 0) // LANES * span + iota((cols, LANES), 0) % span
    diagonal = jnp.where(on_diag, gram, 0.0)
    bounds, rhos = [{}, {}], [{}, {}]
    rows_rho, rows_inverse = [], []
    for k in range(per):
        both = jnp.sum(diagonal[rows_at(k)] + diagonal[rows_at(per + k)], axis=0, keepdims=True)
        for g in range(groups):
            trace = jnp.sum(jnp.where(lane_row // wide == g, both, 0.0), axis=1, keepdims=True)
            load = (0.1 / antennas * 0.5) * trace
            bound = kept["largest"][g][k] + load
            bounds[g][k] = bound
            rhos[g][k] = 1.0 - load / bound
        rows_rho.append(jnp.where(lane_row < wide, rhos[0][k], rhos[1][k]))
        rows_inverse.append(1.0 / jnp.where(lane_row < wide, bounds[0][k], bounds[1][k]))
    r = jnp.concatenate(rows_rho * nj, 0)
    inv = jnp.concatenate(rows_inverse * nj, 0)
    r2 = r * r
    r4 = r2 * r2
    s = [1.0 + 0.0 * r]
    for _ in range(TERMS - 1):
        s.append(1.0 + r * s[-1])
    c = [s[TERMS - 2 - m] for m in range(TERMS - 1)]
    t0 = c[4] + r * (c[5] + r * c[6])
    p0 = c[0] + r * (c[1] + r * (c[2] + r * c[3])) + r4 * t0

    def by(v, count=cols):
        return jnp.concatenate([jnp.broadcast_to(v[i : i + 1], (span, LANES)) for i in range(count // span)], 0)

    x1 = by(inv) * gram
    x2 = by(2.0 * r) * x1 - by(inv * inv) * square
    out = dot(spread_all(x2), jnp.concatenate([x1.astype(BF16), x2.astype(BF16)], 1))
    x3 = by(r) * x2 + by(r2) * x1 - pick(out[:, :LANES])
    x4 = by(2.0 * r2) * x2 - pick(out[:, LANES:])
    tail = by(c[5]) * x1 + by(c[6]) * x2
    head = x1 + x2 + x3
    out = dot(spread_all(x4), jnp.concatenate([tail.astype(BF16), head.astype(BF16)], 1))
    poly = (by(c[1] + r4 * c[5]) * x1 + by(c[2] + r4 * c[6]) * x2 + by(c[3]) * x3 + by(t0) * x4
            - pick(out[:, :LANES]))
    own = (by(1.0 + r4, LANES) * head[:LANES] + by(s[3], LANES) * x4[:LANES]
           - jnp.where(first[:LANES], out[:LANES, LANES:], out[cols : cols + LANES, LANES:]))
    own_low = own - own.astype(BF16).astype(F32)

    for g in range(groups):
        pt = kept["pt"][g]
        pth, ptl = split(pt)
        oh = spread(own, g)
        ends = dot(jnp.concatenate([spread(poly, g), oh, spread(own_low, g)], 0), pth)
        back = (ends[cols : cols + LANES] + ends[cols + LANES :]) + dot(oh, ptl)
        for k in range(per):
            energy = 0.0
            at = slice(k, k + 1), slice(g * wide, g * wide + 1)
            for j in range(nj):
                low = rows_at(j * per + k)
                energy += jnp.sum(pt[low] * (p0[at] * pt[low] - ends[low]), axis=0, keepdims=True)
            bound, whole = bounds[g][k], s[TERMS - 1][at]
            response = antennas * whole - energy * inv[at]
            factor = lax.rsqrt(response) * lax.rsqrt(bound * (1.0 / (nj * t_loc)))
            beam = (whole * pt[rows_at(k)] - back[rows_at(k)]) * factor
            beam = beam.astype(BF16)
            out_ref[0, g * per + k] = beam[:t_loc]
            out_ref[1, g * per + k] = beam[t_loc:]

    sized(send_ref.at[: antennas - nl], 0).wait_send()
    sized(send_ref, 1).wait_send()


def fused_local(ni, nj, samples, steer_index):
    _, nl, t_loc, _ = samples.shape
    beams, antennas = steer_index.shape
    size = 2 * CH_DEV * t_loc
    vmem = pl.BlockSpec(memory_space=pltpu.VMEM)
    table = jnp.asarray(taper_table(CH_DEV * ni))
    out = pl.pallas_call(
        functools.partial(fused, ni, nj),
        out_shape=pltpu.VMEM((2, CH_DEV, t_loc, beams), BF16),
        in_specs=[pl.BlockSpec(memory_space=pl.ANY)] * 3,
        out_specs=vmem,
        scratch_shapes=[
            pltpu.VMEM((2, nl * t_loc, C), BF16),
            pltpu.VMEM(table.shape, BF16),
            pltpu.VMEM((beams, antennas), jnp.int32),
            pltpu.VMEM((nl * t_loc, CH_DEV * ni), F32),
            pltpu.VMEM((nl * t_loc, CH_DEV * ni), F32),
            pltpu.VMEM((antennas, size), BF16),
            pltpu.VMEM((nj, antennas, size), BF16),
            pltpu.VMEM((2, beams, antennas), BF16),
            pltpu.SemaphoreType.DMA((4,)),
            pltpu.SemaphoreType.DMA,
            pltpu.SemaphoreType.DMA((nj,)),
        ],
        compiler_params=pltpu.CompilerParams(collective_id=0, has_side_effects=True),
    )(samples.reshape(2, nl * t_loc, C), table, steer_index)
    return jnp.transpose(out, (0, 1, 3, 2))


def choose(ni, nj, samples, steer_index):
    _, nl, t_loc, _ = samples.shape
    beams, antennas = steer_index.shape
    tiled = nl == 16 and t_loc == 16 and CH_DEV * ni == LANES and antennas == nl * ni
    if tiled and nj == 2:
        return fused_local(ni, nj, samples, steer_index)
    return local(samples, steer_index)


def solution(mesh):
    return jax.shard_map(
        functools.partial(choose, mesh.shape["chan"], mesh.shape["tm"]),
        mesh=mesh,
        in_specs=(P(None, "chan", "tm", None), P()),
        out_specs=P(None, "chan", None, "tm"),
        check_vma=False,
    )
```

```python
import functools
import itertools
import math

import jax
import jax.numpy as jnp
import numpy as np
from jax import lax
from jax.experimental import pallas as pl
from jax.experimental.pallas import tpu as pltpu
from jax.sharding import PartitionSpec as P

C = 1024
PHASES = 256
CH_DEV = 8
ITERS = 3
TERMS = 2**ITERS
LANES = 128


HIGHEST = lax.Precision.HIGHEST
F32 = jnp.float32
BF16 = jnp.bfloat16
NT = (((1,), (1,)), ((), ()))


def transform_table(channels_all):
    offset = (C - channels_all) // 2
    channel_number = jnp.arange(channels_all, dtype=jnp.int32) + offset
    sample_number = jnp.arange(C, dtype=jnp.int32)
    phase_turns = channel_number[:, None] * sample_number[None, :] % C
    phase_angle = 2.0 * math.pi / C * phase_turns.astype(jnp.float32)
    window_taper = (
        0.5 - 0.5 * jnp.cos(2.0 * math.pi / C * sample_number.astype(jnp.float32))
    ) / math.sqrt(C)
    cosine = window_taper[None, :] * jnp.cos(phase_angle)
    sine_part = window_taper[None, :] * jnp.sin(phase_angle)
    coefficients = jnp.stack(
        [jnp.stack([cosine, sine_part], 1), jnp.stack([-sine_part, cosine], 1)], 0
    )
    return coefficients.astype(jnp.bfloat16)


def complex_product(left_real, left_imag, right_real, right_imag):
    real_part = jnp.dot(left_real, right_real, precision=HIGHEST) - jnp.dot(
        left_imag, right_imag, precision=HIGHEST
    )
    imag_part = jnp.dot(left_real, right_imag, precision=HIGHEST) + jnp.dot(
        left_imag, right_real, precision=HIGHEST
    )
    return (real_part, imag_part)


def invert_loaded(covariance_real, covariance_imag):
    matrix_order = covariance_real.shape[0]
    loading = 0.1 * jnp.mean(jnp.diagonal(covariance_real))
    identity = jnp.eye(matrix_order, dtype=jnp.float32)
    loaded = covariance_real + loading * identity
    magnitude = jnp.sqrt(loaded * loaded + covariance_imag * covariance_imag)
    largest = jnp.max(jnp.sum(magnitude, axis=1))

    def iterate(counter, state):
        approx_real, approx_imag = state
        image_real, image_imag = complex_product(loaded, covariance_imag, approx_real, approx_imag)
        square_real, square_imag = complex_product(approx_real, approx_imag, image_real, image_imag)
        return (2.0 * approx_real - square_real, 2.0 * approx_imag - square_imag)

    start_state = (identity / largest, jnp.zeros_like(identity))
    return lax.fori_loop(0, ITERS, iterate, start_state)


def form_weights(covariance_real, covariance_imag, steer_real, steer_imag):
    inverse_real, inverse_imag = invert_loaded(covariance_real, covariance_imag)
    gain_real, gain_imag = complex_product(inverse_real, inverse_imag, steer_real, steer_imag)
    response = jnp.sum(steer_real * gain_real + steer_imag * gain_imag, axis=0)
    factor = lax.rsqrt(response)
    return ((gain_real * factor).astype(jnp.bfloat16), (gain_imag * factor).astype(jnp.bfloat16))


def weights_stacked(covariance_real, covariance_imag, steer_real, steer_imag):
    weight_real, weight_imag = jax.vmap(form_weights, in_axes=(0, 0, None, None))(
        covariance_real, covariance_imag, steer_real, steer_imag
    )
    return jnp.stack([weight_real, weight_imag], 1)


def steering(steer_index):
    phase_angle = 2.0 * math.pi / PHASES * steer_index.astype(jnp.float32)
    return (jnp.cos(phase_angle).T, jnp.sin(phase_angle).T)


def apply_beams(weight_pair, spectrum):
    real_weight = weight_pair[:, 0]
    imag_weight = weight_pair[:, 1]
    beam_real = jnp.einsum(
        "knb,kns->kbs", real_weight, spectrum[0], preferred_element_type=jnp.float32
    ) + jnp.einsum("knb,kns->kbs", imag_weight, spectrum[1], preferred_element_type=jnp.float32)
    beam_imag = jnp.einsum(
        "knb,kns->kbs", real_weight, spectrum[1], preferred_element_type=jnp.float32
    ) - jnp.einsum("knb,kns->kbs", imag_weight, spectrum[0], preferred_element_type=jnp.float32)
    return jnp.stack([beam_real, beam_imag], 0).astype(jnp.bfloat16)


def local(samples, steer_index):
    channels_all = CH_DEV * lax.axis_size("chan")
    coefficients = transform_table(channels_all)
    spectra = lax.dot_general(
        coefficients, samples, (((2, 3), (0, 3)), ((), ())), preferred_element_type=jnp.float32
    ).astype(jnp.bfloat16)
    steer_real, steer_imag = steering(steer_index)
    turned = lax.all_to_all(
        lax.all_to_all(spectra, "chan", split_axis=1, concat_axis=2, tiled=True),
        "tm",
        split_axis=1,
        concat_axis=3,
        tiled=True,
    )
    outer_sums = jnp.einsum("ikns,jkms->kinjm", turned, turned, preferred_element_type=jnp.float32)
    snapshots = turned.shape[3]
    covariance_real = (outer_sums[:, 0, :, 0, :] + outer_sums[:, 1, :, 1, :]) / snapshots
    covariance_imag = (outer_sums[:, 1, :, 0, :] - outer_sums[:, 0, :, 1, :]) / snapshots
    weight_pair = weights_stacked(covariance_real, covariance_imag, steer_real, steer_imag)
    local_beams = apply_beams(weight_pair, turned)
    return lax.all_to_all(local_beams, "tm", split_axis=3, concat_axis=1, tiled=True)


def taper_table(channels_all):
    offset = (C - channels_all) // 2
    channel = np.arange(channels_all) + offset
    sample = np.arange(C)
    angle = 2.0 * math.pi / C * (channel[None, :] * sample[:, None] % C)
    taper = (0.5 - 0.5 * np.cos(2.0 * math.pi / C * sample)) / math.sqrt(C)
    both = np.concatenate([taper[:, None] * np.cos(angle), taper[:, None] * np.sin(angle)], 1)
    return both.astype(np.float32).astype(BF16)


def iota(shape, axis):
    return lax.broadcasted_iota(jnp.int32, shape, axis)


def dot(a, b, dims=(((1,), (0,)), ((), ()))):
    return lax.dot_general(a, b, dims, preferred_element_type=F32)


def split(x):
    high = x.astype(BF16)
    return high, (x - high.astype(F32)).astype(BF16)


def exchange_blocks(rows, count, width):
    lane = iota(rows[0].shape, 1)
    total = count * width
    step = count // 2
    while step:
        low = (lane // width) & step == 0
        done = list(rows)
        for a in range(count):
            if a & step:
                continue
            b = a + step
            up = pltpu.roll(rows[b], step * width, 1)
            down = pltpu.roll(rows[a], total - step * width, 1)
            done[a] = jnp.where(low, rows[a], up)
            done[b] = jnp.where(low, down, rows[b])
        rows = done
        step //= 2
    return rows


def steering_parts(index):
    turn = index & (PHASES - 1)
    quarter = PHASES // 4
    quadrant = (turn + quarter // 2) // quarter
    x = (turn - quarter * quadrant).astype(F32) * (2.0 * math.pi / PHASES)
    y = x * x
    s = x * (1.0 + y * (-1.0 / 6 + y * (1.0 / 120 + y * (-1.0 / 5040 + y * (1.0 / 362880)))))
    c = 1.0 + y * (-0.5 + y * (1.0 / 24 + y * (-1.0 / 720 + y * (1.0 / 40320 - y * (1.0 / 3628800)))))
    odd = quadrant & 1 == 1
    flip_c = (quadrant + 1) & 2 == 2
    flip_s = quadrant & 2 == 2
    cosine = jnp.where(odd, s, c)
    sine = jnp.where(odd, c, s)
    return jnp.where(flip_c, -cosine, cosine), jnp.where(flip_s, -sine, sine)


def fused(ni, nj, samples_hbm, table_hbm, index_hbm, out_ref, samples_ref, table_ref, index_ref, re_ref,
          im_ref, send_ref, recv_ref, steer_ref, load_sem, send_sem, recv_sem):
    nl, t_loc, q = 16, 16, 2 * CH_DEV
    antennas = ni * nl
    size = q * t_loc
    my_i, my_j = lax.axis_index("chan"), lax.axis_index("tm")
    other_j = 1 - my_j

    loads = [pltpu.make_async_copy(src, dst, load_sem.at[i]) for i, (src, dst) in enumerate(
        [(table_hbm, table_ref), (samples_hbm.at[0], samples_ref.at[0]),
         (samples_hbm.at[1], samples_ref.at[1]), (index_hbm, index_ref)])]
    for load in loads:
        load.start()

    barrier = pltpu.get_barrier_semaphore()

    def after(step):
        ahead = my_i + step
        return jnp.where(ahead >= ni, ahead - ni, ahead)

    def around(body):
        lax.fori_loop(1, ni, lambda step, carry: (body(step), carry)[1], 0)

    def greet(peer_i, peer_j):
        pl.semaphore_signal(barrier, inc=1, device_id=(peer_i, peer_j),
                            device_id_type=pl.DeviceIdType.MESH)

    greet(my_i, other_j)

    def greet_both(step):
        greet(after(step), my_j)
        greet(after(step), other_j)

    around(greet_both)

    loads[0].wait()
    loads[1].wait()
    loads[2].wait()
    table = table_ref[...]
    half = table.shape[1] // 2
    first = dot(samples_ref[0], table)
    second = dot(samples_ref[1], table)
    re_ref[...] = first[:, :half] + second[:, half:]
    im_ref[...] = second[:, :half] - first[:, half:]
    parts = []
    for ref in (re_ref, im_ref):
        rows = [ref[pl.ds(t, nl, stride=t_loc), :] for t in range(t_loc)]
        parts.append(exchange_blocks(rows, ni, CH_DEV))
    blocks = jnp.concatenate(
        [jnp.concatenate([a, b], 1) for a, b in zip(*parts)], 0
    ).astype(BF16)
    src, dst = iota((size, size), 0), iota((size, size), 1)
    want = (dst // t_loc % 2) * (t_loc * CH_DEV) + (dst % t_loc) * CH_DEV + dst // (2 * t_loc)
    order = jnp.where(src == want, 1.0, 0.0).astype(BF16)
    send_ref[...] = dot(blocks, order).astype(BF16)

    pl.semaphore_wait(barrier, ni * nj - 1)

    rows_of = lambda i: pl.ds(pl.multiple_of(i * nl, nl), nl)
    mine = rows_of(my_i)

    def block_copy(step, origin, plane):
        peer = after(step)
        return pltpu.make_async_remote_copy(
            src_ref=send_ref.at[rows_of(peer), :],
            dst_ref=recv_ref.at[plane, rows_of(origin), :],
            send_sem=send_sem,
            recv_sem=recv_sem.at[plane],
            device_id=(peer, other_j if plane else my_j),
            device_id_type=pl.DeviceIdType.MESH,
        )

    def send(step):
        block_copy(step, my_i, 0).start()
        block_copy(step, my_i, 1).start()

    block_copy(0, my_i, 1).start()
    around(send)
    recv_ref[0, mine, :] = send_ref[mine, :]

    loads[3].wait()
    cosine, sine = steering_parts(index_ref[...])
    steer_ref[0] = cosine.astype(BF16)
    steer_ref[1] = sine.astype(BF16)

    span = 2 * t_loc
    row_id, col_id = iota((size, size), 0), iota((size, size), 1)
    on_diag = row_id == col_id
    unit = jnp.where(on_diag, 1.0, 0.0).astype(BF16)
    turn_j = jnp.where(row_id == (col_id ^ t_loc), jnp.where(col_id & t_loc == 0, 1.0, -1.0), 0.0).astype(BF16)

    def prepare(plane):
        z = recv_ref[plane]
        zt = dot(unit, z, NT).astype(BF16)
        zj = dot(z, turn_j).astype(BF16)
        zjt = jnp.concatenate(
            [b for i in range(size // span) for b in
             (zt[i * span + t_loc : (i + 1) * span], -zt[i * span : i * span + t_loc])], 0)
        return z, zt, zj, zjt

    def sized(ref, plane):
        return pltpu.make_async_remote_copy(
            src_ref=ref, dst_ref=ref, send_sem=send_sem, recv_sem=recv_sem.at[plane],
            device_id=(my_i, other_j), device_id_type=pl.DeviceIdType.MESH)

    sized(recv_ref.at[0, : antennas - nl], 0).wait_recv()
    sized(recv_ref.at[1], 1).wait_recv()
    planes = [prepare(j) for j in range(nj)]

    groups = size // LANES
    per = CH_DEV // groups
    cols = nj * LANES
    wide = nj * span
    chan_of = lambda x: x // span % per
    lane_chan = chan_of(iota((1, cols), 1))
    half_ants = antennas // 2
    blocks = range(cols // span)
    rows_at = lambda i: slice(i * span, (i + 1) * span)
    lane = iota((span, LANES), 1)
    slot = lane // span
    packed_slot = iota((span, LANES), 1) // span
    first = iota((cols, LANES), 1) < wide

    def shifted(x, amount):
        return x if amount % LANES == 0 else pltpu.roll(x, amount % LANES, 1)

    def pack(grams):
        done = []
        for i in blocks:
            kept = None
            for g in range(groups):
                for j in range(nj):
                    to = g * nj + j
                    moved = shifted(grams[g][rows_at(i), j * LANES : (j + 1) * LANES], (to - i % per) * span)
                    kept = moved if kept is None else jnp.where(slot == to, moved, kept)
            done.append(kept)
        return jnp.concatenate(done, 0)

    def spread(x, g):
        done = []
        for i in range(x.shape[0] // span):
            k = i % per
            done.append(jnp.concatenate(
                [jnp.where(packed_slot == k, shifted(x[rows_at(i)], (k - g * nj - j) * span), 0.0).astype(BF16)
                 for j in range(nj)], 1))
        return jnp.concatenate(done, 0)

    def spread_all(x):
        return jnp.concatenate([spread(x, g) for g in range(groups)], 0)

    def pick(out):
        return jnp.where(first, out[:cols], out[cols:])

    def only(x, k):
        none = jnp.zeros((span, antennas), BF16)
        return jnp.concatenate([x[rows_at(i)] if i % per == k else none for i in blocks], 0)

    def magnitude(re, im):
        power = re * re + im * im
        return power * lax.rsqrt(jnp.maximum(power, 1e-37))

    def group_steps(g, keepers):
        cut = slice(g * LANES, (g + 1) * LANES)
        z = jnp.concatenate([p[0][:, cut] for p in planes], 1)
        zj = jnp.concatenate([p[2][:, cut] for p in planes], 1)
        zt, zjt = (jnp.concatenate([p[i][cut] for p in planes], 0) for i in (1, 3))
        keepers["gram"][g] = dot(zt, z) + dot(zjt, zj)
        keepers["pt"][g] = zt, zjt
        low_t = jnp.concatenate([zt[:, half_ants:], zjt[:, half_ants:]], 1)
        upper = jnp.concatenate([z[:half_ants], zj[:half_ants]], 0)
        yield
        for k in range(per):
            yield
            top = dot(upper, only(zt, k))
            top = magnitude(top[:half_ants], top[half_ants:])
            low = dot(z[half_ants:], only(low_t, k))
            low = magnitude(low[:, :half_ants], low[:, half_ants:])
            rows = jnp.max(jnp.sum(top, axis=1, keepdims=True), axis=0, keepdims=True)
            columns = jnp.sum(top[:, half_ants:], axis=0, keepdims=True) + jnp.sum(low, axis=0, keepdims=True)
            keepers["largest"][g][k] = jnp.maximum(rows, jnp.max(columns, axis=1, keepdims=True))

    kept = {"gram": {}, "pt": {}, "largest": [{}, {}]}
    for _ in itertools.zip_longest(*[group_steps(g, kept) for g in range(groups)]):
        pass

    gram = pack(kept["gram"])
    gram_b = gram.astype(BF16)
    square = pick(dot(spread_all(gram), gram_b))

    lane_row = iota((1, LANES), 1)
    on_diag = iota((cols, LANES), 1) % wide == iota((cols, LANES), 0) // LANES * span + iota((cols, LANES), 0) % span
    diagonal = jnp.where(on_diag, gram, 0.0)
    bounds, rhos = [{}, {}], [{}, {}]
    rows_rho, rows_inverse = [], []
    for k in range(per):
        both = jnp.sum(diagonal[rows_at(k)] + diagonal[rows_at(per + k)], axis=0, keepdims=True)
        for g in range(groups):
            trace = jnp.sum(jnp.where(lane_row // wide == g, both, 0.0), axis=1, keepdims=True)
            load = (0.1 / antennas * 0.5) * trace
            bound = kept["largest"][g][k] + load
            bounds[g][k] = bound
            rhos[g][k] = 1.0 - load / bound
        rows_rho.append(jnp.where(lane_row < wide, rhos[0][k], rhos[1][k]))
        rows_inverse.append(1.0 / jnp.where(lane_row < wide, bounds[0][k], bounds[1][k]))
    r = jnp.concatenate(rows_rho * nj, 0)
    inv = jnp.concatenate(rows_inverse * nj, 0)
    r2 = r * r
    r4 = r2 * r2
    s = [1.0 + 0.0 * r]
    for _ in range(TERMS - 1):
        s.append(1.0 + r * s[-1])
    c = [s[TERMS - 2 - m] for m in range(TERMS - 1)]
    t0 = c[4] + r * (c[5] + r * c[6])
    p0 = c[0] + r * (c[1] + r * (c[2] + r * c[3])) + r4 * t0

    def by(v, count=cols):
        return jnp.concatenate([jnp.broadcast_to(v[i : i + 1], (span, LANES)) for i in range(count // span)], 0)

    x1 = by(inv) * gram
    x2 = by(2.0 * r) * x1 - by(inv * inv) * square
    out = dot(spread_all(x2), jnp.concatenate([x1.astype(BF16), x2.astype(BF16)], 1))
    x3 = by(r) * x2 + by(r2) * x1 - pick(out[:, :LANES])
    x4 = by(2.0 * r2) * x2 - pick(out[:, LANES:])
    tail = by(c[5]) * x1 + by(c[6]) * x2
    head = x1 + x2 + x3
    out = dot(spread_all(x4), jnp.concatenate([tail.astype(BF16), head.astype(BF16)], 1))
    poly = (by(c[1] + r4 * c[5]) * x1 + by(c[2] + r4 * c[6]) * x2 + by(c[3]) * x3 + by(t0) * x4
            - pick(out[:, :LANES]))
    own = (by(1.0 + r4, LANES) * head[:LANES] + by(s[3], LANES) * x4[:LANES]
           - jnp.where(first[:LANES], out[:LANES, LANES:], out[cols : cols + LANES, LANES:]))
    own_low = own - own.astype(BF16).astype(F32)

    for g in range(groups):
        zt, zjt = kept["pt"][g]
        pt = dot(zt, steer_ref[0], NT) + dot(zjt, steer_ref[1], NT)
        pth, ptl = split(pt)
        oh = spread(own, g)
        ends = dot(jnp.concatenate([spread(poly, g), oh, spread(own_low, g)], 0), pth)
        back = (ends[cols : cols + LANES] + ends[cols + LANES :]) + dot(oh, ptl)
        for k in range(per):
            energy = 0.0
            at = slice(k, k + 1), slice(g * wide, g * wide + 1)
            for j in range(nj):
                low = rows_at(j * per + k)
                energy += jnp.sum(pt[low] * (p0[at] * pt[low] - ends[low]), axis=0, keepdims=True)
            bound, whole = bounds[g][k], s[TERMS - 1][at]
            response = antennas * whole - energy * inv[at]
            factor = lax.rsqrt(response) * lax.rsqrt(bound * (1.0 / (nj * t_loc)))
            beam = (whole * pt[rows_at(k)] - back[rows_at(k)]) * factor
            beam = beam.astype(BF16)
            out_ref[0, g * per + k] = beam[:t_loc]
            out_ref[1, g * per + k] = beam[t_loc:]

    sized(send_ref.at[: antennas - nl], 0).wait_send()
    sized(send_ref, 1).wait_send()


def fused_local(ni, nj, samples, steer_index):
    _, nl, t_loc, _ = samples.shape
    beams, antennas = steer_index.shape
    size = 2 * CH_DEV * t_loc
    vmem = pl.BlockSpec(memory_space=pltpu.VMEM)
    table = jnp.asarray(taper_table(CH_DEV * ni))
    out = pl.pallas_call(
        functools.partial(fused, ni, nj),
        out_shape=pltpu.VMEM((2, CH_DEV, t_loc, beams), BF16),
        in_specs=[pl.BlockSpec(memory_space=pl.ANY)] * 3,
        out_specs=vmem,
        scratch_shapes=[
            pltpu.VMEM((2, nl * t_loc, C), BF16),
            pltpu.VMEM(table.shape, BF16),
            pltpu.VMEM((beams, antennas), jnp.int32),
            pltpu.VMEM((nl * t_loc, CH_DEV * ni), F32),
            pltpu.VMEM((nl * t_loc, CH_DEV * ni), F32),
            pltpu.VMEM((antennas, size), BF16),
            pltpu.VMEM((nj, antennas, size), BF16),
            pltpu.VMEM((2, beams, antennas), BF16),
            pltpu.SemaphoreType.DMA((4,)),
            pltpu.SemaphoreType.DMA,
            pltpu.SemaphoreType.DMA((nj,)),
        ],
        compiler_params=pltpu.CompilerParams(collective_id=0, has_side_effects=True),
    )(samples.reshape(2, nl * t_loc, C), table, steer_index)
    return jnp.transpose(out, (0, 1, 3, 2))


def choose(ni, nj, samples, steer_index):
    _, nl, t_loc, _ = samples.shape
    beams, antennas = steer_index.shape
    tiled = nl == 16 and t_loc == 16 and CH_DEV * ni == LANES and antennas == nl * ni
    if tiled and nj == 2:
        return fused_local(ni, nj, samples, steer_index)
    return local(samples, steer_index)


def solution(mesh):
    return jax.shard_map(
        functools.partial(choose, mesh.shape["chan"], mesh.shape["tm"]),
        mesh=mesh,
        in_specs=(P(None, "chan", "tm", None), P()),
        out_specs=P(None, "chan", None, "tm"),
        check_vma=False,
    )
```

```python
import functools
import itertools
import math

import jax
import jax.numpy as jnp
import numpy as np
from jax import lax
from jax.experimental import pallas as pl
from jax.experimental.pallas import tpu as pltpu
from jax.sharding import PartitionSpec as P

C = 1024
PHASES = 256
CH_DEV = 8
ITERS = 3
TERMS = 2**ITERS
LANES = 128


HIGHEST = lax.Precision.HIGHEST
F32 = jnp.float32
BF16 = jnp.bfloat16
NT = (((1,), (1,)), ((), ()))


def transform_table(channels_all):
    offset = (C - channels_all) // 2
    channel_number = jnp.arange(channels_all, dtype=jnp.int32) + offset
    sample_number = jnp.arange(C, dtype=jnp.int32)
    phase_turns = channel_number[:, None] * sample_number[None, :] % C
    phase_angle = 2.0 * math.pi / C * phase_turns.astype(jnp.float32)
    window_taper = (
        0.5 - 0.5 * jnp.cos(2.0 * math.pi / C * sample_number.astype(jnp.float32))
    ) / math.sqrt(C)
    cosine = window_taper[None, :] * jnp.cos(phase_angle)
    sine_part = window_taper[None, :] * jnp.sin(phase_angle)
    coefficients = jnp.stack(
        [jnp.stack([cosine, sine_part], 1), jnp.stack([-sine_part, cosine], 1)], 0
    )
    return coefficients.astype(jnp.bfloat16)


def complex_product(left_real, left_imag, right_real, right_imag):
    real_part = jnp.dot(left_real, right_real, precision=HIGHEST) - jnp.dot(
        left_imag, right_imag, precision=HIGHEST
    )
    imag_part = jnp.dot(left_real, right_imag, precision=HIGHEST) + jnp.dot(
        left_imag, right_real, precision=HIGHEST
    )
    return (real_part, imag_part)


def invert_loaded(covariance_real, covariance_imag):
    matrix_order = covariance_real.shape[0]
    loading = 0.1 * jnp.mean(jnp.diagonal(covariance_real))
    identity = jnp.eye(matrix_order, dtype=jnp.float32)
    loaded = covariance_real + loading * identity
    magnitude = jnp.sqrt(loaded * loaded + covariance_imag * covariance_imag)
    largest = jnp.max(jnp.sum(magnitude, axis=1))

    def iterate(counter, state):
        approx_real, approx_imag = state
        image_real, image_imag = complex_product(loaded, covariance_imag, approx_real, approx_imag)
        square_real, square_imag = complex_product(approx_real, approx_imag, image_real, image_imag)
        return (2.0 * approx_real - square_real, 2.0 * approx_imag - square_imag)

    start_state = (identity / largest, jnp.zeros_like(identity))
    return lax.fori_loop(0, ITERS, iterate, start_state)


def form_weights(covariance_real, covariance_imag, steer_real, steer_imag):
    inverse_real, inverse_imag = invert_loaded(covariance_real, covariance_imag)
    gain_real, gain_imag = complex_product(inverse_real, inverse_imag, steer_real, steer_imag)
    response = jnp.sum(steer_real * gain_real + steer_imag * gain_imag, axis=0)
    factor = lax.rsqrt(response)
    return ((gain_real * factor).astype(jnp.bfloat16), (gain_imag * factor).astype(jnp.bfloat16))


def weights_stacked(covariance_real, covariance_imag, steer_real, steer_imag):
    weight_real, weight_imag = jax.vmap(form_weights, in_axes=(0, 0, None, None))(
        covariance_real, covariance_imag, steer_real, steer_imag
    )
    return jnp.stack([weight_real, weight_imag], 1)


def steering(steer_index):
    phase_angle = 2.0 * math.pi / PHASES * steer_index.astype(jnp.float32)
    return (jnp.cos(phase_angle).T, jnp.sin(phase_angle).T)


def apply_beams(weight_pair, spectrum):
    real_weight = weight_pair[:, 0]
    imag_weight = weight_pair[:, 1]
    beam_real = jnp.einsum(
        "knb,kns->kbs", real_weight, spectrum[0], preferred_element_type=jnp.float32
    ) + jnp.einsum("knb,kns->kbs", imag_weight, spectrum[1], preferred_element_type=jnp.float32)
    beam_imag = jnp.einsum(
        "knb,kns->kbs", real_weight, spectrum[1], preferred_element_type=jnp.float32
    ) - jnp.einsum("knb,kns->kbs", imag_weight, spectrum[0], preferred_element_type=jnp.float32)
    return jnp.stack([beam_real, beam_imag], 0).astype(jnp.bfloat16)


def local(samples, steer_index):
    channels_all = CH_DEV * lax.axis_size("chan")
    coefficients = transform_table(channels_all)
    spectra = lax.dot_general(
        coefficients, samples, (((2, 3), (0, 3)), ((), ())), preferred_element_type=jnp.float32
    ).astype(jnp.bfloat16)
    steer_real, steer_imag = steering(steer_index)
    turned = lax.all_to_all(
        lax.all_to_all(spectra, "chan", split_axis=1, concat_axis=2, tiled=True),
        "tm",
        split_axis=1,
        concat_axis=3,
        tiled=True,
    )
    outer_sums = jnp.einsum("ikns,jkms->kinjm", turned, turned, preferred_element_type=jnp.float32)
    snapshots = turned.shape[3]
    covariance_real = (outer_sums[:, 0, :, 0, :] + outer_sums[:, 1, :, 1, :]) / snapshots
    covariance_imag = (outer_sums[:, 1, :, 0, :] - outer_sums[:, 0, :, 1, :]) / snapshots
    weight_pair = weights_stacked(covariance_real, covariance_imag, steer_real, steer_imag)
    local_beams = apply_beams(weight_pair, turned)
    return lax.all_to_all(local_beams, "tm", split_axis=3, concat_axis=1, tiled=True)


def taper_table(channels_all):
    offset = (C - channels_all) // 2
    channel = np.arange(channels_all) + offset
    sample = np.arange(C)
    angle = 2.0 * math.pi / C * (channel[None, :] * sample[:, None] % C)
    taper = (0.5 - 0.5 * np.cos(2.0 * math.pi / C * sample)) / math.sqrt(C)
    both = np.concatenate([taper[:, None] * np.cos(angle), taper[:, None] * np.sin(angle)], 1)
    return both.astype(np.float32).astype(BF16)


def iota(shape, axis):
    return lax.broadcasted_iota(jnp.int32, shape, axis)


def dot(a, b, dims=(((1,), (0,)), ((), ()))):
    return lax.dot_general(a, b, dims, preferred_element_type=F32)


def split(x):
    high = x.astype(BF16)
    return high, (x - high.astype(F32)).astype(BF16)


def exchange_blocks(rows, count, width):
    lane = iota(rows[0].shape, 1)
    total = count * width
    step = count // 2
    while step:
        low = (lane // width) & step == 0
        done = list(rows)
        for a in range(count):
            if a & step:
                continue
            b = a + step
            up = pltpu.roll(rows[b], step * width, 1)
            down = pltpu.roll(rows[a], total - step * width, 1)
            done[a] = jnp.where(low, rows[a], up)
            done[b] = jnp.where(low, down, rows[b])
        rows = done
        step //= 2
    return rows


def steering_parts(index):
    turn = index & (PHASES - 1)
    quarter = PHASES // 4
    quadrant = (turn + quarter // 2) // quarter
    x = (turn - quarter * quadrant).astype(F32) * (2.0 * math.pi / PHASES)
    y = x * x
    s = x * (1.0 + y * (-1.0 / 6 + y * (1.0 / 120 + y * (-1.0 / 5040 + y * (1.0 / 362880)))))
    c = 1.0 + y * (-0.5 + y * (1.0 / 24 + y * (-1.0 / 720 + y * (1.0 / 40320 - y * (1.0 / 3628800)))))
    odd = quadrant & 1 == 1
    flip_c = (quadrant + 1) & 2 == 2
    flip_s = quadrant & 2 == 2
    cosine = jnp.where(odd, s, c)
    sine = jnp.where(odd, c, s)
    return jnp.where(flip_c, -cosine, cosine), jnp.where(flip_s, -sine, sine)


def fused(ni, nj, samples_hbm, table_hbm, index_hbm, out_ref, samples_ref, table_ref, index_ref, re_ref,
          im_ref, send_ref, recv_ref, steer_ref, load_sem, send_sem, recv_sem):
    nl, t_loc, q = 16, 16, 2 * CH_DEV
    antennas = ni * nl
    size = q * t_loc
    my_i, my_j = lax.axis_index("chan"), lax.axis_index("tm")
    other_j = 1 - my_j

    loads = [pltpu.make_async_copy(src, dst, load_sem.at[i]) for i, (src, dst) in enumerate(
        [(table_hbm, table_ref), (samples_hbm.at[0], samples_ref.at[0]),
         (samples_hbm.at[1], samples_ref.at[1]), (index_hbm, index_ref)])]
    for load in loads:
        load.start()

    barrier = pltpu.get_barrier_semaphore()

    def after(step):
        ahead = my_i + step
        return jnp.where(ahead >= ni, ahead - ni, ahead)

    def around(body):
        lax.fori_loop(1, ni, lambda step, carry: (body(step), carry)[1], 0)

    def greet(peer_i, peer_j):
        pl.semaphore_signal(barrier, inc=1, device_id=(peer_i, peer_j),
                            device_id_type=pl.DeviceIdType.MESH)

    greet(my_i, other_j)

    def greet_both(step):
        greet(after(step), my_j)
        greet(after(step), other_j)

    around(greet_both)

    loads[0].wait()
    loads[1].wait()
    loads[2].wait()
    table = table_ref[...]
    half = table.shape[1] // 2
    first = dot(samples_ref[0], table)
    second = dot(samples_ref[1], table)
    re_ref[...] = first[:, :half] + second[:, half:]
    im_ref[...] = second[:, :half] - first[:, half:]
    parts = []
    for ref in (re_ref, im_ref):
        rows = [ref[pl.ds(t, nl, stride=t_loc), :] for t in range(t_loc)]
        parts.append(exchange_blocks(rows, ni, CH_DEV))
    blocks = jnp.concatenate(
        [jnp.concatenate([a, b], 1) for a, b in zip(*parts)], 0
    ).astype(BF16)
    src, dst = iota((size, size), 0), iota((size, size), 1)
    want = (dst // t_loc % 2) * (t_loc * CH_DEV) + (dst % t_loc) * CH_DEV + dst // (2 * t_loc)
    order = jnp.where(src == want, 1.0, 0.0).astype(BF16)
    send_ref[...] = dot(blocks, order).astype(BF16)

    pl.semaphore_wait(barrier, ni * nj - 1)

    rows_of = lambda i: pl.ds(pl.multiple_of(i * nl, nl), nl)
    mine = rows_of(my_i)

    def peer_of(step):
        if isinstance(step, int) and step == 0:
            return my_i
        usual = step - 2
        usual = jnp.where(usual >= ni - my_i, usual + 2, usual)
        moved = jnp.where(step <= 2, step - 1, lax.rem(my_i + usual, ni))
        return jnp.where((my_i >= 2) & (my_i < 16), moved, after(step))

    def block_copy(step, origin, plane):
        peer = peer_of(step)
        return pltpu.make_async_remote_copy(
            src_ref=send_ref.at[rows_of(peer), :],
            dst_ref=recv_ref.at[plane, rows_of(origin), :],
            send_sem=send_sem,
            recv_sem=recv_sem.at[plane],
            device_id=(peer, other_j if plane else my_j),
            device_id_type=pl.DeviceIdType.MESH,
        )

    def send(step):
        block_copy(step, my_i, 0).start()
        block_copy(step, my_i, 1).start()

    block_copy(0, my_i, 1).start()
    around(send)
    recv_ref[0, mine, :] = send_ref[mine, :]

    loads[3].wait()
    cosine, sine = steering_parts(index_ref[...])
    steer_ref[0] = cosine.astype(BF16)
    steer_ref[1] = sine.astype(BF16)

    span = 2 * t_loc
    row_id, col_id = iota((size, size), 0), iota((size, size), 1)
    on_diag = row_id == col_id
    unit = jnp.where(on_diag, 1.0, 0.0).astype(BF16)
    turn_j = jnp.where(row_id == (col_id ^ t_loc), jnp.where(col_id & t_loc == 0, 1.0, -1.0), 0.0).astype(BF16)

    def prepare(plane):
        z = recv_ref[plane]
        zt = dot(unit, z, NT).astype(BF16)
        zj = dot(z, turn_j).astype(BF16)
        zjt = jnp.concatenate(
            [b for i in range(size // span) for b in
             (zt[i * span + t_loc : (i + 1) * span], -zt[i * span : i * span + t_loc])], 0)
        return z, zt, zj, zjt

    def sized(ref, plane):
        return pltpu.make_async_remote_copy(
            src_ref=ref, dst_ref=ref, send_sem=send_sem, recv_sem=recv_sem.at[plane],
            device_id=(my_i, other_j), device_id_type=pl.DeviceIdType.MESH)

    sized(recv_ref.at[0, : antennas - nl], 0).wait_recv()
    sized(recv_ref.at[1], 1).wait_recv()
    planes = [prepare(j) for j in range(nj)]

    groups = size // LANES
    per = CH_DEV // groups
    cols = nj * LANES
    wide = nj * span
    chan_of = lambda x: x // span % per
    lane_chan = chan_of(iota((1, cols), 1))
    half_ants = antennas // 2
    blocks = range(cols // span)
    rows_at = lambda i: slice(i * span, (i + 1) * span)
    lane = iota((span, LANES), 1)
    slot = lane // span
    packed_slot = iota((span, LANES), 1) // span
    first = iota((cols, LANES), 1) < wide

    def shifted(x, amount):
        return x if amount % LANES == 0 else pltpu.roll(x, amount % LANES, 1)

    def pack(grams):
        done = []
        for i in blocks:
            kept = None
            for g in range(groups):
                for j in range(nj):
                    to = g * nj + j
                    moved = shifted(grams[g][rows_at(i), j * LANES : (j + 1) * LANES], (to - i % per) * span)
                    kept = moved if kept is None else jnp.where(slot == to, moved, kept)
            done.append(kept)
        return jnp.concatenate(done, 0)

    def spread(x, g):
        x = x.astype(BF16)
        done = []
        for i in range(x.shape[0] // span):
            k = i % per
            done.append(jnp.concatenate(
                [jnp.where(packed_slot == k, shifted(x[rows_at(i)], (k - g * nj - j) * span), jnp.zeros((), BF16))
                 for j in range(nj)], 1))
        return jnp.concatenate(done, 0)

    def spread_all(x):
        return jnp.concatenate([spread(x, g) for g in range(groups)], 0)

    def pick(out):
        return jnp.where(first, out[:cols], out[cols:])

    def only(x, k):
        none = jnp.zeros((span, antennas), BF16)
        return jnp.concatenate([x[rows_at(i)] if i % per == k else none for i in blocks], 0)

    def magnitude(re, im):
        power = re * re + im * im
        return power * lax.rsqrt(jnp.maximum(power, 1e-37))

    def group_steps(g, keepers):
        cut = slice(g * LANES, (g + 1) * LANES)
        z = jnp.concatenate([p[0][:, cut] for p in planes], 1)
        zj = jnp.concatenate([p[2][:, cut] for p in planes], 1)
        zt, zjt = (jnp.concatenate([p[i][cut] for p in planes], 0) for i in (1, 3))
        keepers["gram"][g] = dot(zt, z) + dot(zjt, zj)
        keepers["pt"][g] = zt, zjt
        low_t = jnp.concatenate([zt[:, half_ants:], zjt[:, half_ants:]], 1)
        upper = jnp.concatenate([z[:half_ants], zj[:half_ants]], 0)
        yield
        for k in range(per):
            yield
            top = dot(upper, only(zt, k))
            top = magnitude(top[:half_ants], top[half_ants:])
            low = dot(z[half_ants:], only(low_t, k))
            low = magnitude(low[:, :half_ants], low[:, half_ants:])
            rows = jnp.max(jnp.sum(top, axis=1, keepdims=True), axis=0, keepdims=True)
            columns = jnp.sum(top[:, half_ants:], axis=0, keepdims=True) + jnp.sum(low, axis=0, keepdims=True)
            keepers["largest"][g][k] = jnp.maximum(rows, jnp.max(columns, axis=1, keepdims=True))

    kept = {"gram": {}, "pt": {}, "largest": [{}, {}]}
    for _ in itertools.zip_longest(*[group_steps(g, kept) for g in range(groups)]):
        pass

    gram = pack(kept["gram"])
    gram_b = gram.astype(BF16)
    square = pick(dot(spread_all(gram), gram_b))

    lane_row = iota((1, LANES), 1)
    on_diag = iota((cols, LANES), 1) % wide == iota((cols, LANES), 0) // LANES * span + iota((cols, LANES), 0) % span
    diagonal = jnp.where(on_diag, gram, 0.0)
    loads_of, largest_of = [], []
    for k in range(per):
        both = jnp.sum(diagonal[rows_at(k)] + diagonal[rows_at(per + k)], axis=0, keepdims=True)
        traces = [jnp.sum(jnp.where(lane_row // wide == g, both, 0.0), axis=1, keepdims=True) for g in range(groups)]
        loads_of.append(jnp.where(lane_row < wide, traces[0], traces[1]))
        largest_of.append(jnp.where(lane_row < wide, kept["largest"][0][k], kept["largest"][1][k]))
    load = (0.1 / antennas * 0.5) * jnp.concatenate(loads_of * nj, 0)
    bound = jnp.concatenate(largest_of * nj, 0) + load
    inv = 1.0 / bound
    r = 1.0 - load * inv
    r2 = r * r
    r4 = r2 * r2
    s = [1.0 + 0.0 * r]
    for _ in range(TERMS - 1):
        s.append(1.0 + r * s[-1])
    c = [s[TERMS - 2 - m] for m in range(TERMS - 1)]
    t0 = c[4] + r * (c[5] + r * c[6])
    p0 = c[0] + r * (c[1] + r * (c[2] + r * c[3])) + r4 * t0

    def by(v, count=cols):
        return jnp.concatenate([jnp.broadcast_to(v[i : i + 1], (span, LANES)) for i in range(count // span)], 0)

    x1 = by(inv) * gram
    x2 = by(2.0 * r) * x1 - by(inv * inv) * square
    out = dot(spread_all(x2), jnp.concatenate([x1.astype(BF16), x2.astype(BF16)], 1))
    x3 = by(r) * x2 + by(r2) * x1 - pick(out[:, :LANES])
    x4 = by(2.0 * r2) * x2 - pick(out[:, LANES:])
    tail = by(c[5]) * x1 + by(c[6]) * x2
    head = x1 + x2 + x3
    out = dot(spread_all(x4), jnp.concatenate([tail.astype(BF16), head.astype(BF16)], 1))
    poly = (by(c[1] + r4 * c[5]) * x1 + by(c[2] + r4 * c[6]) * x2 + by(c[3]) * x3 + by(t0) * x4
            - pick(out[:, :LANES]))
    own = (by(1.0 + r4, LANES) * head[:LANES] + by(s[3], LANES) * x4[:LANES]
           - jnp.where(first[:LANES], out[:LANES, LANES:], out[cols : cols + LANES, LANES:]))
    own_low = own - own.astype(BF16).astype(F32)

    for g in range(groups):
        zt, zjt = kept["pt"][g]
        pt = dot(zt, steer_ref[0], NT) + dot(zjt, steer_ref[1], NT)
        pth, ptl = split(pt)
        oh = spread(own, g)
        ends = dot(jnp.concatenate([spread(poly, g), oh, spread(own_low, g)], 0), pth)
        back = (ends[cols : cols + LANES] + ends[cols + LANES :]) + dot(oh, ptl)
        for k in range(per):
            energy = 0.0
            at = slice(k, k + 1), slice(g * wide, g * wide + 1)
            for j in range(nj):
                low = rows_at(j * per + k)
                energy += jnp.sum(pt[low] * (p0[at] * pt[low] - ends[low]), axis=0, keepdims=True)
            whole = s[TERMS - 1][at]
            response = antennas * whole - energy * inv[at]
            factor = lax.rsqrt(response * (bound[at] * (1.0 / (nj * t_loc))))
            beam = (whole * pt[rows_at(k)] - back[rows_at(k)]) * factor
            beam = beam.astype(BF16)
            out_ref[0, g * per + k] = beam[:t_loc]
            out_ref[1, g * per + k] = beam[t_loc:]

    sized(send_ref.at[: antennas - nl], 0).wait_send()
    sized(send_ref, 1).wait_send()


def fused_local(ni, nj, samples, steer_index):
    _, nl, t_loc, _ = samples.shape
    beams, antennas = steer_index.shape
    size = 2 * CH_DEV * t_loc
    vmem = pl.BlockSpec(memory_space=pltpu.VMEM)
    table = jnp.asarray(taper_table(CH_DEV * ni))
    out = pl.pallas_call(
        functools.partial(fused, ni, nj),
        out_shape=pltpu.VMEM((2, CH_DEV, t_loc, beams), BF16),
        in_specs=[pl.BlockSpec(memory_space=pl.ANY)] * 3,
        out_specs=vmem,
        scratch_shapes=[
            pltpu.VMEM((2, nl * t_loc, C), BF16),
            pltpu.VMEM(table.shape, BF16),
            pltpu.VMEM((beams, antennas), jnp.int32),
            pltpu.VMEM((nl * t_loc, CH_DEV * ni), F32),
            pltpu.VMEM((nl * t_loc, CH_DEV * ni), F32),
            pltpu.VMEM((antennas, size), BF16),
            pltpu.VMEM((nj, antennas, size), BF16),
            pltpu.VMEM((2, beams, antennas), BF16),
            pltpu.SemaphoreType.DMA((4,)),
            pltpu.SemaphoreType.DMA,
            pltpu.SemaphoreType.DMA((nj,)),
        ],
        compiler_params=pltpu.CompilerParams(collective_id=0, has_side_effects=True),
    )(samples.reshape(2, nl * t_loc, C), table, steer_index)
    return jnp.transpose(out, (0, 1, 3, 2))


def choose(ni, nj, samples, steer_index):
    _, nl, t_loc, _ = samples.shape
    beams, antennas = steer_index.shape
    tiled = nl == 16 and t_loc == 16 and CH_DEV * ni == LANES and antennas == nl * ni
    if tiled and nj == 2:
        return fused_local(ni, nj, samples, steer_index)
    return local(samples, steer_index)


def solution(mesh):
    return jax.shard_map(
        functools.partial(choose, mesh.shape["chan"], mesh.shape["tm"]),
        mesh=mesh,
        in_specs=(P(None, "chan", "tm", None), P()),
        out_specs=P(None, "chan", None, "tm"),
        check_vma=False,
    )
```

```python
import functools
import itertools
import math

import jax
import jax.numpy as jnp
import numpy as np
from jax import lax
from jax.experimental import pallas as pl
from jax.experimental.pallas import tpu as pltpu
from jax.sharding import PartitionSpec as P

C = 1024
PHASES = 256
CH_DEV = 8
ITERS = 3
TERMS = 2**ITERS
LANES = 128


HIGHEST = lax.Precision.HIGHEST
F32 = jnp.float32
BF16 = jnp.bfloat16
NT = (((1,), (1,)), ((), ()))


def transform_table(channels_all):
    offset = (C - channels_all) // 2
    channel_number = jnp.arange(channels_all, dtype=jnp.int32) + offset
    sample_number = jnp.arange(C, dtype=jnp.int32)
    phase_turns = channel_number[:, None] * sample_number[None, :] % C
    phase_angle = 2.0 * math.pi / C * phase_turns.astype(jnp.float32)
    window_taper = (
        0.5 - 0.5 * jnp.cos(2.0 * math.pi / C * sample_number.astype(jnp.float32))
    ) / math.sqrt(C)
    cosine = window_taper[None, :] * jnp.cos(phase_angle)
    sine_part = window_taper[None, :] * jnp.sin(phase_angle)
    coefficients = jnp.stack(
        [jnp.stack([cosine, sine_part], 1), jnp.stack([-sine_part, cosine], 1)], 0
    )
    return coefficients.astype(jnp.bfloat16)


def complex_product(left_real, left_imag, right_real, right_imag):
    real_part = jnp.dot(left_real, right_real, precision=HIGHEST) - jnp.dot(
        left_imag, right_imag, precision=HIGHEST
    )
    imag_part = jnp.dot(left_real, right_imag, precision=HIGHEST) + jnp.dot(
        left_imag, right_real, precision=HIGHEST
    )
    return (real_part, imag_part)


def invert_loaded(covariance_real, covariance_imag):
    matrix_order = covariance_real.shape[0]
    loading = 0.1 * jnp.mean(jnp.diagonal(covariance_real))
    identity = jnp.eye(matrix_order, dtype=jnp.float32)
    loaded = covariance_real + loading * identity
    magnitude = jnp.sqrt(loaded * loaded + covariance_imag * covariance_imag)
    largest = jnp.max(jnp.sum(magnitude, axis=1))

    def iterate(counter, state):
        approx_real, approx_imag = state
        image_real, image_imag = complex_product(loaded, covariance_imag, approx_real, approx_imag)
        square_real, square_imag = complex_product(approx_real, approx_imag, image_real, image_imag)
        return (2.0 * approx_real - square_real, 2.0 * approx_imag - square_imag)

    start_state = (identity / largest, jnp.zeros_like(identity))
    return lax.fori_loop(0, ITERS, iterate, start_state)


def form_weights(covariance_real, covariance_imag, steer_real, steer_imag):
    inverse_real, inverse_imag = invert_loaded(covariance_real, covariance_imag)
    gain_real, gain_imag = complex_product(inverse_real, inverse_imag, steer_real, steer_imag)
    response = jnp.sum(steer_real * gain_real + steer_imag * gain_imag, axis=0)
    factor = lax.rsqrt(response)
    return ((gain_real * factor).astype(jnp.bfloat16), (gain_imag * factor).astype(jnp.bfloat16))


def weights_stacked(covariance_real, covariance_imag, steer_real, steer_imag):
    weight_real, weight_imag = jax.vmap(form_weights, in_axes=(0, 0, None, None))(
        covariance_real, covariance_imag, steer_real, steer_imag
    )
    return jnp.stack([weight_real, weight_imag], 1)


def steering(steer_index):
    phase_angle = 2.0 * math.pi / PHASES * steer_index.astype(jnp.float32)
    return (jnp.cos(phase_angle).T, jnp.sin(phase_angle).T)


def apply_beams(weight_pair, spectrum):
    real_weight = weight_pair[:, 0]
    imag_weight = weight_pair[:, 1]
    beam_real = jnp.einsum(
        "knb,kns->kbs", real_weight, spectrum[0], preferred_element_type=jnp.float32
    ) + jnp.einsum("knb,kns->kbs", imag_weight, spectrum[1], preferred_element_type=jnp.float32)
    beam_imag = jnp.einsum(
        "knb,kns->kbs", real_weight, spectrum[1], preferred_element_type=jnp.float32
    ) - jnp.einsum("knb,kns->kbs", imag_weight, spectrum[0], preferred_element_type=jnp.float32)
    return jnp.stack([beam_real, beam_imag], 0).astype(jnp.bfloat16)


def local(samples, steer_index):
    channels_all = CH_DEV * lax.axis_size("chan")
    coefficients = transform_table(channels_all)
    spectra = lax.dot_general(
        coefficients, samples, (((2, 3), (0, 3)), ((), ())), preferred_element_type=jnp.float32
    ).astype(jnp.bfloat16)
    steer_real, steer_imag = steering(steer_index)
    turned = lax.all_to_all(
        lax.all_to_all(spectra, "chan", split_axis=1, concat_axis=2, tiled=True),
        "tm",
        split_axis=1,
        concat_axis=3,
        tiled=True,
    )
    outer_sums = jnp.einsum("ikns,jkms->kinjm", turned, turned, preferred_element_type=jnp.float32)
    snapshots = turned.shape[3]
    covariance_real = (outer_sums[:, 0, :, 0, :] + outer_sums[:, 1, :, 1, :]) / snapshots
    covariance_imag = (outer_sums[:, 1, :, 0, :] - outer_sums[:, 0, :, 1, :]) / snapshots
    weight_pair = weights_stacked(covariance_real, covariance_imag, steer_real, steer_imag)
    local_beams = apply_beams(weight_pair, turned)
    return lax.all_to_all(local_beams, "tm", split_axis=3, concat_axis=1, tiled=True)


def taper_table(channels_all):
    offset = (C - channels_all) // 2
    channel = np.arange(channels_all) + offset
    sample = np.arange(C)
    angle = 2.0 * math.pi / C * (channel[None, :] * sample[:, None] % C)
    taper = (0.5 - 0.5 * np.cos(2.0 * math.pi / C * sample)) / math.sqrt(C)
    both = np.concatenate([taper[:, None] * np.cos(angle), taper[:, None] * np.sin(angle)], 1)
    return both.astype(np.float32).astype(BF16)


def iota(shape, axis):
    return lax.broadcasted_iota(jnp.int32, shape, axis)


def dot(a, b, dims=(((1,), (0,)), ((), ()))):
    return lax.dot_general(a, b, dims, preferred_element_type=F32)


def split(x):
    high = x.astype(BF16)
    return high, (x - high.astype(F32)).astype(BF16)


def exchange_blocks(rows, count, width):
    place = iota(rows[0].shape, 1) // width
    turned = [rows[0]] + [pltpu.roll(rows[t], t * width, 1) for t in range(1, count)]
    rows = [turned[-i % count] for i in range(count)]
    step = 1
    while step < count:
        take = place & step != 0
        rows = [jnp.where(take, rows[i - step], rows[i]) for i in range(count)]
        step *= 2
    return rows


def steering_parts(index):
    turn = index & (PHASES - 1)
    quarter = PHASES // 4
    quadrant = (turn + quarter // 2) // quarter
    x = (turn - quarter * quadrant).astype(F32) * (2.0 * math.pi / PHASES)
    y = x * x
    s = x * (1.0 + y * (-1.0 / 6 + y * (1.0 / 120 + y * (-1.0 / 5040 + y * (1.0 / 362880)))))
    c = 1.0 + y * (-0.5 + y * (1.0 / 24 + y * (-1.0 / 720 + y * (1.0 / 40320 - y * (1.0 / 3628800)))))
    odd = quadrant & 1 == 1
    flip_c = (quadrant + 1) & 2 == 2
    flip_s = quadrant & 2 == 2
    cosine = jnp.where(odd, s, c)
    sine = jnp.where(odd, c, s)
    return jnp.where(flip_c, -cosine, cosine), jnp.where(flip_s, -sine, sine)


def fused(ni, nj, samples_hbm, table_hbm, index_hbm, out_ref, samples_ref, table_ref, index_ref, re_ref,
          im_ref, send_ref, recv_ref, steer_ref, load_sem, send_sem, recv_sem):
    nl, t_loc, q = 16, 16, 2 * CH_DEV
    antennas = ni * nl
    size = q * t_loc
    my_i, my_j = lax.axis_index("chan"), lax.axis_index("tm")
    other_j = 1 - my_j

    loads = [pltpu.make_async_copy(src, dst, load_sem.at[i]) for i, (src, dst) in enumerate(
        [(table_hbm, table_ref), (samples_hbm.at[0], samples_ref.at[0]),
         (samples_hbm.at[1], samples_ref.at[1]), (index_hbm, index_ref)])]
    for load in loads:
        load.start()

    barrier = pltpu.get_barrier_semaphore()

    def after(step):
        ahead = my_i + step
        return jnp.where(ahead >= ni, ahead - ni, ahead)

    def around(body):
        lax.fori_loop(1, ni, lambda step, carry: (body(step), carry)[1], 0)

    def greet(peer_i, peer_j):
        pl.semaphore_signal(barrier, inc=1, device_id=(peer_i, peer_j),
                            device_id_type=pl.DeviceIdType.MESH)

    greet(my_i, other_j)

    def greet_both(step):
        greet(after(step), my_j)
        greet(after(step), other_j)

    around(greet_both)

    loads[0].wait()
    loads[1].wait()
    loads[2].wait()
    table = table_ref[...]
    half = table.shape[1] // 2
    first = dot(samples_ref[0], table)
    second = dot(samples_ref[1], table)
    re_ref[...] = first[:, :half] + second[:, half:]
    im_ref[...] = second[:, :half] - first[:, half:]
    parts = []
    for ref in (re_ref, im_ref):
        rows = [ref[pl.ds(t, nl, stride=t_loc), :].astype(BF16) for t in range(t_loc)]
        parts.append(exchange_blocks(rows, ni, CH_DEV))
    send_ref[...] = jnp.concatenate([jnp.concatenate([a, b], 1) for a, b in zip(*parts)], 0)

    pl.semaphore_wait(barrier, ni * nj - 1)

    rows_of = lambda i: pl.ds(pl.multiple_of(i * nl, nl), nl)
    mine = rows_of(my_i)

    def peer_of(step):
        if isinstance(step, int) and step == 0:
            return my_i
        usual = step - 2
        usual = jnp.where(usual >= ni - my_i, usual + 2, usual)
        moved = jnp.where(step <= 2, step - 1, lax.rem(my_i + usual, ni))
        return jnp.where((my_i >= 2) & (my_i < 16), moved, after(step))

    def block_copy(step, origin, plane):
        peer = peer_of(step)
        return pltpu.make_async_remote_copy(
            src_ref=send_ref.at[rows_of(peer), :],
            dst_ref=recv_ref.at[plane, rows_of(origin), :],
            send_sem=send_sem,
            recv_sem=recv_sem.at[plane],
            device_id=(peer, other_j if plane else my_j),
            device_id_type=pl.DeviceIdType.MESH,
        )

    def send(step):
        block_copy(step, my_i, 0).start()
        block_copy(step, my_i, 1).start()

    block_copy(0, my_i, 1).start()
    around(send)
    recv_ref[0, mine, :] = send_ref[mine, :]

    loads[3].wait()
    cosine, sine = steering_parts(index_ref[...])
    steer_ref[0] = cosine.astype(BF16)
    steer_ref[1] = sine.astype(BF16)

    span = 2 * t_loc
    row_id, col_id = iota((size, size), 0), iota((size, size), 1)

    def source(column):
        shift = (column % t_loc + my_i) % t_loc
        return column // t_loc % 2 * (t_loc * CH_DEV) + shift * CH_DEV + column // span

    order = jnp.where(row_id == source(col_id), 1.0, 0.0).astype(BF16)
    order_t = jnp.where(col_id == source(row_id), 1.0, 0.0).astype(BF16)
    order_j = jnp.where(row_id == source(col_id ^ t_loc), jnp.where(col_id & t_loc == 0, 1.0, -1.0), 0.0).astype(BF16)

    def prepare(plane):
        held = recv_ref[plane]
        zt = dot(order_t, held, NT).astype(BF16)
        z = dot(held, order).astype(BF16)
        zj = dot(held, order_j).astype(BF16)
        zjt = jnp.concatenate(
            [b for i in range(size // span) for b in
             (zt[i * span + t_loc : (i + 1) * span], -zt[i * span : i * span + t_loc])], 0)
        return z, zt, zj, zjt

    def sized(ref, plane):
        return pltpu.make_async_remote_copy(
            src_ref=ref, dst_ref=ref, send_sem=send_sem, recv_sem=recv_sem.at[plane],
            device_id=(my_i, other_j), device_id_type=pl.DeviceIdType.MESH)

    sized(recv_ref.at[0, : antennas - nl], 0).wait_recv()
    sized(recv_ref.at[1], 1).wait_recv()
    planes = [prepare(j) for j in range(nj)]

    groups = size // LANES
    per = CH_DEV // groups
    cols = nj * LANES
    wide = nj * span
    chan_of = lambda x: x // span % per
    lane_chan = chan_of(iota((1, cols), 1))
    half_ants = antennas // 2
    blocks = range(cols // span)
    rows_at = lambda i: slice(i * span, (i + 1) * span)
    lane = iota((span, LANES), 1)
    slot = lane // span
    packed_slot = iota((span, LANES), 1) // span
    first = iota((cols, LANES), 1) < wide

    def shifted(x, amount):
        return x if amount % LANES == 0 else pltpu.roll(x, amount % LANES, 1)

    def pack(grams):
        done = []
        for i in blocks:
            kept = None
            for g in range(groups):
                for j in range(nj):
                    to = g * nj + j
                    moved = shifted(grams[g][rows_at(i), j * LANES : (j + 1) * LANES], (to - i % per) * span)
                    kept = moved if kept is None else jnp.where(slot == to, moved, kept)
            done.append(kept)
        return jnp.concatenate(done, 0)

    def spread(x, g):
        x = x.astype(BF16)
        done = []
        for i in range(x.shape[0] // span):
            k = i % per
            done.append(jnp.concatenate(
                [jnp.where(packed_slot == k, shifted(x[rows_at(i)], (k - g * nj - j) * span), jnp.zeros((), BF16))
                 for j in range(nj)], 1))
        return jnp.concatenate(done, 0)

    def spread_all(x):
        return jnp.concatenate([spread(x, g) for g in range(groups)], 0)

    def pick(out):
        return jnp.where(first, out[:cols], out[cols:])

    def only(x, k):
        none = jnp.zeros((span, antennas), BF16)
        return jnp.concatenate([x[rows_at(i)] if i % per == k else none for i in blocks], 0)

    def magnitude(re, im):
        power = re * re + im * im
        return power * lax.rsqrt(jnp.maximum(power, 1e-37))

    def group_steps(g, keepers):
        cut = slice(g * LANES, (g + 1) * LANES)
        z = jnp.concatenate([p[0][:, cut] for p in planes], 1)
        zj = jnp.concatenate([p[2][:, cut] for p in planes], 1)
        zt, zjt = (jnp.concatenate([p[i][cut] for p in planes], 0) for i in (1, 3))
        keepers["gram"][g] = dot(zt, z) + dot(zjt, zj)
        keepers["pt"][g] = zt, zjt
        low_t = jnp.concatenate([zt[:, half_ants:], zjt[:, half_ants:]], 1)
        upper = jnp.concatenate([z[:half_ants], zj[:half_ants]], 0)
        yield
        for k in range(per):
            yield
            top = dot(upper, only(zt, k))
            top = magnitude(top[:half_ants], top[half_ants:])
            low = dot(z[half_ants:], only(low_t, k))
            low = magnitude(low[:, :half_ants], low[:, half_ants:])
            rows = jnp.max(jnp.sum(top, axis=1, keepdims=True), axis=0, keepdims=True)
            columns = jnp.sum(top[:, half_ants:], axis=0, keepdims=True) + jnp.sum(low, axis=0, keepdims=True)
            keepers["largest"][g][k] = jnp.maximum(rows, jnp.max(columns, axis=1, keepdims=True))

    kept = {"gram": {}, "pt": {}, "largest": [{}, {}]}
    for _ in itertools.zip_longest(*[group_steps(g, kept) for g in range(groups)]):
        pass

    gram = pack(kept["gram"])
    gram_b = gram.astype(BF16)
    square = pick(dot(spread_all(gram), gram_b))

    lane_row = iota((1, LANES), 1)
    on_diag = iota((cols, LANES), 1) % wide == iota((cols, LANES), 0) // LANES * span + iota((cols, LANES), 0) % span
    diagonal = jnp.where(on_diag, gram, 0.0)
    loads_of, largest_of = [], []
    for k in range(per):
        both = jnp.sum(diagonal[rows_at(k)] + diagonal[rows_at(per + k)], axis=0, keepdims=True)
        traces = [jnp.sum(jnp.where(lane_row // wide == g, both, 0.0), axis=1, keepdims=True) for g in range(groups)]
        loads_of.append(jnp.where(lane_row < wide, traces[0], traces[1]))
        largest_of.append(jnp.where(lane_row < wide, kept["largest"][0][k], kept["largest"][1][k]))
    load = (0.1 / antennas * 0.5) * jnp.concatenate(loads_of * nj, 0)
    bound = jnp.concatenate(largest_of * nj, 0) + load
    inv = 1.0 / bound
    r = 1.0 - load * inv
    r2 = r * r
    r4 = r2 * r2
    s = [1.0 + 0.0 * r]
    for _ in range(TERMS - 1):
        s.append(1.0 + r * s[-1])
    c = [s[TERMS - 2 - m] for m in range(TERMS - 1)]
    t0 = c[4] + r * (c[5] + r * c[6])
    p0 = c[0] + r * (c[1] + r * (c[2] + r * c[3])) + r4 * t0

    def by(v, count=cols):
        return jnp.concatenate([jnp.broadcast_to(v[i : i + 1], (span, LANES)) for i in range(count // span)], 0)

    x1 = by(inv) * gram
    x2 = by(2.0 * r) * x1 - by(inv * inv) * square
    out = dot(spread_all(x2), jnp.concatenate([x1.astype(BF16), x2.astype(BF16)], 1))
    x3 = by(r) * x2 + by(r2) * x1 - pick(out[:, :LANES])
    x4 = by(2.0 * r2) * x2 - pick(out[:, LANES:])
    tail = by(c[5]) * x1 + by(c[6]) * x2
    head = x1 + x2 + x3
    out = dot(spread_all(x4), jnp.concatenate([tail.astype(BF16), head.astype(BF16)], 1))
    poly = (by(c[1] + r4 * c[5]) * x1 + by(c[2] + r4 * c[6]) * x2 + by(c[3]) * x3 + by(t0) * x4
            - pick(out[:, :LANES]))
    own = (by(1.0 + r4, LANES) * head[:LANES] + by(s[3], LANES) * x4[:LANES]
           - jnp.where(first[:LANES], out[:LANES, LANES:], out[cols : cols + LANES, LANES:]))
    own_low = own - own.astype(BF16).astype(F32)

    for g in range(groups):
        zt, zjt = kept["pt"][g]
        pt = dot(zt, steer_ref[0], NT) + dot(zjt, steer_ref[1], NT)
        pth, ptl = split(pt)
        oh = spread(own, g)
        ends = dot(jnp.concatenate([spread(poly, g), oh, spread(own_low, g)], 0), pth)
        back = (ends[cols : cols + LANES] + ends[cols + LANES :]) + dot(oh, ptl)
        for k in range(per):
            energy = 0.0
            at = slice(k, k + 1), slice(g * wide, g * wide + 1)
            for j in range(nj):
                low = rows_at(j * per + k)
                energy += jnp.sum(pt[low] * (p0[at] * pt[low] - ends[low]), axis=0, keepdims=True)
            whole = s[TERMS - 1][at]
            response = antennas * whole - energy * inv[at]
            factor = lax.rsqrt(response * (bound[at] * (1.0 / (nj * t_loc))))
            beam = (whole * pt[rows_at(k)] - back[rows_at(k)]) * factor
            beam = beam.astype(BF16)
            out_ref[0, g * per + k] = beam[:t_loc]
            out_ref[1, g * per + k] = beam[t_loc:]

    sized(send_ref.at[: antennas - nl], 0).wait_send()
    sized(send_ref, 1).wait_send()


def fused_local(ni, nj, samples, steer_index):
    _, nl, t_loc, _ = samples.shape
    beams, antennas = steer_index.shape
    size = 2 * CH_DEV * t_loc
    vmem = pl.BlockSpec(memory_space=pltpu.VMEM)
    table = jnp.asarray(taper_table(CH_DEV * ni))
    out = pl.pallas_call(
        functools.partial(fused, ni, nj),
        out_shape=pltpu.VMEM((2, CH_DEV, t_loc, beams), BF16),
        in_specs=[pl.BlockSpec(memory_space=pl.ANY)] * 3,
        out_specs=vmem,
        scratch_shapes=[
            pltpu.VMEM((2, nl * t_loc, C), BF16),
            pltpu.VMEM(table.shape, BF16),
            pltpu.VMEM((beams, antennas), jnp.int32),
            pltpu.VMEM((nl * t_loc, CH_DEV * ni), F32),
            pltpu.VMEM((nl * t_loc, CH_DEV * ni), F32),
            pltpu.VMEM((antennas, size), BF16),
            pltpu.VMEM((nj, antennas, size), BF16),
            pltpu.VMEM((2, beams, antennas), BF16),
            pltpu.SemaphoreType.DMA((4,)),
            pltpu.SemaphoreType.DMA,
            pltpu.SemaphoreType.DMA((nj,)),
        ],
        compiler_params=pltpu.CompilerParams(collective_id=0, has_side_effects=True),
    )(samples.reshape(2, nl * t_loc, C), table, steer_index)
    return jnp.transpose(out, (0, 1, 3, 2))


def choose(ni, nj, samples, steer_index):
    _, nl, t_loc, _ = samples.shape
    beams, antennas = steer_index.shape
    tiled = nl == 16 and t_loc == 16 and CH_DEV * ni == LANES and antennas == nl * ni
    if tiled and nj == 2:
        return fused_local(ni, nj, samples, steer_index)
    return local(samples, steer_index)


def solution(mesh):
    return jax.shard_map(
        functools.partial(choose, mesh.shape["chan"], mesh.shape["tm"]),
        mesh=mesh,
        in_specs=(P(None, "chan", "tm", None), P()),
        out_specs=P(None, "chan", None, "tm"),
        check_vma=False,
    )
```

```python
import functools
import itertools
import math

import jax
import jax.numpy as jnp
import numpy as np
from jax import lax
from jax.experimental import pallas as pl
from jax.experimental.pallas import tpu as pltpu
from jax.sharding import PartitionSpec as P

C = 1024
PHASES = 256
CH_DEV = 8
ITERS = 3
TERMS = 2**ITERS
LANES = 128


HIGHEST = lax.Precision.HIGHEST
F32 = jnp.float32
BF16 = jnp.bfloat16
NT = (((1,), (1,)), ((), ()))


def transform_table(channels_all):
    offset = (C - channels_all) // 2
    channel_number = jnp.arange(channels_all, dtype=jnp.int32) + offset
    sample_number = jnp.arange(C, dtype=jnp.int32)
    phase_turns = channel_number[:, None] * sample_number[None, :] % C
    phase_angle = 2.0 * math.pi / C * phase_turns.astype(jnp.float32)
    window_taper = (
        0.5 - 0.5 * jnp.cos(2.0 * math.pi / C * sample_number.astype(jnp.float32))
    ) / math.sqrt(C)
    cosine = window_taper[None, :] * jnp.cos(phase_angle)
    sine_part = window_taper[None, :] * jnp.sin(phase_angle)
    coefficients = jnp.stack(
        [jnp.stack([cosine, sine_part], 1), jnp.stack([-sine_part, cosine], 1)], 0
    )
    return coefficients.astype(jnp.bfloat16)


def complex_product(left_real, left_imag, right_real, right_imag):
    real_part = jnp.dot(left_real, right_real, precision=HIGHEST) - jnp.dot(
        left_imag, right_imag, precision=HIGHEST
    )
    imag_part = jnp.dot(left_real, right_imag, precision=HIGHEST) + jnp.dot(
        left_imag, right_real, precision=HIGHEST
    )
    return (real_part, imag_part)


def invert_loaded(covariance_real, covariance_imag):
    matrix_order = covariance_real.shape[0]
    loading = 0.1 * jnp.mean(jnp.diagonal(covariance_real))
    identity = jnp.eye(matrix_order, dtype=jnp.float32)
    loaded = covariance_real + loading * identity
    magnitude = jnp.sqrt(loaded * loaded + covariance_imag * covariance_imag)
    largest = jnp.max(jnp.sum(magnitude, axis=1))

    def iterate(counter, state):
        approx_real, approx_imag = state
        image_real, image_imag = complex_product(loaded, covariance_imag, approx_real, approx_imag)
        square_real, square_imag = complex_product(approx_real, approx_imag, image_real, image_imag)
        return (2.0 * approx_real - square_real, 2.0 * approx_imag - square_imag)

    start_state = (identity / largest, jnp.zeros_like(identity))
    return lax.fori_loop(0, ITERS, iterate, start_state)


def form_weights(covariance_real, covariance_imag, steer_real, steer_imag):
    inverse_real, inverse_imag = invert_loaded(covariance_real, covariance_imag)
    gain_real, gain_imag = complex_product(inverse_real, inverse_imag, steer_real, steer_imag)
    response = jnp.sum(steer_real * gain_real + steer_imag * gain_imag, axis=0)
    factor = lax.rsqrt(response)
    return ((gain_real * factor).astype(jnp.bfloat16), (gain_imag * factor).astype(jnp.bfloat16))


def weights_stacked(covariance_real, covariance_imag, steer_real, steer_imag):
    weight_real, weight_imag = jax.vmap(form_weights, in_axes=(0, 0, None, None))(
        covariance_real, covariance_imag, steer_real, steer_imag
    )
    return jnp.stack([weight_real, weight_imag], 1)


def steering(steer_index):
    phase_angle = 2.0 * math.pi / PHASES * steer_index.astype(jnp.float32)
    return (jnp.cos(phase_angle).T, jnp.sin(phase_angle).T)


def apply_beams(weight_pair, spectrum):
    real_weight = weight_pair[:, 0]
    imag_weight = weight_pair[:, 1]
    beam_real = jnp.einsum(
        "knb,kns->kbs", real_weight, spectrum[0], preferred_element_type=jnp.float32
    ) + jnp.einsum("knb,kns->kbs", imag_weight, spectrum[1], preferred_element_type=jnp.float32)
    beam_imag = jnp.einsum(
        "knb,kns->kbs", real_weight, spectrum[1], preferred_element_type=jnp.float32
    ) - jnp.einsum("knb,kns->kbs", imag_weight, spectrum[0], preferred_element_type=jnp.float32)
    return jnp.stack([beam_real, beam_imag], 0).astype(jnp.bfloat16)


def local(samples, steer_index):
    channels_all = CH_DEV * lax.axis_size("chan")
    coefficients = transform_table(channels_all)
    spectra = lax.dot_general(
        coefficients, samples, (((2, 3), (0, 3)), ((), ())), preferred_element_type=jnp.float32
    ).astype(jnp.bfloat16)
    steer_real, steer_imag = steering(steer_index)
    turned = lax.all_to_all(
        lax.all_to_all(spectra, "chan", split_axis=1, concat_axis=2, tiled=True),
        "tm",
        split_axis=1,
        concat_axis=3,
        tiled=True,
    )
    outer_sums = jnp.einsum("ikns,jkms->kinjm", turned, turned, preferred_element_type=jnp.float32)
    snapshots = turned.shape[3]
    covariance_real = (outer_sums[:, 0, :, 0, :] + outer_sums[:, 1, :, 1, :]) / snapshots
    covariance_imag = (outer_sums[:, 1, :, 0, :] - outer_sums[:, 0, :, 1, :]) / snapshots
    weight_pair = weights_stacked(covariance_real, covariance_imag, steer_real, steer_imag)
    local_beams = apply_beams(weight_pair, turned)
    return lax.all_to_all(local_beams, "tm", split_axis=3, concat_axis=1, tiled=True)


def taper_table(channels_all):
    offset = (C - channels_all) // 2
    channel = np.arange(channels_all) + offset
    sample = np.arange(C)
    angle = 2.0 * math.pi / C * (channel[None, :] * sample[:, None] % C)
    taper = (0.5 - 0.5 * np.cos(2.0 * math.pi / C * sample)) / math.sqrt(C)
    both = np.concatenate([taper[:, None] * np.cos(angle), taper[:, None] * np.sin(angle)], 1)
    return both.astype(np.float32).astype(BF16)


def iota(shape, axis):
    return lax.broadcasted_iota(jnp.int32, shape, axis)


def dot(a, b, dims=(((1,), (0,)), ((), ()))):
    return lax.dot_general(a, b, dims, preferred_element_type=F32)


def split(x):
    high = x.astype(BF16)
    return high, (x - high.astype(F32)).astype(BF16)


def exchange_blocks(rows, count, width):
    place = iota(rows[0].shape, 1) // width
    turned = [rows[0]] + [pltpu.roll(rows[t], t * width, 1) for t in range(1, count)]
    rows = [turned[-i % count] for i in range(count)]
    step = 1
    while step < count:
        take = place & step != 0
        rows = [jnp.where(take, rows[i - step], rows[i]) for i in range(count)]
        step *= 2
    return rows


def steering_parts(index):
    turn = index & (PHASES - 1)
    quarter = PHASES // 4
    quadrant = (turn + quarter // 2) // quarter
    x = (turn - quarter * quadrant).astype(F32) * (2.0 * math.pi / PHASES)
    y = x * x
    s = x * (1.0 + y * (-1.0 / 6 + y * (1.0 / 120 + y * (-1.0 / 5040 + y * (1.0 / 362880)))))
    c = 1.0 + y * (-0.5 + y * (1.0 / 24 + y * (-1.0 / 720 + y * (1.0 / 40320 - y * (1.0 / 3628800)))))
    odd = quadrant & 1 == 1
    flip_c = (quadrant + 1) & 2 == 2
    flip_s = quadrant & 2 == 2
    cosine = jnp.where(odd, s, c)
    sine = jnp.where(odd, c, s)
    return jnp.where(flip_c, -cosine, cosine), jnp.where(flip_s, -sine, sine)


def fused(ni, nj, samples_hbm, table_hbm, index_hbm, out_ref, samples_ref, table_ref, index_ref, re_ref,
          im_ref, send_ref, recv_ref, steer_ref, load_sem, send_sem, recv_sem, told):
    nl, t_loc, q = 16, 16, 2 * CH_DEV
    antennas = ni * nl
    size = q * t_loc
    my_i, my_j = lax.axis_index("chan"), lax.axis_index("tm")
    other_j = 1 - my_j

    loads = [pltpu.make_async_copy(src, dst, load_sem.at[i]) for i, (src, dst) in enumerate(
        [(table_hbm, table_ref), (samples_hbm.at[0], samples_ref.at[0]),
         (samples_hbm.at[1], samples_ref.at[1]), (index_hbm, index_ref)])]
    for load in loads:
        load.start()

    barrier = pltpu.get_barrier_semaphore()

    def after(step):
        ahead = my_i + step
        return jnp.where(ahead >= ni, ahead - ni, ahead)

    def around(body):
        lax.fori_loop(1, ni, lambda step, carry: (body(step), carry)[1], 0)

    def greet(peer_i, peer_j):
        pl.semaphore_signal(barrier, inc=1, device_id=(peer_i, peer_j),
                            device_id_type=pl.DeviceIdType.MESH)

    greet(my_i, other_j)

    level = ni // 4
    my_level = my_i // level

    def greet_both(step):
        peer = after(step)
        near = (peer >= 2 * level) | (my_level <= peer // level + 1)

        @pl.when(near)
        def _():
            greet(peer, my_j)
            greet(peer, other_j)

    around(greet_both)

    loads[0].wait()
    loads[1].wait()
    loads[2].wait()
    table = table_ref[...]
    half = table.shape[1] // 2
    first = dot(samples_ref[0], table)
    second = dot(samples_ref[1], table)
    re_ref[...] = first[:, :half] + second[:, half:]
    im_ref[...] = second[:, :half] - first[:, half:]
    parts = []
    for ref in (re_ref, im_ref):
        rows = [ref[pl.ds(t, nl, stride=t_loc), :].astype(BF16) for t in range(t_loc)]
        parts.append(exchange_blocks(rows, ni, CH_DEV))
    send_ref[...] = jnp.concatenate([jnp.concatenate([a, b], 1) for a, b in zip(*parts)], 0)

    pl.semaphore_wait(barrier, jnp.minimum(my_level + 2, 4) * (level * nj) - 1)

    def tell(distance, which):
        pl.semaphore_signal(told.at[which], inc=1, device_id=(my_i - distance * level, my_j),
                            device_id_type=pl.DeviceIdType.MESH)

    @pl.when(my_level == 1)
    def _():
        tell(1, 0)

    @pl.when(my_level == 2)
    def _():
        tell(2, 1)
        tell(1, 1)

    rows_of = lambda i: pl.ds(pl.multiple_of(i * nl, nl), nl)
    mine = rows_of(my_i)

    def peer_of(step):
        if isinstance(step, int) and step == 0:
            return my_i
        begin = jnp.where(my_level == 2, 2, jnp.where(my_level == 1, 11, jnp.where(my_level == 0, 0, 3)))
        usual = lax.rem(step - 3 + begin, 13) + 1
        usual = jnp.where(usual >= ni - my_i, usual + 2, usual)
        moved = jnp.where(step <= 2, step - 1, lax.rem(my_i + usual, ni))
        return jnp.where((my_i >= 2) & (my_i < 16), moved, after(step))

    def block_copy(step, origin, plane):
        peer = peer_of(step)
        return pltpu.make_async_remote_copy(
            src_ref=send_ref.at[rows_of(peer), :],
            dst_ref=recv_ref.at[plane, rows_of(origin), :],
            send_sem=send_sem,
            recv_sem=recv_sem.at[plane],
            device_id=(peer, other_j if plane else my_j),
            device_id_type=pl.DeviceIdType.MESH,
        )

    def send(step):
        peer = peer_of(step)

        @pl.when((my_level == 0) & (peer == 2 * level))
        def _():
            pl.semaphore_wait(told.at[0], 1)

        @pl.when((my_level <= 1) & (peer == 3 * level))
        def _():
            pl.semaphore_wait(told.at[1], 1)

        block_copy(step, my_i, 0).start()
        block_copy(step, my_i, 1).start()

    block_copy(0, my_i, 1).start()
    around(send)
    recv_ref[0, mine, :] = send_ref[mine, :]

    loads[3].wait()
    cosine, sine = steering_parts(index_ref[...])
    steer_ref[0] = cosine.astype(BF16)
    steer_ref[1] = sine.astype(BF16)

    span = 2 * t_loc
    row_id, col_id = iota((size, size), 0), iota((size, size), 1)

    def source(column):
        shift = (column % t_loc + my_i) % t_loc
        return column // t_loc % 2 * (t_loc * CH_DEV) + shift * CH_DEV + column // span

    order = jnp.where(row_id == source(col_id), 1.0, 0.0).astype(BF16)
    order_t = jnp.where(col_id == source(row_id), 1.0, 0.0).astype(BF16)
    order_j = jnp.where(row_id == source(col_id ^ t_loc), jnp.where(col_id & t_loc == 0, 1.0, -1.0), 0.0).astype(BF16)

    def prepare(plane):
        held = recv_ref[plane]
        zt = dot(order_t, held, NT).astype(BF16)
        z = dot(held, order).astype(BF16)
        zj = dot(held, order_j).astype(BF16)
        zjt = jnp.concatenate(
            [b for i in range(size // span) for b in
             (zt[i * span + t_loc : (i + 1) * span], -zt[i * span : i * span + t_loc])], 0)
        return z, zt, zj, zjt

    def sized(ref, plane):
        return pltpu.make_async_remote_copy(
            src_ref=ref, dst_ref=ref, send_sem=send_sem, recv_sem=recv_sem.at[plane],
            device_id=(my_i, other_j), device_id_type=pl.DeviceIdType.MESH)

    sized(recv_ref.at[0, : antennas - nl], 0).wait_recv()
    sized(recv_ref.at[1], 1).wait_recv()
    planes = [prepare(j) for j in range(nj)]

    groups = size // LANES
    per = CH_DEV // groups
    cols = nj * LANES
    wide = nj * span
    chan_of = lambda x: x // span % per
    lane_chan = chan_of(iota((1, cols), 1))
    half_ants = antennas // 2
    blocks = range(cols // span)
    rows_at = lambda i: slice(i * span, (i + 1) * span)
    lane = iota((span, LANES), 1)
    slot = lane // span
    packed_slot = iota((span, LANES), 1) // span
    first = iota((cols, LANES), 1) < wide

    def shifted(x, amount):
        return x if amount % LANES == 0 else pltpu.roll(x, amount % LANES, 1)

    def pack(grams):
        done = []
        for i in blocks:
            kept = None
            for g in range(groups):
                for j in range(nj):
                    to = g * nj + j
                    moved = shifted(grams[g][rows_at(i), j * LANES : (j + 1) * LANES], (to - i % per) * span)
                    kept = moved if kept is None else jnp.where(slot == to, moved, kept)
            done.append(kept)
        return jnp.concatenate(done, 0)

    def spread(x, g):
        x = x.astype(BF16)
        done = []
        for i in range(x.shape[0] // span):
            k = i % per
            done.append(jnp.concatenate(
                [jnp.where(packed_slot == k, shifted(x[rows_at(i)], (k - g * nj - j) * span), jnp.zeros((), BF16))
                 for j in range(nj)], 1))
        return jnp.concatenate(done, 0)

    def spread_all(x):
        return jnp.concatenate([spread(x, g) for g in range(groups)], 0)

    def pick(out):
        return jnp.where(first, out[:cols], out[cols:])

    def only(x, k):
        none = jnp.zeros((span, antennas), BF16)
        return jnp.concatenate([x[rows_at(i)] if i % per == k else none for i in blocks], 0)

    def magnitude(re, im):
        power = re * re + im * im
        return power * lax.rsqrt(jnp.maximum(power, 1e-37))

    def group_steps(g, keepers):
        cut = slice(g * LANES, (g + 1) * LANES)
        z = jnp.concatenate([p[0][:, cut] for p in planes], 1)
        zj = jnp.concatenate([p[2][:, cut] for p in planes], 1)
        zt, zjt = (jnp.concatenate([p[i][cut] for p in planes], 0) for i in (1, 3))
        keepers["gram"][g] = dot(zt, z) + dot(zjt, zj)
        keepers["pt"][g] = zt, zjt
        low_t = jnp.concatenate([zt[:, half_ants:], zjt[:, half_ants:]], 1)
        upper = jnp.concatenate([z[:half_ants], zj[:half_ants]], 0)
        yield
        for k in range(per):
            yield
            top = dot(upper, only(zt, k))
            top = magnitude(top[:half_ants], top[half_ants:])
            low = dot(z[half_ants:], only(low_t, k))
            low = magnitude(low[:, :half_ants], low[:, half_ants:])
            rows = jnp.max(jnp.sum(top, axis=1, keepdims=True), axis=0, keepdims=True)
            columns = jnp.sum(top[:, half_ants:], axis=0, keepdims=True) + jnp.sum(low, axis=0, keepdims=True)
            keepers["largest"][g][k] = jnp.maximum(rows, jnp.max(columns, axis=1, keepdims=True))

    kept = {"gram": {}, "pt": {}, "largest": [{}, {}]}
    for _ in itertools.zip_longest(*[group_steps(g, kept) for g in range(groups)]):
        pass

    gram = pack(kept["gram"])
    gram_b = gram.astype(BF16)
    square = pick(dot(spread_all(gram), gram_b))

    lane_row = iota((1, LANES), 1)
    on_diag = iota((cols, LANES), 1) % wide == iota((cols, LANES), 0) // LANES * span + iota((cols, LANES), 0) % span
    diagonal = jnp.where(on_diag, gram, 0.0)
    loads_of, largest_of = [], []
    for k in range(per):
        both = jnp.sum(diagonal[rows_at(k)] + diagonal[rows_at(per + k)], axis=0, keepdims=True)
        traces = [jnp.sum(jnp.where(lane_row // wide == g, both, 0.0), axis=1, keepdims=True) for g in range(groups)]
        loads_of.append(jnp.where(lane_row < wide, traces[0], traces[1]))
        largest_of.append(jnp.where(lane_row < wide, kept["largest"][0][k], kept["largest"][1][k]))
    load = (0.1 / antennas * 0.5) * jnp.concatenate(loads_of * nj, 0)
    bound = jnp.concatenate(largest_of * nj, 0) + load
    inv = 1.0 / bound
    r = 1.0 - load * inv
    r2 = r * r
    r4 = r2 * r2
    s = [1.0 + 0.0 * r]
    for _ in range(TERMS - 1):
        s.append(1.0 + r * s[-1])
    c = [s[TERMS - 2 - m] for m in range(TERMS - 1)]
    t0 = c[4] + r * (c[5] + r * c[6])
    p0 = c[0] + r * (c[1] + r * (c[2] + r * c[3])) + r4 * t0

    def by(v, count=cols):
        return jnp.concatenate([jnp.broadcast_to(v[i : i + 1], (span, LANES)) for i in range(count // span)], 0)

    x1 = by(inv) * gram
    x2 = by(2.0 * r) * x1 - by(inv * inv) * square
    out = dot(spread_all(x2), jnp.concatenate([x1.astype(BF16), x2.astype(BF16)], 1))
    x3 = by(r) * x2 + by(r2) * x1 - pick(out[:, :LANES])
    x4 = by(2.0 * r2) * x2 - pick(out[:, LANES:])
    tail = by(c[5]) * x1 + by(c[6]) * x2
    head = x1 + x2 + x3
    out = dot(spread_all(x4), jnp.concatenate([tail.astype(BF16), head.astype(BF16)], 1))
    poly = (by(c[1] + r4 * c[5]) * x1 + by(c[2] + r4 * c[6]) * x2 + by(c[3]) * x3 + by(t0) * x4
            - pick(out[:, :LANES]))
    own = (by(1.0 + r4, LANES) * head[:LANES] + by(s[3], LANES) * x4[:LANES]
           - jnp.where(first[:LANES], out[:LANES, LANES:], out[cols : cols + LANES, LANES:]))
    own_low = own - own.astype(BF16).astype(F32)

    for g in range(groups):
        zt, zjt = kept["pt"][g]
        pt = dot(zt, steer_ref[0], NT) + dot(zjt, steer_ref[1], NT)
        pth, ptl = split(pt)
        oh = spread(own, g)
        ends = dot(jnp.concatenate([spread(poly, g), oh, spread(own_low, g)], 0), pth)
        back = (ends[cols : cols + LANES] + ends[cols + LANES :]) + dot(oh, ptl)
        for k in range(per):
            energy = 0.0
            at = slice(k, k + 1), slice(g * wide, g * wide + 1)
            for j in range(nj):
                low = rows_at(j * per + k)
                energy += jnp.sum(pt[low] * (p0[at] * pt[low] - ends[low]), axis=0, keepdims=True)
            whole = s[TERMS - 1][at]
            response = antennas * whole - energy * inv[at]
            factor = lax.rsqrt(response * (bound[at] * (1.0 / (nj * t_loc))))
            beam = (whole * pt[rows_at(k)] - back[rows_at(k)]) * factor
            beam = beam.astype(BF16)
            out_ref[0, g * per + k] = beam[:t_loc]
            out_ref[1, g * per + k] = beam[t_loc:]

    sized(send_ref.at[: antennas - nl], 0).wait_send()
    sized(send_ref, 1).wait_send()


def fused_local(ni, nj, samples, steer_index):
    _, nl, t_loc, _ = samples.shape
    beams, antennas = steer_index.shape
    size = 2 * CH_DEV * t_loc
    vmem = pl.BlockSpec(memory_space=pltpu.VMEM)
    table = jnp.asarray(taper_table(CH_DEV * ni))
    out = pl.pallas_call(
        functools.partial(fused, ni, nj),
        out_shape=pltpu.VMEM((2, CH_DEV, t_loc, beams), BF16),
        in_specs=[pl.BlockSpec(memory_space=pl.ANY)] * 3,
        out_specs=vmem,
        scratch_shapes=[
            pltpu.VMEM((2, nl * t_loc, C), BF16),
            pltpu.VMEM(table.shape, BF16),
            pltpu.VMEM((beams, antennas), jnp.int32),
            pltpu.VMEM((nl * t_loc, CH_DEV * ni), F32),
            pltpu.VMEM((nl * t_loc, CH_DEV * ni), F32),
            pltpu.VMEM((antennas, size), BF16),
            pltpu.VMEM((nj, antennas, size), BF16),
            pltpu.VMEM((2, beams, antennas), BF16),
            pltpu.SemaphoreType.DMA((4,)),
            pltpu.SemaphoreType.DMA,
            pltpu.SemaphoreType.DMA((nj,)),
            pltpu.SemaphoreType.REGULAR((2,)),
        ],
        compiler_params=pltpu.CompilerParams(collective_id=0, has_side_effects=True),
    )(samples.reshape(2, nl * t_loc, C), table, steer_index)
    return jnp.transpose(out, (0, 1, 3, 2))


def choose(ni, nj, samples, steer_index):
    _, nl, t_loc, _ = samples.shape
    beams, antennas = steer_index.shape
    tiled = nl == 16 and t_loc == 16 and CH_DEV * ni == LANES and antennas == nl * ni
    if tiled and nj == 2:
        return fused_local(ni, nj, samples, steer_index)
    return local(samples, steer_index)


def solution(mesh):
    return jax.shard_map(
        functools.partial(choose, mesh.shape["chan"], mesh.shape["tm"]),
        mesh=mesh,
        in_specs=(P(None, "chan", "tm", None), P()),
        out_specs=P(None, "chan", None, "tm"),
        check_vma=False,
    )
```

```python
import functools
import itertools
import math

import jax
import jax.numpy as jnp
import numpy as np
from jax import lax
from jax.experimental import pallas as pl
from jax.experimental.pallas import tpu as pltpu
from jax.sharding import PartitionSpec as P

C = 1024
PHASES = 256
CH_DEV = 8
ITERS = 3
TERMS = 2**ITERS
LANES = 128


HIGHEST = lax.Precision.HIGHEST
F32 = jnp.float32
BF16 = jnp.bfloat16
NT = (((1,), (1,)), ((), ()))


def transform_table(channels_all):
    offset = (C - channels_all) // 2
    channel_number = jnp.arange(channels_all, dtype=jnp.int32) + offset
    sample_number = jnp.arange(C, dtype=jnp.int32)
    phase_turns = channel_number[:, None] * sample_number[None, :] % C
    phase_angle = 2.0 * math.pi / C * phase_turns.astype(jnp.float32)
    window_taper = (
        0.5 - 0.5 * jnp.cos(2.0 * math.pi / C * sample_number.astype(jnp.float32))
    ) / math.sqrt(C)
    cosine = window_taper[None, :] * jnp.cos(phase_angle)
    sine_part = window_taper[None, :] * jnp.sin(phase_angle)
    coefficients = jnp.stack(
        [jnp.stack([cosine, sine_part], 1), jnp.stack([-sine_part, cosine], 1)], 0
    )
    return coefficients.astype(jnp.bfloat16)


def complex_product(left_real, left_imag, right_real, right_imag):
    real_part = jnp.dot(left_real, right_real, precision=HIGHEST) - jnp.dot(
        left_imag, right_imag, precision=HIGHEST
    )
    imag_part = jnp.dot(left_real, right_imag, precision=HIGHEST) + jnp.dot(
        left_imag, right_real, precision=HIGHEST
    )
    return (real_part, imag_part)


def invert_loaded(covariance_real, covariance_imag):
    matrix_order = covariance_real.shape[0]
    loading = 0.1 * jnp.mean(jnp.diagonal(covariance_real))
    identity = jnp.eye(matrix_order, dtype=jnp.float32)
    loaded = covariance_real + loading * identity
    magnitude = jnp.sqrt(loaded * loaded + covariance_imag * covariance_imag)
    largest = jnp.max(jnp.sum(magnitude, axis=1))

    def iterate(counter, state):
        approx_real, approx_imag = state
        image_real, image_imag = complex_product(loaded, covariance_imag, approx_real, approx_imag)
        square_real, square_imag = complex_product(approx_real, approx_imag, image_real, image_imag)
        return (2.0 * approx_real - square_real, 2.0 * approx_imag - square_imag)

    start_state = (identity / largest, jnp.zeros_like(identity))
    return lax.fori_loop(0, ITERS, iterate, start_state)


def form_weights(covariance_real, covariance_imag, steer_real, steer_imag):
    inverse_real, inverse_imag = invert_loaded(covariance_real, covariance_imag)
    gain_real, gain_imag = complex_product(inverse_real, inverse_imag, steer_real, steer_imag)
    response = jnp.sum(steer_real * gain_real + steer_imag * gain_imag, axis=0)
    factor = lax.rsqrt(response)
    return ((gain_real * factor).astype(jnp.bfloat16), (gain_imag * factor).astype(jnp.bfloat16))


def weights_stacked(covariance_real, covariance_imag, steer_real, steer_imag):
    weight_real, weight_imag = jax.vmap(form_weights, in_axes=(0, 0, None, None))(
        covariance_real, covariance_imag, steer_real, steer_imag
    )
    return jnp.stack([weight_real, weight_imag], 1)


def steering(steer_index):
    phase_angle = 2.0 * math.pi / PHASES * steer_index.astype(jnp.float32)
    return (jnp.cos(phase_angle).T, jnp.sin(phase_angle).T)


def apply_beams(weight_pair, spectrum):
    real_weight = weight_pair[:, 0]
    imag_weight = weight_pair[:, 1]
    beam_real = jnp.einsum(
        "knb,kns->kbs", real_weight, spectrum[0], preferred_element_type=jnp.float32
    ) + jnp.einsum("knb,kns->kbs", imag_weight, spectrum[1], preferred_element_type=jnp.float32)
    beam_imag = jnp.einsum(
        "knb,kns->kbs", real_weight, spectrum[1], preferred_element_type=jnp.float32
    ) - jnp.einsum("knb,kns->kbs", imag_weight, spectrum[0], preferred_element_type=jnp.float32)
    return jnp.stack([beam_real, beam_imag], 0).astype(jnp.bfloat16)


def local(samples, steer_index):
    channels_all = CH_DEV * lax.axis_size("chan")
    coefficients = transform_table(channels_all)
    spectra = lax.dot_general(
        coefficients, samples, (((2, 3), (0, 3)), ((), ())), preferred_element_type=jnp.float32
    ).astype(jnp.bfloat16)
    steer_real, steer_imag = steering(steer_index)
    turned = lax.all_to_all(
        lax.all_to_all(spectra, "chan", split_axis=1, concat_axis=2, tiled=True),
        "tm",
        split_axis=1,
        concat_axis=3,
        tiled=True,
    )
    outer_sums = jnp.einsum("ikns,jkms->kinjm", turned, turned, preferred_element_type=jnp.float32)
    snapshots = turned.shape[3]
    covariance_real = (outer_sums[:, 0, :, 0, :] + outer_sums[:, 1, :, 1, :]) / snapshots
    covariance_imag = (outer_sums[:, 1, :, 0, :] - outer_sums[:, 0, :, 1, :]) / snapshots
    weight_pair = weights_stacked(covariance_real, covariance_imag, steer_real, steer_imag)
    local_beams = apply_beams(weight_pair, turned)
    return lax.all_to_all(local_beams, "tm", split_axis=3, concat_axis=1, tiled=True)


def taper_table(channels_all):
    offset = (C - channels_all) // 2
    channel = np.arange(channels_all) + offset
    sample = np.arange(C)
    angle = 2.0 * math.pi / C * (channel[None, :] * sample[:, None] % C)
    taper = (0.5 - 0.5 * np.cos(2.0 * math.pi / C * sample)) / math.sqrt(C)
    both = np.concatenate([taper[:, None] * np.cos(angle), taper[:, None] * np.sin(angle)], 1)
    return both.astype(np.float32).astype(BF16)


def iota(shape, axis):
    return lax.broadcasted_iota(jnp.int32, shape, axis)


def dot(a, b, dims=(((1,), (0,)), ((), ()))):
    return lax.dot_general(a, b, dims, preferred_element_type=F32)


def split(x):
    high = x.astype(BF16)
    return high, (x - high.astype(F32)).astype(BF16)


def exchange_blocks(rows, count, width):
    place = iota(rows[0].shape, 1) // width
    turned = [rows[0]] + [pltpu.roll(rows[t], t * width, 1) for t in range(1, count)]
    rows = [turned[-i % count] for i in range(count)]
    step = 1
    while step < count:
        take = place & step != 0
        rows = [jnp.where(take, rows[i - step], rows[i]) for i in range(count)]
        step *= 2
    return rows


def steering_parts(index):
    turn = index & (PHASES - 1)
    quarter = PHASES // 4
    quadrant = (turn + quarter // 2) // quarter
    x = (turn - quarter * quadrant).astype(F32) * (2.0 * math.pi / PHASES)
    y = x * x
    s = x * (1.0 + y * (-1.0 / 6 + y * (1.0 / 120 + y * (-1.0 / 5040 + y * (1.0 / 362880)))))
    c = 1.0 + y * (-0.5 + y * (1.0 / 24 + y * (-1.0 / 720 + y * (1.0 / 40320 - y * (1.0 / 3628800)))))
    odd = quadrant & 1 == 1
    flip_c = (quadrant + 1) & 2 == 2
    flip_s = quadrant & 2 == 2
    cosine = jnp.where(odd, s, c)
    sine = jnp.where(odd, c, s)
    return jnp.where(flip_c, -cosine, cosine), jnp.where(flip_s, -sine, sine)


def fused(ni, nj, samples_hbm, table_hbm, index_hbm, out_ref, samples_ref, table_ref, index_ref, re_ref,
          im_ref, send_ref, recv_ref, steer_ref, load_sem, send_sem, recv_sem, told):
    nl, t_loc, q = 16, 16, 2 * CH_DEV
    antennas = ni * nl
    size = q * t_loc
    my_i, my_j = lax.axis_index("chan"), lax.axis_index("tm")
    other_j = 1 - my_j

    pieces = 2
    depth = table_ref.shape[0] // pieces
    moves = []
    for i in range(pieces):
        at = slice(i * depth, (i + 1) * depth)
        moves.append((table_hbm.at[at], table_ref.at[at]))
        moves.append((samples_hbm.at[:, :, at], samples_ref.at[:, :, at]))
    moves.append((index_hbm, index_ref))
    loads = [pltpu.make_async_copy(src, dst, load_sem.at[i]) for i, (src, dst) in enumerate(moves)]
    for load in loads:
        load.start()

    barrier = pltpu.get_barrier_semaphore()

    def after(step):
        ahead = my_i + step
        return jnp.where(ahead >= ni, ahead - ni, ahead)

    def around(body):
        lax.fori_loop(1, ni, lambda step, carry: (body(step), carry)[1], 0)

    def greet(peer_i, peer_j):
        pl.semaphore_signal(barrier, inc=1, device_id=(peer_i, peer_j),
                            device_id_type=pl.DeviceIdType.MESH)

    greet(my_i, other_j)

    level = ni // 4
    my_level = my_i // level

    def greet_both(step):
        peer = after(step)
        near = (peer >= 2 * level) | (my_level <= peer // level + 1)

        @pl.when(near)
        def _():
            greet(peer, my_j)
            greet(peer, other_j)

    around(greet_both)

    half = table_ref.shape[1] // 2
    first = second = 0.0
    for i in range(pieces):
        at = slice(i * depth, (i + 1) * depth)
        loads[2 * i].wait()
        loads[2 * i + 1].wait()
        first += dot(samples_ref[0, :, at], table_ref[at])
        second += dot(samples_ref[1, :, at], table_ref[at])
    re_ref[...] = first[:, :half] + second[:, half:]
    im_ref[...] = second[:, :half] - first[:, half:]
    parts = []
    for ref in (re_ref, im_ref):
        rows = [ref[pl.ds(t, nl, stride=t_loc), :].astype(BF16) for t in range(t_loc)]
        parts.append(exchange_blocks(rows, ni, CH_DEV))
    send_ref[...] = jnp.concatenate([jnp.concatenate([a, b], 1) for a, b in zip(*parts)], 0)

    pl.semaphore_wait(barrier, jnp.minimum(my_level + 2, 4) * (level * nj) - 1)

    def tell(distance, which):
        pl.semaphore_signal(told.at[which], inc=1, device_id=(my_i - distance * level, my_j),
                            device_id_type=pl.DeviceIdType.MESH)

    @pl.when(my_level == 1)
    def _():
        tell(1, 0)

    @pl.when(my_level == 2)
    def _():
        tell(2, 1)
        tell(1, 1)

    rows_of = lambda i: pl.ds(pl.multiple_of(i * nl, nl), nl)
    mine = rows_of(my_i)

    def peer_of(step):
        if isinstance(step, int) and step == 0:
            return my_i
        begin = jnp.where(my_level == 2, 2, jnp.where(my_level == 1, 11, jnp.where(my_level == 0, 0, 3)))
        usual = lax.rem(step - 3 + begin, 13) + 1
        usual = jnp.where(usual >= ni - my_i, usual + 2, usual)
        moved = jnp.where(step <= 2, step - 1, lax.rem(my_i + usual, ni))
        return jnp.where((my_i >= 2) & (my_i < 16), moved, after(step))

    def block_copy(step, origin, plane):
        peer = peer_of(step)
        return pltpu.make_async_remote_copy(
            src_ref=send_ref.at[rows_of(peer), :],
            dst_ref=recv_ref.at[plane, rows_of(origin), :],
            send_sem=send_sem,
            recv_sem=recv_sem.at[plane],
            device_id=(peer, other_j if plane else my_j),
            device_id_type=pl.DeviceIdType.MESH,
        )

    def send(step):
        peer = peer_of(step)

        @pl.when((my_level == 0) & (peer == 2 * level))
        def _():
            pl.semaphore_wait(told.at[0], 1)

        @pl.when((my_level <= 1) & (peer == 3 * level))
        def _():
            pl.semaphore_wait(told.at[1], 1)

        block_copy(step, my_i, 1).start()
        block_copy(step, my_i, 0).start()

    block_copy(0, my_i, 1).start()
    around(send)
    recv_ref[0, mine, :] = send_ref[mine, :]

    loads[-1].wait()
    cosine, sine = steering_parts(index_ref[...])
    steer_ref[0] = cosine.astype(BF16)
    steer_ref[1] = sine.astype(BF16)

    span = 2 * t_loc
    row_id, col_id = iota((size, size), 0), iota((size, size), 1)

    def source(column):
        shift = (column % t_loc + my_i) % t_loc
        return column // t_loc % 2 * (t_loc * CH_DEV) + shift * CH_DEV + column // span

    order = jnp.where(row_id == source(col_id), 1.0, 0.0).astype(BF16)
    order_t = jnp.where(col_id == source(row_id), 1.0, 0.0).astype(BF16)
    order_j = jnp.where(row_id == source(col_id ^ t_loc), jnp.where(col_id & t_loc == 0, 1.0, -1.0), 0.0).astype(BF16)

    def prepare(plane):
        held = recv_ref[plane]
        zt = dot(order_t, held, NT).astype(BF16)
        z = dot(held, order).astype(BF16)
        zj = dot(held, order_j).astype(BF16)
        zjt = jnp.concatenate(
            [b for i in range(size // span) for b in
             (zt[i * span + t_loc : (i + 1) * span], -zt[i * span : i * span + t_loc])], 0)
        return z, zt, zj, zjt

    def sized(ref, plane):
        return pltpu.make_async_remote_copy(
            src_ref=ref, dst_ref=ref, send_sem=send_sem, recv_sem=recv_sem.at[plane],
            device_id=(my_i, other_j), device_id_type=pl.DeviceIdType.MESH)

    sized(recv_ref.at[0, : antennas - nl], 0).wait_recv()
    sized(recv_ref.at[1], 1).wait_recv()
    planes = [prepare(j) for j in range(nj)]

    groups = size // LANES
    per = CH_DEV // groups
    cols = nj * LANES
    wide = nj * span
    chan_of = lambda x: x // span % per
    lane_chan = chan_of(iota((1, cols), 1))
    half_ants = antennas // 2
    blocks = range(cols // span)
    rows_at = lambda i: slice(i * span, (i + 1) * span)
    lane = iota((span, LANES), 1)
    slot = lane // span
    packed_slot = iota((span, LANES), 1) // span
    first = iota((cols, LANES), 1) < wide

    def shifted(x, amount):
        return x if amount % LANES == 0 else pltpu.roll(x, amount % LANES, 1)

    def pack(grams):
        done = []
        for i in blocks:
            kept = None
            for g in range(groups):
                for j in range(nj):
                    to = g * nj + j
                    moved = shifted(grams[g][rows_at(i), j * LANES : (j + 1) * LANES], (to - i % per) * span)
                    kept = moved if kept is None else jnp.where(slot == to, moved, kept)
            done.append(kept)
        return jnp.concatenate(done, 0)

    def spread(x, g):
        x = x.astype(BF16)
        done = []
        for i in range(x.shape[0] // span):
            k = i % per
            done.append(jnp.concatenate(
                [jnp.where(packed_slot == k, shifted(x[rows_at(i)], (k - g * nj - j) * span), jnp.zeros((), BF16))
                 for j in range(nj)], 1))
        return jnp.concatenate(done, 0)

    def spread_all(x):
        return jnp.concatenate([spread(x, g) for g in range(groups)], 0)

    def pick(out):
        return jnp.where(first, out[:cols], out[cols:])

    def only(x, k):
        none = jnp.zeros((span, antennas), BF16)
        return jnp.concatenate([x[rows_at(i)] if i % per == k else none for i in blocks], 0)

    def magnitude(re, im):
        power = re * re + im * im
        return power * lax.rsqrt(jnp.maximum(power, 1e-37))

    def group_steps(g, keepers):
        cut = slice(g * LANES, (g + 1) * LANES)
        z = jnp.concatenate([p[0][:, cut] for p in planes], 1)
        zj = jnp.concatenate([p[2][:, cut] for p in planes], 1)
        zt, zjt = (jnp.concatenate([p[i][cut] for p in planes], 0) for i in (1, 3))
        keepers["gram"][g] = dot(zt, z) + dot(zjt, zj)
        keepers["pt"][g] = zt, zjt
        low_t = jnp.concatenate([zt[:, half_ants:], zjt[:, half_ants:]], 1)
        upper = jnp.concatenate([z[:half_ants], zj[:half_ants]], 0)
        yield
        for k in range(per):
            yield
            top = dot(upper, only(zt, k))
            top = magnitude(top[:half_ants], top[half_ants:])
            low = dot(z[half_ants:], only(low_t, k))
            low = magnitude(low[:, :half_ants], low[:, half_ants:])
            rows = jnp.max(jnp.sum(top, axis=1, keepdims=True), axis=0, keepdims=True)
            columns = jnp.sum(top[:, half_ants:], axis=0, keepdims=True) + jnp.sum(low, axis=0, keepdims=True)
            keepers["largest"][g][k] = jnp.maximum(rows, jnp.max(columns, axis=1, keepdims=True))

    kept = {"gram": {}, "pt": {}, "largest": [{}, {}]}
    for _ in itertools.zip_longest(*[group_steps(g, kept) for g in range(groups)]):
        pass

    gram = pack(kept["gram"])
    gram_b = gram.astype(BF16)
    square = pick(dot(spread_all(gram), gram_b))

    lane_row = iota((1, LANES), 1)
    on_diag = iota((cols, LANES), 1) % wide == iota((cols, LANES), 0) // LANES * span + iota((cols, LANES), 0) % span
    diagonal = jnp.where(on_diag, gram, 0.0)
    loads_of, largest_of = [], []
    for k in range(per):
        both = jnp.sum(diagonal[rows_at(k)] + diagonal[rows_at(per + k)], axis=0, keepdims=True)
        traces = [jnp.sum(jnp.where(lane_row // wide == g, both, 0.0), axis=1, keepdims=True) for g in range(groups)]
        loads_of.append(jnp.where(lane_row < wide, traces[0], traces[1]))
        largest_of.append(jnp.where(lane_row < wide, kept["largest"][0][k], kept["largest"][1][k]))
    load = (0.1 / antennas * 0.5) * jnp.concatenate(loads_of * nj, 0)
    bound = jnp.concatenate(largest_of * nj, 0) + load
    inv = 1.0 / bound
    r = 1.0 - load * inv
    r2 = r * r
    r4 = r2 * r2
    s = [1.0 + 0.0 * r]
    for _ in range(TERMS - 1):
        s.append(1.0 + r * s[-1])
    c = [s[TERMS - 2 - m] for m in range(TERMS - 1)]
    t0 = c[4] + r * (c[5] + r * c[6])
    p0 = c[0] + r * (c[1] + r * (c[2] + r * c[3])) + r4 * t0

    def by(v, count=cols):
        return jnp.concatenate([jnp.broadcast_to(v[i : i + 1], (span, LANES)) for i in range(count // span)], 0)

    x1 = by(inv) * gram
    x2 = by(2.0 * r) * x1 - by(inv * inv) * square
    out = dot(spread_all(x2), jnp.concatenate([x1.astype(BF16), x2.astype(BF16)], 1))
    x3 = by(r) * x2 + by(r2) * x1 - pick(out[:, :LANES])
    x4 = by(2.0 * r2) * x2 - pick(out[:, LANES:])
    tail = by(c[5]) * x1 + by(c[6]) * x2
    head = x1 + x2 + x3
    out = dot(spread_all(x4), jnp.concatenate([tail.astype(BF16), head.astype(BF16)], 1))
    poly = (by(c[1] + r4 * c[5]) * x1 + by(c[2] + r4 * c[6]) * x2 + by(c[3]) * x3 + by(t0) * x4
            - pick(out[:, :LANES]))
    own = (by(1.0 + r4, LANES) * head[:LANES] + by(s[3], LANES) * x4[:LANES]
           - jnp.where(first[:LANES], out[:LANES, LANES:], out[cols : cols + LANES, LANES:]))
    own_low = own - own.astype(BF16).astype(F32)

    for g in range(groups):
        zt, zjt = kept["pt"][g]
        pt = dot(zt, steer_ref[0], NT) + dot(zjt, steer_ref[1], NT)
        pth, ptl = split(pt)
        oh = spread(own, g)
        ends = dot(jnp.concatenate([spread(poly, g), oh, spread(own_low, g)], 0), pth)
        back = (ends[cols : cols + LANES] + ends[cols + LANES :]) + dot(oh, ptl)
        for k in range(per):
            energy = 0.0
            at = slice(k, k + 1), slice(g * wide, g * wide + 1)
            for j in range(nj):
                low = rows_at(j * per + k)
                energy += jnp.sum(pt[low] * (p0[at] * pt[low] - ends[low]), axis=0, keepdims=True)
            whole = s[TERMS - 1][at]
            response = antennas * whole - energy * inv[at]
            factor = lax.rsqrt(response * (bound[at] * (1.0 / (nj * t_loc))))
            beam = (whole * pt[rows_at(k)] - back[rows_at(k)]) * factor
            beam = beam.astype(BF16)
            out_ref[0, g * per + k] = beam[:t_loc]
            out_ref[1, g * per + k] = beam[t_loc:]

    sized(send_ref.at[: antennas - nl], 0).wait_send()
    sized(send_ref, 1).wait_send()


def fused_local(ni, nj, samples, steer_index):
    _, nl, t_loc, _ = samples.shape
    beams, antennas = steer_index.shape
    size = 2 * CH_DEV * t_loc
    vmem = pl.BlockSpec(memory_space=pltpu.VMEM)
    table = jnp.asarray(taper_table(CH_DEV * ni))
    out = pl.pallas_call(
        functools.partial(fused, ni, nj),
        out_shape=pltpu.VMEM((2, CH_DEV, t_loc, beams), BF16),
        in_specs=[pl.BlockSpec(memory_space=pl.ANY)] * 3,
        out_specs=vmem,
        scratch_shapes=[
            pltpu.VMEM((2, nl * t_loc, C), BF16),
            pltpu.VMEM(table.shape, BF16),
            pltpu.VMEM((beams, antennas), jnp.int32),
            pltpu.VMEM((nl * t_loc, CH_DEV * ni), F32),
            pltpu.VMEM((nl * t_loc, CH_DEV * ni), F32),
            pltpu.VMEM((antennas, size), BF16),
            pltpu.VMEM((nj, antennas, size), BF16),
            pltpu.VMEM((2, beams, antennas), BF16),
            pltpu.SemaphoreType.DMA((5,)),
            pltpu.SemaphoreType.DMA,
            pltpu.SemaphoreType.DMA((nj,)),
            pltpu.SemaphoreType.REGULAR((2,)),
        ],
        compiler_params=pltpu.CompilerParams(collective_id=0, has_side_effects=True),
    )(samples.reshape(2, nl * t_loc, C), table, steer_index)
    return jnp.transpose(out, (0, 1, 3, 2))


def choose(ni, nj, samples, steer_index):
    _, nl, t_loc, _ = samples.shape
    beams, antennas = steer_index.shape
    tiled = nl == 16 and t_loc == 16 and CH_DEV * ni == LANES and antennas == nl * ni
    if tiled and nj == 2:
        return fused_local(ni, nj, samples, steer_index)
    return local(samples, steer_index)


def solution(mesh):
    return jax.shard_map(
        functools.partial(choose, mesh.shape["chan"], mesh.shape["tm"]),
        mesh=mesh,
        in_specs=(P(None, "chan", "tm", None), P()),
        out_specs=P(None, "chan", None, "tm"),
        check_vma=False,
    )
```

```python
import functools
import itertools
import math

import jax
import jax.numpy as jnp
import numpy as np
from jax import lax
from jax.experimental import pallas as pl
from jax.experimental.pallas import tpu as pltpu
from jax.sharding import PartitionSpec as P

C = 1024
PHASES = 256
CH_DEV = 8
ITERS = 3
TERMS = 2**ITERS
LANES = 128


HIGHEST = lax.Precision.HIGHEST
F32 = jnp.float32
BF16 = jnp.bfloat16
NT = (((1,), (1,)), ((), ()))


def transform_table(channels_all):
    offset = (C - channels_all) // 2
    channel_number = jnp.arange(channels_all, dtype=jnp.int32) + offset
    sample_number = jnp.arange(C, dtype=jnp.int32)
    phase_turns = channel_number[:, None] * sample_number[None, :] % C
    phase_angle = 2.0 * math.pi / C * phase_turns.astype(jnp.float32)
    window_taper = (
        0.5 - 0.5 * jnp.cos(2.0 * math.pi / C * sample_number.astype(jnp.float32))
    ) / math.sqrt(C)
    cosine = window_taper[None, :] * jnp.cos(phase_angle)
    sine_part = window_taper[None, :] * jnp.sin(phase_angle)
    coefficients = jnp.stack(
        [jnp.stack([cosine, sine_part], 1), jnp.stack([-sine_part, cosine], 1)], 0
    )
    return coefficients.astype(jnp.bfloat16)


def complex_product(left_real, left_imag, right_real, right_imag):
    real_part = jnp.dot(left_real, right_real, precision=HIGHEST) - jnp.dot(
        left_imag, right_imag, precision=HIGHEST
    )
    imag_part = jnp.dot(left_real, right_imag, precision=HIGHEST) + jnp.dot(
        left_imag, right_real, precision=HIGHEST
    )
    return (real_part, imag_part)


def invert_loaded(covariance_real, covariance_imag):
    matrix_order = covariance_real.shape[0]
    loading = 0.1 * jnp.mean(jnp.diagonal(covariance_real))
    identity = jnp.eye(matrix_order, dtype=jnp.float32)
    loaded = covariance_real + loading * identity
    magnitude = jnp.sqrt(loaded * loaded + covariance_imag * covariance_imag)
    largest = jnp.max(jnp.sum(magnitude, axis=1))

    def iterate(counter, state):
        approx_real, approx_imag = state
        image_real, image_imag = complex_product(loaded, covariance_imag, approx_real, approx_imag)
        square_real, square_imag = complex_product(approx_real, approx_imag, image_real, image_imag)
        return (2.0 * approx_real - square_real, 2.0 * approx_imag - square_imag)

    start_state = (identity / largest, jnp.zeros_like(identity))
    return lax.fori_loop(0, ITERS, iterate, start_state)


def form_weights(covariance_real, covariance_imag, steer_real, steer_imag):
    inverse_real, inverse_imag = invert_loaded(covariance_real, covariance_imag)
    gain_real, gain_imag = complex_product(inverse_real, inverse_imag, steer_real, steer_imag)
    response = jnp.sum(steer_real * gain_real + steer_imag * gain_imag, axis=0)
    factor = lax.rsqrt(response)
    return ((gain_real * factor).astype(jnp.bfloat16), (gain_imag * factor).astype(jnp.bfloat16))


def weights_stacked(covariance_real, covariance_imag, steer_real, steer_imag):
    weight_real, weight_imag = jax.vmap(form_weights, in_axes=(0, 0, None, None))(
        covariance_real, covariance_imag, steer_real, steer_imag
    )
    return jnp.stack([weight_real, weight_imag], 1)


def steering(steer_index):
    phase_angle = 2.0 * math.pi / PHASES * steer_index.astype(jnp.float32)
    return (jnp.cos(phase_angle).T, jnp.sin(phase_angle).T)


def apply_beams(weight_pair, spectrum):
    real_weight = weight_pair[:, 0]
    imag_weight = weight_pair[:, 1]
    beam_real = jnp.einsum(
        "knb,kns->kbs", real_weight, spectrum[0], preferred_element_type=jnp.float32
    ) + jnp.einsum("knb,kns->kbs", imag_weight, spectrum[1], preferred_element_type=jnp.float32)
    beam_imag = jnp.einsum(
        "knb,kns->kbs", real_weight, spectrum[1], preferred_element_type=jnp.float32
    ) - jnp.einsum("knb,kns->kbs", imag_weight, spectrum[0], preferred_element_type=jnp.float32)
    return jnp.stack([beam_real, beam_imag], 0).astype(jnp.bfloat16)


def local(samples, steer_index):
    channels_all = CH_DEV * lax.axis_size("chan")
    coefficients = transform_table(channels_all)
    spectra = lax.dot_general(
        coefficients, samples, (((2, 3), (0, 3)), ((), ())), preferred_element_type=jnp.float32
    ).astype(jnp.bfloat16)
    steer_real, steer_imag = steering(steer_index)
    turned = lax.all_to_all(
        lax.all_to_all(spectra, "chan", split_axis=1, concat_axis=2, tiled=True),
        "tm",
        split_axis=1,
        concat_axis=3,
        tiled=True,
    )
    outer_sums = jnp.einsum("ikns,jkms->kinjm", turned, turned, preferred_element_type=jnp.float32)
    snapshots = turned.shape[3]
    covariance_real = (outer_sums[:, 0, :, 0, :] + outer_sums[:, 1, :, 1, :]) / snapshots
    covariance_imag = (outer_sums[:, 1, :, 0, :] - outer_sums[:, 0, :, 1, :]) / snapshots
    weight_pair = weights_stacked(covariance_real, covariance_imag, steer_real, steer_imag)
    local_beams = apply_beams(weight_pair, turned)
    return lax.all_to_all(local_beams, "tm", split_axis=3, concat_axis=1, tiled=True)


def taper_table(channels_all):
    offset = (C - channels_all) // 2
    channel = np.arange(channels_all) + offset
    sample = np.arange(C)
    angle = 2.0 * math.pi / C * (channel[None, :] * sample[:, None] % C)
    taper = (0.5 - 0.5 * np.cos(2.0 * math.pi / C * sample)) / math.sqrt(C)
    both = np.concatenate([taper[:, None] * np.cos(angle), taper[:, None] * np.sin(angle)], 1)
    return both.astype(np.float32).astype(BF16)


def iota(shape, axis):
    return lax.broadcasted_iota(jnp.int32, shape, axis)


def dot(a, b, dims=(((1,), (0,)), ((), ()))):
    return lax.dot_general(a, b, dims, preferred_element_type=F32)


def split(x):
    high = x.astype(BF16)
    return high, (x - high.astype(F32)).astype(BF16)


def exchange_blocks(rows, count, width):
    place = iota(rows[0].shape, 1) // width
    turned = [rows[0]] + [pltpu.roll(rows[t], t * width, 1) for t in range(1, count)]
    rows = [turned[-i % count] for i in range(count)]
    step = 1
    while step < count:
        take = place & step != 0
        rows = [jnp.where(take, rows[i - step], rows[i]) for i in range(count)]
        step *= 2
    return rows


def steering_parts(index):
    turn = index & (PHASES - 1)
    quarter = PHASES // 4
    quadrant = (turn + quarter // 2) // quarter
    x = (turn - quarter * quadrant).astype(F32) * (2.0 * math.pi / PHASES)
    y = x * x
    s = x * (1.0 + y * (-1.0 / 6 + y * (1.0 / 120 + y * (-1.0 / 5040 + y * (1.0 / 362880)))))
    c = 1.0 + y * (-0.5 + y * (1.0 / 24 + y * (-1.0 / 720 + y * (1.0 / 40320 - y * (1.0 / 3628800)))))
    odd = quadrant & 1 == 1
    flip_c = (quadrant + 1) & 2 == 2
    flip_s = quadrant & 2 == 2
    cosine = jnp.where(odd, s, c)
    sine = jnp.where(odd, c, s)
    return jnp.where(flip_c, -cosine, cosine), jnp.where(flip_s, -sine, sine)


def fused(ni, nj, samples_hbm, table_hbm, index_hbm, out_ref, samples_ref, table_ref, index_ref, re_ref,
          im_ref, send_ref, recv_ref, steer_ref, load_sem, send_sem, recv_sem, told):
    nl, t_loc, q = 16, 16, 2 * CH_DEV
    antennas = ni * nl
    size = q * t_loc
    my_i, my_j = lax.axis_index("chan"), lax.axis_index("tm")
    other_j = 1 - my_j

    loads = [pltpu.make_async_copy(src, dst, load_sem.at[i]) for i, (src, dst) in enumerate(
        [(table_hbm, table_ref), (samples_hbm.at[0], samples_ref.at[0]),
         (samples_hbm.at[1], samples_ref.at[1]), (index_hbm, index_ref)])]
    for load in loads:
        load.start()

    barrier = pltpu.get_barrier_semaphore()

    def after(step):
        ahead = my_i + step
        return jnp.where(ahead >= ni, ahead - ni, ahead)

    def around(body):
        lax.fori_loop(1, ni, lambda step, carry: (body(step), carry)[1], 0)

    def greet(peer_i, peer_j):
        pl.semaphore_signal(barrier, inc=1, device_id=(peer_i, peer_j),
                            device_id_type=pl.DeviceIdType.MESH)

    greet(my_i, other_j)

    level = ni // 4
    my_level = my_i // level

    def greet_both(step):
        peer = after(step)
        near = (peer >= 2 * level) | (my_level <= peer // level + 1)

        @pl.when(near)
        def _():
            greet(peer, my_j)
            greet(peer, other_j)

    around(greet_both)

    loads[0].wait()
    loads[1].wait()
    loads[2].wait()
    table = table_ref[...]
    half = table.shape[1] // 2
    first = dot(samples_ref[0], table)
    second = dot(samples_ref[1], table)
    re_ref[...] = first[:, :half] + second[:, half:]
    im_ref[...] = second[:, :half] - first[:, half:]
    parts = []
    for ref in (re_ref, im_ref):
        rows = [ref[pl.ds(t, nl, stride=t_loc), :].astype(BF16) for t in range(t_loc)]
        parts.append(exchange_blocks(rows, ni, CH_DEV))
    send_ref[...] = jnp.concatenate([jnp.concatenate([a, b], 1) for a, b in zip(*parts)], 0)

    pl.semaphore_wait(barrier, jnp.minimum(my_level + 2, 4) * (level * nj) - 1)

    def tell(distance, which):
        pl.semaphore_signal(told.at[which], inc=1, device_id=(my_i - distance * level, my_j),
                            device_id_type=pl.DeviceIdType.MESH)

    @pl.when(my_level == 1)
    def _():
        tell(1, 0)

    @pl.when(my_level == 2)
    def _():
        tell(2, 1)
        tell(1, 1)

    rows_of = lambda i: pl.ds(pl.multiple_of(i * nl, nl), nl)
    mine = rows_of(my_i)

    def peer_of(step):
        if isinstance(step, int) and step == 0:
            return my_i
        begin = jnp.where(my_level == 2, 2, jnp.where(my_level == 1, 11, jnp.where(my_level == 0, 0, 3)))
        usual = lax.rem(step - 3 + begin, 13) + 1
        usual = jnp.where(usual >= ni - my_i, usual + 2, usual)
        moved = jnp.where(step <= 2, step - 1, lax.rem(my_i + usual, ni))
        return jnp.where((my_i >= 2) & (my_i < 16), moved, after(step))

    def block_copy(step, origin, plane):
        peer = peer_of(step)
        return pltpu.make_async_remote_copy(
            src_ref=send_ref.at[rows_of(peer), :],
            dst_ref=recv_ref.at[plane, rows_of(origin), :],
            send_sem=send_sem,
            recv_sem=recv_sem.at[plane],
            device_id=(peer, other_j if plane else my_j),
            device_id_type=pl.DeviceIdType.MESH,
        )

    def send(step):
        peer = peer_of(step)

        @pl.when((my_level == 0) & (peer == 2 * level))
        def _():
            pl.semaphore_wait(told.at[0], 1)

        @pl.when((my_level <= 1) & (peer == 3 * level))
        def _():
            pl.semaphore_wait(told.at[1], 1)

        block_copy(step, my_i, 1).start()
        block_copy(step, my_i, 0).start()

    block_copy(0, my_i, 1).start()
    around(send)
    recv_ref[0, mine, :] = send_ref[mine, :]

    loads[3].wait()
    cosine, sine = steering_parts(index_ref[...])
    steer_ref[0] = cosine.astype(BF16)
    steer_ref[1] = sine.astype(BF16)

    span = 2 * t_loc
    row_id, col_id = iota((size, size), 0), iota((size, size), 1)

    def source(column):
        shift = (column % t_loc + my_i) % t_loc
        return column // t_loc % 2 * (t_loc * CH_DEV) + shift * CH_DEV + column // span

    order = jnp.where(row_id == source(col_id), 1.0, 0.0).astype(BF16)
    order_t = jnp.where(col_id == source(row_id), 1.0, 0.0).astype(BF16)
    order_j = jnp.where(row_id == source(col_id ^ t_loc), jnp.where(col_id & t_loc == 0, 1.0, -1.0), 0.0).astype(BF16)

    def prepare(plane):
        held = recv_ref[plane]
        zt = dot(order_t, held, NT).astype(BF16)
        z = dot(held, order).astype(BF16)
        zj = dot(held, order_j).astype(BF16)
        zjt = jnp.concatenate(
            [b for i in range(size // span) for b in
             (zt[i * span + t_loc : (i + 1) * span], -zt[i * span : i * span + t_loc])], 0)
        return z, zt, zj, zjt

    def sized(ref, plane):
        return pltpu.make_async_remote_copy(
            src_ref=ref, dst_ref=ref, send_sem=send_sem, recv_sem=recv_sem.at[plane],
            device_id=(my_i, other_j), device_id_type=pl.DeviceIdType.MESH)

    sized(recv_ref.at[0, : antennas - nl], 0).wait_recv()
    sized(recv_ref.at[1], 1).wait_recv()
    planes = [prepare(j) for j in range(nj)]

    groups = size // LANES
    per = CH_DEV // groups
    cols = nj * LANES
    wide = nj * span
    chan_of = lambda x: x // span % per
    lane_chan = chan_of(iota((1, cols), 1))
    half_ants = antennas // 2
    blocks = range(cols // span)
    rows_at = lambda i: slice(i * span, (i + 1) * span)
    lane = iota((span, LANES), 1)
    slot = lane // span
    packed_slot = iota((span, LANES), 1) // span
    first = iota((cols, LANES), 1) < wide

    def shifted(x, amount):
        return x if amount % LANES == 0 else pltpu.roll(x, amount % LANES, 1)

    def pack(grams):
        done = []
        for i in blocks:
            kept = None
            for g in range(groups):
                for j in range(nj):
                    to = g * nj + j
                    moved = shifted(grams[g][rows_at(i), j * LANES : (j + 1) * LANES], (to - i % per) * span)
                    kept = moved if kept is None else jnp.where(slot == to, moved, kept)
            done.append(kept)
        return jnp.concatenate(done, 0)

    def spread(x, g):
        x = x.astype(BF16)
        done = []
        for i in range(x.shape[0] // span):
            k = i % per
            done.append(jnp.concatenate(
                [jnp.where(packed_slot == k, shifted(x[rows_at(i)], (k - g * nj - j) * span), jnp.zeros((), BF16))
                 for j in range(nj)], 1))
        return jnp.concatenate(done, 0)

    def spread_all(x):
        return jnp.concatenate([spread(x, g) for g in range(groups)], 0)

    def pick(out):
        return jnp.where(first, out[:cols], out[cols:])

    def only(x, k):
        none = jnp.zeros((span, antennas), BF16)
        return jnp.concatenate([x[rows_at(i)] if i % per == k else none for i in blocks], 0)

    def magnitude(re, im):
        power = re * re + im * im
        return power * lax.rsqrt(jnp.maximum(power, 1e-37))

    def group_steps(g, keepers):
        cut = slice(g * LANES, (g + 1) * LANES)
        z = jnp.concatenate([p[0][:, cut] for p in planes], 1)
        zj = jnp.concatenate([p[2][:, cut] for p in planes], 1)
        zt, zjt = (jnp.concatenate([p[i][cut] for p in planes], 0) for i in (1, 3))
        keepers["gram"][g] = dot(zt, z) + dot(zjt, zj)
        keepers["pt"][g] = zt, zjt
        low_t = jnp.concatenate([zt[:, half_ants:], zjt[:, half_ants:]], 1)
        upper = jnp.concatenate([z[:half_ants], zj[:half_ants]], 0)
        yield
        for k in range(per):
            yield
            top = dot(upper, only(zt, k))
            top = magnitude(top[:half_ants], top[half_ants:])
            low = dot(z[half_ants:], only(low_t, k))
            low = magnitude(low[:, :half_ants], low[:, half_ants:])
            rows = jnp.max(jnp.sum(top, axis=1, keepdims=True), axis=0, keepdims=True)
            columns = jnp.sum(top[:, half_ants:], axis=0, keepdims=True) + jnp.sum(low, axis=0, keepdims=True)
            keepers["largest"][g][k] = jnp.maximum(rows, jnp.max(columns, axis=1, keepdims=True))

    kept = {"gram": {}, "pt": {}, "largest": [{}, {}]}
    for _ in itertools.zip_longest(*[group_steps(g, kept) for g in range(groups)]):
        pass

    gram = pack(kept["gram"])
    gram_b = gram.astype(BF16)
    square = pick(dot(spread_all(gram), gram_b))

    lane_row = iota((1, LANES), 1)
    on_diag = iota((cols, LANES), 1) % wide == iota((cols, LANES), 0) // LANES * span + iota((cols, LANES), 0) % span
    diagonal = jnp.where(on_diag, gram, 0.0)
    loads_of, largest_of = [], []
    for k in range(per):
        both = jnp.sum(diagonal[rows_at(k)] + diagonal[rows_at(per + k)], axis=0, keepdims=True)
        traces = [jnp.sum(jnp.where(lane_row // wide == g, both, 0.0), axis=1, keepdims=True) for g in range(groups)]
        loads_of.append(jnp.where(lane_row < wide, traces[0], traces[1]))
        largest_of.append(jnp.where(lane_row < wide, kept["largest"][0][k], kept["largest"][1][k]))
    load = (0.1 / antennas * 0.5) * jnp.concatenate(loads_of * nj, 0)
    bound = jnp.concatenate(largest_of * nj, 0) + load
    inv = 1.0 / bound
    r = 1.0 - load * inv
    r2 = r * r
    r4 = r2 * r2
    s = [1.0 + 0.0 * r]
    for _ in range(TERMS - 1):
        s.append(1.0 + r * s[-1])
    c = [s[TERMS - 2 - m] for m in range(TERMS - 1)]
    t0 = c[4] + r * (c[5] + r * c[6])
    p0 = c[0] + r * (c[1] + r * (c[2] + r * c[3])) + r4 * t0

    def by(v, count=cols):
        return jnp.concatenate([jnp.broadcast_to(v[i : i + 1], (span, LANES)) for i in range(count // span)], 0)

    x1 = by(inv) * gram
    x2 = by(2.0 * r) * x1 - by(inv * inv) * square
    out = dot(spread_all(x2), jnp.concatenate([x1.astype(BF16), x2.astype(BF16)], 1))
    x3 = by(r) * x2 + by(r2) * x1 - pick(out[:, :LANES])
    x4 = by(2.0 * r2) * x2 - pick(out[:, LANES:])
    tail = by(c[5]) * x1 + by(c[6]) * x2
    head = x1 + x2 + x3
    out = dot(spread_all(x4), jnp.concatenate([tail.astype(BF16), head.astype(BF16)], 1))
    poly = (by(c[1] + r4 * c[5]) * x1 + by(c[2] + r4 * c[6]) * x2 + by(c[3]) * x3 + by(t0) * x4
            - pick(out[:, :LANES]))
    own = (by(1.0 + r4, LANES) * head[:LANES] + by(s[3], LANES) * x4[:LANES]
           - jnp.where(first[:LANES], out[:LANES, LANES:], out[cols : cols + LANES, LANES:]))
    own_low = own - own.astype(BF16).astype(F32)

    for g in range(groups):
        zt, zjt = kept["pt"][g]
        pt = dot(zt, steer_ref[0], NT) + dot(zjt, steer_ref[1], NT)
        pth, ptl = split(pt)
        oh = spread(own, g)
        ends = dot(jnp.concatenate([spread(poly, g), oh, spread(own_low, g)], 0), pth)
        back = (ends[cols : cols + LANES] + ends[cols + LANES :]) + dot(oh, ptl)
        for k in range(per):
            energy = 0.0
            at = slice(k, k + 1), slice(g * wide, g * wide + 1)
            for j in range(nj):
                low = rows_at(j * per + k)
                energy += jnp.sum(pt[low] * (p0[at] * pt[low] - ends[low]), axis=0, keepdims=True)
            whole = s[TERMS - 1][at]
            response = antennas * whole - energy * inv[at]
            factor = lax.rsqrt(response * (bound[at] * (1.0 / (nj * t_loc))))
            beam = (whole * pt[rows_at(k)] - back[rows_at(k)]) * factor
            beam = beam.astype(BF16)
            out_ref[0, g * per + k] = beam[:t_loc]
            out_ref[1, g * per + k] = beam[t_loc:]

    sized(send_ref.at[: antennas - nl], 0).wait_send()
    sized(send_ref, 1).wait_send()


def fused_local(ni, nj, samples, steer_index):
    _, nl, t_loc, _ = samples.shape
    beams, antennas = steer_index.shape
    size = 2 * CH_DEV * t_loc
    vmem = pl.BlockSpec(memory_space=pltpu.VMEM)
    table = jnp.asarray(taper_table(CH_DEV * ni))
    out = pl.pallas_call(
        functools.partial(fused, ni, nj),
        out_shape=pltpu.VMEM((2, CH_DEV, t_loc, beams), BF16),
        in_specs=[pl.BlockSpec(memory_space=pl.ANY)] * 3,
        out_specs=vmem,
        scratch_shapes=[
            pltpu.VMEM((2, nl * t_loc, C), BF16),
            pltpu.VMEM(table.shape, BF16),
            pltpu.VMEM((beams, antennas), jnp.int32),
            pltpu.VMEM((nl * t_loc, CH_DEV * ni), F32),
            pltpu.VMEM((nl * t_loc, CH_DEV * ni), F32),
            pltpu.VMEM((antennas, size), BF16),
            pltpu.VMEM((nj, antennas, size), BF16),
            pltpu.VMEM((2, beams, antennas), BF16),
            pltpu.SemaphoreType.DMA((4,)),
            pltpu.SemaphoreType.DMA,
            pltpu.SemaphoreType.DMA((nj,)),
            pltpu.SemaphoreType.REGULAR((2,)),
        ],
        compiler_params=pltpu.CompilerParams(collective_id=0, has_side_effects=True),
    )(samples.reshape(2, nl * t_loc, C), table, steer_index)
    return jnp.transpose(out, (0, 1, 3, 2))


def choose(ni, nj, samples, steer_index):
    _, nl, t_loc, _ = samples.shape
    beams, antennas = steer_index.shape
    tiled = nl == 16 and t_loc == 16 and CH_DEV * ni == LANES and antennas == nl * ni
    if tiled and nj == 2:
        return fused_local(ni, nj, samples, steer_index)
    return local(samples, steer_index)


def solution(mesh):
    return jax.shard_map(
        functools.partial(choose, mesh.shape["chan"], mesh.shape["tm"]),
        mesh=mesh,
        in_specs=(P(None, "chan", "tm", None), P()),
        out_specs=P(None, "chan", None, "tm"),
        check_vma=False,
    )
```

```python
import functools
import itertools
import math

import jax
import jax.numpy as jnp
import numpy as np
from jax import lax
from jax.experimental import pallas as pl
from jax.experimental.pallas import tpu as pltpu
from jax.sharding import PartitionSpec as P

C = 1024
PHASES = 256
CH_DEV = 8
ITERS = 3
TERMS = 2**ITERS
LANES = 128


HIGHEST = lax.Precision.HIGHEST
F32 = jnp.float32
BF16 = jnp.bfloat16
NT = (((1,), (1,)), ((), ()))


def transform_table(channels_all):
    offset = (C - channels_all) // 2
    channel_number = jnp.arange(channels_all, dtype=jnp.int32) + offset
    sample_number = jnp.arange(C, dtype=jnp.int32)
    phase_turns = channel_number[:, None] * sample_number[None, :] % C
    phase_angle = 2.0 * math.pi / C * phase_turns.astype(jnp.float32)
    window_taper = (
        0.5 - 0.5 * jnp.cos(2.0 * math.pi / C * sample_number.astype(jnp.float32))
    ) / math.sqrt(C)
    cosine = window_taper[None, :] * jnp.cos(phase_angle)
    sine_part = window_taper[None, :] * jnp.sin(phase_angle)
    coefficients = jnp.stack(
        [jnp.stack([cosine, sine_part], 1), jnp.stack([-sine_part, cosine], 1)], 0
    )
    return coefficients.astype(jnp.bfloat16)


def complex_product(left_real, left_imag, right_real, right_imag):
    real_part = jnp.dot(left_real, right_real, precision=HIGHEST) - jnp.dot(
        left_imag, right_imag, precision=HIGHEST
    )
    imag_part = jnp.dot(left_real, right_imag, precision=HIGHEST) + jnp.dot(
        left_imag, right_real, precision=HIGHEST
    )
    return (real_part, imag_part)


def invert_loaded(covariance_real, covariance_imag):
    matrix_order = covariance_real.shape[0]
    loading = 0.1 * jnp.mean(jnp.diagonal(covariance_real))
    identity = jnp.eye(matrix_order, dtype=jnp.float32)
    loaded = covariance_real + loading * identity
    magnitude = jnp.sqrt(loaded * loaded + covariance_imag * covariance_imag)
    largest = jnp.max(jnp.sum(magnitude, axis=1))

    def iterate(counter, state):
        approx_real, approx_imag = state
        image_real, image_imag = complex_product(loaded, covariance_imag, approx_real, approx_imag)
        square_real, square_imag = complex_product(approx_real, approx_imag, image_real, image_imag)
        return (2.0 * approx_real - square_real, 2.0 * approx_imag - square_imag)

    start_state = (identity / largest, jnp.zeros_like(identity))
    return lax.fori_loop(0, ITERS, iterate, start_state)


def form_weights(covariance_real, covariance_imag, steer_real, steer_imag):
    inverse_real, inverse_imag = invert_loaded(covariance_real, covariance_imag)
    gain_real, gain_imag = complex_product(inverse_real, inverse_imag, steer_real, steer_imag)
    response = jnp.sum(steer_real * gain_real + steer_imag * gain_imag, axis=0)
    factor = lax.rsqrt(response)
    return ((gain_real * factor).astype(jnp.bfloat16), (gain_imag * factor).astype(jnp.bfloat16))


def weights_stacked(covariance_real, covariance_imag, steer_real, steer_imag):
    weight_real, weight_imag = jax.vmap(form_weights, in_axes=(0, 0, None, None))(
        covariance_real, covariance_imag, steer_real, steer_imag
    )
    return jnp.stack([weight_real, weight_imag], 1)


def steering(steer_index):
    phase_angle = 2.0 * math.pi / PHASES * steer_index.astype(jnp.float32)
    return (jnp.cos(phase_angle).T, jnp.sin(phase_angle).T)


def apply_beams(weight_pair, spectrum):
    real_weight = weight_pair[:, 0]
    imag_weight = weight_pair[:, 1]
    beam_real = jnp.einsum(
        "knb,kns->kbs", real_weight, spectrum[0], preferred_element_type=jnp.float32
    ) + jnp.einsum("knb,kns->kbs", imag_weight, spectrum[1], preferred_element_type=jnp.float32)
    beam_imag = jnp.einsum(
        "knb,kns->kbs", real_weight, spectrum[1], preferred_element_type=jnp.float32
    ) - jnp.einsum("knb,kns->kbs", imag_weight, spectrum[0], preferred_element_type=jnp.float32)
    return jnp.stack([beam_real, beam_imag], 0).astype(jnp.bfloat16)


def local(samples, steer_index):
    channels_all = CH_DEV * lax.axis_size("chan")
    coefficients = transform_table(channels_all)
    spectra = lax.dot_general(
        coefficients, samples, (((2, 3), (0, 3)), ((), ())), preferred_element_type=jnp.float32
    ).astype(jnp.bfloat16)
    steer_real, steer_imag = steering(steer_index)
    turned = lax.all_to_all(
        lax.all_to_all(spectra, "chan", split_axis=1, concat_axis=2, tiled=True),
        "tm",
        split_axis=1,
        concat_axis=3,
        tiled=True,
    )
    outer_sums = jnp.einsum("ikns,jkms->kinjm", turned, turned, preferred_element_type=jnp.float32)
    snapshots = turned.shape[3]
    covariance_real = (outer_sums[:, 0, :, 0, :] + outer_sums[:, 1, :, 1, :]) / snapshots
    covariance_imag = (outer_sums[:, 1, :, 0, :] - outer_sums[:, 0, :, 1, :]) / snapshots
    weight_pair = weights_stacked(covariance_real, covariance_imag, steer_real, steer_imag)
    local_beams = apply_beams(weight_pair, turned)
    return lax.all_to_all(local_beams, "tm", split_axis=3, concat_axis=1, tiled=True)


def taper_table(channels_all):
    offset = (C - channels_all) // 2
    channel = np.arange(channels_all) + offset
    sample = np.arange(C)
    angle = 2.0 * math.pi / C * (channel[None, :] * sample[:, None] % C)
    taper = (0.5 - 0.5 * np.cos(2.0 * math.pi / C * sample)) / math.sqrt(C)
    both = np.concatenate([taper[:, None] * np.cos(angle), taper[:, None] * np.sin(angle)], 1)
    return both.astype(np.float32).astype(BF16)


def iota(shape, axis):
    return lax.broadcasted_iota(jnp.int32, shape, axis)


def dot(a, b, dims=(((1,), (0,)), ((), ()))):
    return lax.dot_general(a, b, dims, preferred_element_type=F32)


def split(x):
    high = x.astype(BF16)
    return high, (x - high.astype(F32)).astype(BF16)


def exchange_blocks(rows, count, width):
    place = iota(rows[0].shape, 1) // width
    turned = [rows[0]] + [pltpu.roll(rows[t], t * width, 1) for t in range(1, count)]
    rows = [turned[-i % count] for i in range(count)]
    step = 1
    while step < count:
        take = place & step != 0
        rows = [jnp.where(take, rows[i - step], rows[i]) for i in range(count)]
        step *= 2
    return rows


def steering_parts(index):
    turn = index & (PHASES - 1)
    quarter = PHASES // 4
    quadrant = (turn + quarter // 2) // quarter
    x = (turn - quarter * quadrant).astype(F32) * (2.0 * math.pi / PHASES)
    y = x * x
    s = x * (1.0 + y * (-1.0 / 6 + y * (1.0 / 120 + y * (-1.0 / 5040 + y * (1.0 / 362880)))))
    c = 1.0 + y * (-0.5 + y * (1.0 / 24 + y * (-1.0 / 720 + y * (1.0 / 40320 - y * (1.0 / 3628800)))))
    odd = quadrant & 1 == 1
    flip_c = (quadrant + 1) & 2 == 2
    flip_s = quadrant & 2 == 2
    cosine = jnp.where(odd, s, c)
    sine = jnp.where(odd, c, s)
    return jnp.where(flip_c, -cosine, cosine), jnp.where(flip_s, -sine, sine)


def fused(ni, nj, samples_hbm, table_hbm, index_hbm, out_ref, samples_ref, table_ref, index_ref, re_ref,
          im_ref, send_ref, recv_ref, steer_ref, load_sem, send_sem, recv_sem, told):
    nl, t_loc, q = 16, 16, 2 * CH_DEV
    antennas = ni * nl
    size = q * t_loc
    my_i, my_j = lax.axis_index("chan"), lax.axis_index("tm")
    other_j = 1 - my_j

    loads = [pltpu.make_async_copy(src, dst, load_sem.at[i]) for i, (src, dst) in enumerate(
        [(table_hbm, table_ref), (samples_hbm.at[0], samples_ref.at[0]),
         (samples_hbm.at[1], samples_ref.at[1]), (index_hbm, index_ref)])]
    for load in loads[:3]:
        load.start()

    barrier = pltpu.get_barrier_semaphore()

    def after(step):
        ahead = my_i + step
        return jnp.where(ahead >= ni, ahead - ni, ahead)

    def around(body):
        lax.fori_loop(1, ni, lambda step, carry: (body(step), carry)[1], 0)

    def greet(peer_i, peer_j):
        pl.semaphore_signal(barrier, inc=1, device_id=(peer_i, peer_j),
                            device_id_type=pl.DeviceIdType.MESH)

    greet(my_i, other_j)

    level = ni // 4
    my_level = my_i // level

    def greet_both(step):
        peer = after(step)
        near = (peer >= 2 * level) | (my_level <= peer // level + 1)

        @pl.when(near)
        def _():
            greet(peer, my_j)
            greet(peer, other_j)

    around(greet_both)

    loads[0].wait()
    loads[1].wait()
    loads[2].wait()
    loads[3].start()
    table = table_ref[...]
    half = table.shape[1] // 2
    first = dot(samples_ref[0], table)
    second = dot(samples_ref[1], table)
    re_ref[...] = first[:, :half] + second[:, half:]
    im_ref[...] = second[:, :half] - first[:, half:]
    parts = []
    for ref in (re_ref, im_ref):
        rows = [ref[pl.ds(t, nl, stride=t_loc), :].astype(BF16) for t in range(t_loc)]
        parts.append(exchange_blocks(rows, ni, CH_DEV))
    send_ref[...] = jnp.concatenate([jnp.concatenate([a, b], 1) for a, b in zip(*parts)], 0)

    pl.semaphore_wait(barrier, jnp.minimum(my_level + 2, 4) * (level * nj) - 1)

    def tell(distance, which):
        pl.semaphore_signal(told.at[which], inc=1, device_id=(my_i - distance * level, my_j),
                            device_id_type=pl.DeviceIdType.MESH)

    @pl.when(my_level == 1)
    def _():
        tell(1, 0)

    @pl.when(my_level == 2)
    def _():
        tell(2, 1)
        tell(1, 1)

    rows_of = lambda i: pl.ds(pl.multiple_of(i * nl, nl), nl)
    mine = rows_of(my_i)

    def peer_of(step):
        if isinstance(step, int) and step == 0:
            return my_i
        begin = jnp.where(my_level == 2, 2, jnp.where(my_level == 1, 11, jnp.where(my_level == 0, 0, 3)))
        usual = lax.rem(step - 3 + begin, 13) + 1
        usual = jnp.where(usual >= ni - my_i, usual + 2, usual)
        moved = jnp.where(step <= 2, step - 1, lax.rem(my_i + usual, ni))
        return jnp.where((my_i >= 2) & (my_i < 16), moved, after(step))

    def block_copy(step, origin, plane):
        peer = peer_of(step)
        return pltpu.make_async_remote_copy(
            src_ref=send_ref.at[rows_of(peer), :],
            dst_ref=recv_ref.at[plane, rows_of(origin), :],
            send_sem=send_sem,
            recv_sem=recv_sem.at[plane],
            device_id=(peer, other_j if plane else my_j),
            device_id_type=pl.DeviceIdType.MESH,
        )

    def send(step):
        peer = peer_of(step)

        @pl.when((my_level == 0) & (peer == 2 * level))
        def _():
            pl.semaphore_wait(told.at[0], 1)

        @pl.when((my_level <= 1) & (peer == 3 * level))
        def _():
            pl.semaphore_wait(told.at[1], 1)

        block_copy(step, my_i, 1).start()
        block_copy(step, my_i, 0).start()

    block_copy(0, my_i, 1).start()
    around(send)
    recv_ref[0, mine, :] = send_ref[mine, :]

    loads[3].wait()
    cosine, sine = steering_parts(index_ref[...])
    steer_ref[0] = cosine.astype(BF16)
    steer_ref[1] = sine.astype(BF16)

    span = 2 * t_loc
    row_id, col_id = iota((size, size), 0), iota((size, size), 1)

    def source(column):
        shift = (column % t_loc + my_i) % t_loc
        return column // t_loc % 2 * (t_loc * CH_DEV) + shift * CH_DEV + column // span

    order = jnp.where(row_id == source(col_id), 1.0, 0.0).astype(BF16)
    order_t = jnp.where(col_id == source(row_id), 1.0, 0.0).astype(BF16)
    order_j = jnp.where(row_id == source(col_id ^ t_loc), jnp.where(col_id & t_loc == 0, 1.0, -1.0), 0.0).astype(BF16)

    def prepare(plane):
        held = recv_ref[plane]
        zt = dot(order_t, held, NT).astype(BF16)
        z = dot(held, order).astype(BF16)
        zj = dot(held, order_j).astype(BF16)
        zjt = jnp.concatenate(
            [b for i in range(size // span) for b in
             (zt[i * span + t_loc : (i + 1) * span], -zt[i * span : i * span + t_loc])], 0)
        return z, zt, zj, zjt

    def sized(ref, plane):
        return pltpu.make_async_remote_copy(
            src_ref=ref, dst_ref=ref, send_sem=send_sem, recv_sem=recv_sem.at[plane],
            device_id=(my_i, other_j), device_id_type=pl.DeviceIdType.MESH)

    sized(recv_ref.at[0, : antennas - nl], 0).wait_recv()
    sized(recv_ref.at[1], 1).wait_recv()
    planes = [prepare(j) for j in range(nj)]

    groups = size // LANES
    per = CH_DEV // groups
    cols = nj * LANES
    wide = nj * span
    chan_of = lambda x: x // span % per
    lane_chan = chan_of(iota((1, cols), 1))
    half_ants = antennas // 2
    blocks = range(cols // span)
    rows_at = lambda i: slice(i * span, (i + 1) * span)
    lane = iota((span, LANES), 1)
    slot = lane // span
    packed_slot = iota((span, LANES), 1) // span
    first = iota((cols, LANES), 1) < wide

    def shifted(x, amount):
        return x if amount % LANES == 0 else pltpu.roll(x, amount % LANES, 1)

    def pack(grams):
        done = []
        for i in blocks:
            kept = None
            for g in range(groups):
                for j in range(nj):
                    to = g * nj + j
                    moved = shifted(grams[g][rows_at(i), j * LANES : (j + 1) * LANES], (to - i % per) * span)
                    kept = moved if kept is None else jnp.where(slot == to, moved, kept)
            done.append(kept)
        return jnp.concatenate(done, 0)

    def spread(x, g):
        x = x.astype(BF16)
        done = []
        for i in range(x.shape[0] // span):
            k = i % per
            done.append(jnp.concatenate(
                [jnp.where(packed_slot == k, shifted(x[rows_at(i)], (k - g * nj - j) * span), jnp.zeros((), BF16))
                 for j in range(nj)], 1))
        return jnp.concatenate(done, 0)

    def spread_all(x):
        return jnp.concatenate([spread(x, g) for g in range(groups)], 0)

    def pick(out):
        return jnp.where(first, out[:cols], out[cols:])

    def only(x, k):
        none = jnp.zeros((span, antennas), BF16)
        return jnp.concatenate([x[rows_at(i)] if i % per == k else none for i in blocks], 0)

    def magnitude(re, im):
        power = re * re + im * im
        return power * lax.rsqrt(jnp.maximum(power, 1e-37))

    def group_steps(g, keepers):
        cut = slice(g * LANES, (g + 1) * LANES)
        z = jnp.concatenate([p[0][:, cut] for p in planes], 1)
        zj = jnp.concatenate([p[2][:, cut] for p in planes], 1)
        zt, zjt = (jnp.concatenate([p[i][cut] for p in planes], 0) for i in (1, 3))
        keepers["gram"][g] = dot(zt, z) + dot(zjt, zj)
        keepers["pt"][g] = zt, zjt
        low_t = jnp.concatenate([zt[:, half_ants:], zjt[:, half_ants:]], 1)
        upper = jnp.concatenate([z[:half_ants], zj[:half_ants]], 0)
        yield
        for k in range(per):
            yield
            top = dot(upper, only(zt, k))
            top = magnitude(top[:half_ants], top[half_ants:])
            low = dot(z[half_ants:], only(low_t, k))
            low = magnitude(low[:, :half_ants], low[:, half_ants:])
            rows = jnp.max(jnp.sum(top, axis=1, keepdims=True), axis=0, keepdims=True)
            columns = jnp.sum(top[:, half_ants:], axis=0, keepdims=True) + jnp.sum(low, axis=0, keepdims=True)
            keepers["largest"][g][k] = jnp.maximum(rows, jnp.max(columns, axis=1, keepdims=True))

    kept = {"gram": {}, "pt": {}, "largest": [{}, {}]}
    for _ in itertools.zip_longest(*[group_steps(g, kept) for g in range(groups)]):
        pass

    gram = pack(kept["gram"])
    gram_b = gram.astype(BF16)
    square = pick(dot(spread_all(gram), gram_b))

    lane_row = iota((1, LANES), 1)
    on_diag = iota((cols, LANES), 1) % wide == iota((cols, LANES), 0) // LANES * span + iota((cols, LANES), 0) % span
    diagonal = jnp.where(on_diag, gram, 0.0)
    loads_of, largest_of = [], []
    for k in range(per):
        both = jnp.sum(diagonal[rows_at(k)] + diagonal[rows_at(per + k)], axis=0, keepdims=True)
        traces = [jnp.sum(jnp.where(lane_row // wide == g, both, 0.0), axis=1, keepdims=True) for g in range(groups)]
        loads_of.append(jnp.where(lane_row < wide, traces[0], traces[1]))
        largest_of.append(jnp.where(lane_row < wide, kept["largest"][0][k], kept["largest"][1][k]))
    load = (0.1 / antennas * 0.5) * jnp.concatenate(loads_of * nj, 0)
    bound = jnp.concatenate(largest_of * nj, 0) + load
    inv = 1.0 / bound
    r = 1.0 - load * inv
    r2 = r * r
    r4 = r2 * r2
    s = [1.0 + 0.0 * r]
    for _ in range(TERMS - 1):
        s.append(1.0 + r * s[-1])
    c = [s[TERMS - 2 - m] for m in range(TERMS - 1)]
    t0 = c[4] + r * (c[5] + r * c[6])
    p0 = c[0] + r * (c[1] + r * (c[2] + r * c[3])) + r4 * t0

    def by(v, count=cols):
        return jnp.concatenate([jnp.broadcast_to(v[i : i + 1], (span, LANES)) for i in range(count // span)], 0)

    x1 = by(inv) * gram
    x2 = by(2.0 * r) * x1 - by(inv * inv) * square
    out = dot(spread_all(x2), jnp.concatenate([x1.astype(BF16), x2.astype(BF16)], 1))
    x3 = by(r) * x2 + by(r2) * x1 - pick(out[:, :LANES])
    x4 = by(2.0 * r2) * x2 - pick(out[:, LANES:])
    tail = by(c[5]) * x1 + by(c[6]) * x2
    head = x1 + x2 + x3
    out = dot(spread_all(x4), jnp.concatenate([tail.astype(BF16), head.astype(BF16)], 1))
    poly = (by(c[1] + r4 * c[5]) * x1 + by(c[2] + r4 * c[6]) * x2 + by(c[3]) * x3 + by(t0) * x4
            - pick(out[:, :LANES]))
    own = (by(1.0 + r4, LANES) * head[:LANES] + by(s[3], LANES) * x4[:LANES]
           - jnp.where(first[:LANES], out[:LANES, LANES:], out[cols : cols + LANES, LANES:]))
    own_low = own - own.astype(BF16).astype(F32)

    for g in range(groups):
        zt, zjt = kept["pt"][g]
        pt = dot(zt, steer_ref[0], NT) + dot(zjt, steer_ref[1], NT)
        pth, ptl = split(pt)
        oh = spread(own, g)
        ends = dot(jnp.concatenate([spread(poly, g), oh, spread(own_low, g)], 0), pth)
        back = (ends[cols : cols + LANES] + ends[cols + LANES :]) + dot(oh, ptl)
        for k in range(per):
            energy = 0.0
            at = slice(k, k + 1), slice(g * wide, g * wide + 1)
            for j in range(nj):
                low = rows_at(j * per + k)
                energy += jnp.sum(pt[low] * (p0[at] * pt[low] - ends[low]), axis=0, keepdims=True)
            whole = s[TERMS - 1][at]
            response = antennas * whole - energy * inv[at]
            factor = lax.rsqrt(response * (bound[at] * (1.0 / (nj * t_loc))))
            beam = (whole * pt[rows_at(k)] - back[rows_at(k)]) * factor
            beam = beam.astype(BF16)
            out_ref[0, g * per + k] = beam[:t_loc]
            out_ref[1, g * per + k] = beam[t_loc:]

    sized(send_ref.at[: antennas - nl], 0).wait_send()
    sized(send_ref, 1).wait_send()


def fused_local(ni, nj, samples, steer_index):
    _, nl, t_loc, _ = samples.shape
    beams, antennas = steer_index.shape
    size = 2 * CH_DEV * t_loc
    vmem = pl.BlockSpec(memory_space=pltpu.VMEM)
    table = jnp.asarray(taper_table(CH_DEV * ni))
    out = pl.pallas_call(
        functools.partial(fused, ni, nj),
        out_shape=pltpu.VMEM((2, CH_DEV, t_loc, beams), BF16),
        in_specs=[pl.BlockSpec(memory_space=pl.ANY)] * 3,
        out_specs=vmem,
        scratch_shapes=[
            pltpu.VMEM((2, nl * t_loc, C), BF16),
            pltpu.VMEM(table.shape, BF16),
            pltpu.VMEM((beams, antennas), jnp.int32),
            pltpu.VMEM((nl * t_loc, CH_DEV * ni), F32),
            pltpu.VMEM((nl * t_loc, CH_DEV * ni), F32),
            pltpu.VMEM((antennas, size), BF16),
            pltpu.VMEM((nj, antennas, size), BF16),
            pltpu.VMEM((2, beams, antennas), BF16),
            pltpu.SemaphoreType.DMA((4,)),
            pltpu.SemaphoreType.DMA,
            pltpu.SemaphoreType.DMA((nj,)),
            pltpu.SemaphoreType.REGULAR((2,)),
        ],
        compiler_params=pltpu.CompilerParams(collective_id=0, has_side_effects=True),
    )(samples.reshape(2, nl * t_loc, C), table, steer_index)
    return jnp.transpose(out, (0, 1, 3, 2))


def choose(ni, nj, samples, steer_index):
    _, nl, t_loc, _ = samples.shape
    beams, antennas = steer_index.shape
    tiled = nl == 16 and t_loc == 16 and CH_DEV * ni == LANES and antennas == nl * ni
    if tiled and nj == 2:
        return fused_local(ni, nj, samples, steer_index)
    return local(samples, steer_index)


def solution(mesh):
    return jax.shard_map(
        functools.partial(choose, mesh.shape["chan"], mesh.shape["tm"]),
        mesh=mesh,
        in_specs=(P(None, "chan", "tm", None), P()),
        out_specs=P(None, "chan", None, "tm"),
        check_vma=False,
    )
```

```python
import functools
import itertools
import math

import jax
import jax.numpy as jnp
import numpy as np
from jax import lax
from jax.experimental import pallas as pl
from jax.experimental.pallas import tpu as pltpu
from jax.sharding import PartitionSpec as P

C = 1024
PHASES = 256
CH_DEV = 8
ITERS = 3
TERMS = 2**ITERS
LANES = 128


HIGHEST = lax.Precision.HIGHEST
F32 = jnp.float32
BF16 = jnp.bfloat16
NT = (((1,), (1,)), ((), ()))


def transform_table(channels_all):
    offset = (C - channels_all) // 2
    channel_number = jnp.arange(channels_all, dtype=jnp.int32) + offset
    sample_number = jnp.arange(C, dtype=jnp.int32)
    phase_turns = channel_number[:, None] * sample_number[None, :] % C
    phase_angle = 2.0 * math.pi / C * phase_turns.astype(jnp.float32)
    window_taper = (
        0.5 - 0.5 * jnp.cos(2.0 * math.pi / C * sample_number.astype(jnp.float32))
    ) / math.sqrt(C)
    cosine = window_taper[None, :] * jnp.cos(phase_angle)
    sine_part = window_taper[None, :] * jnp.sin(phase_angle)
    coefficients = jnp.stack(
        [jnp.stack([cosine, sine_part], 1), jnp.stack([-sine_part, cosine], 1)], 0
    )
    return coefficients.astype(jnp.bfloat16)


def complex_product(left_real, left_imag, right_real, right_imag):
    real_part = jnp.dot(left_real, right_real, precision=HIGHEST) - jnp.dot(
        left_imag, right_imag, precision=HIGHEST
    )
    imag_part = jnp.dot(left_real, right_imag, precision=HIGHEST) + jnp.dot(
        left_imag, right_real, precision=HIGHEST
    )
    return (real_part, imag_part)


def invert_loaded(covariance_real, covariance_imag):
    matrix_order = covariance_real.shape[0]
    loading = 0.1 * jnp.mean(jnp.diagonal(covariance_real))
    identity = jnp.eye(matrix_order, dtype=jnp.float32)
    loaded = covariance_real + loading * identity
    magnitude = jnp.sqrt(loaded * loaded + covariance_imag * covariance_imag)
    largest = jnp.max(jnp.sum(magnitude, axis=1))

    def iterate(counter, state):
        approx_real, approx_imag = state
        image_real, image_imag = complex_product(loaded, covariance_imag, approx_real, approx_imag)
        square_real, square_imag = complex_product(approx_real, approx_imag, image_real, image_imag)
        return (2.0 * approx_real - square_real, 2.0 * approx_imag - square_imag)

    start_state = (identity / largest, jnp.zeros_like(identity))
    return lax.fori_loop(0, ITERS, iterate, start_state)


def form_weights(covariance_real, covariance_imag, steer_real, steer_imag):
    inverse_real, inverse_imag = invert_loaded(covariance_real, covariance_imag)
    gain_real, gain_imag = complex_product(inverse_real, inverse_imag, steer_real, steer_imag)
    response = jnp.sum(steer_real * gain_real + steer_imag * gain_imag, axis=0)
    factor = lax.rsqrt(response)
    return ((gain_real * factor).astype(jnp.bfloat16), (gain_imag * factor).astype(jnp.bfloat16))


def weights_stacked(covariance_real, covariance_imag, steer_real, steer_imag):
    weight_real, weight_imag = jax.vmap(form_weights, in_axes=(0, 0, None, None))(
        covariance_real, covariance_imag, steer_real, steer_imag
    )
    return jnp.stack([weight_real, weight_imag], 1)


def steering(steer_index):
    phase_angle = 2.0 * math.pi / PHASES * steer_index.astype(jnp.float32)
    return (jnp.cos(phase_angle).T, jnp.sin(phase_angle).T)


def apply_beams(weight_pair, spectrum):
    real_weight = weight_pair[:, 0]
    imag_weight = weight_pair[:, 1]
    beam_real = jnp.einsum(
        "knb,kns->kbs", real_weight, spectrum[0], preferred_element_type=jnp.float32
    ) + jnp.einsum("knb,kns->kbs", imag_weight, spectrum[1], preferred_element_type=jnp.float32)
    beam_imag = jnp.einsum(
        "knb,kns->kbs", real_weight, spectrum[1], preferred_element_type=jnp.float32
    ) - jnp.einsum("knb,kns->kbs", imag_weight, spectrum[0], preferred_element_type=jnp.float32)
    return jnp.stack([beam_real, beam_imag], 0).astype(jnp.bfloat16)


def local(samples, steer_index):
    channels_all = CH_DEV * lax.axis_size("chan")
    coefficients = transform_table(channels_all)
    spectra = lax.dot_general(
        coefficients, samples, (((2, 3), (0, 3)), ((), ())), preferred_element_type=jnp.float32
    ).astype(jnp.bfloat16)
    steer_real, steer_imag = steering(steer_index)
    turned = lax.all_to_all(
        lax.all_to_all(spectra, "chan", split_axis=1, concat_axis=2, tiled=True),
        "tm",
        split_axis=1,
        concat_axis=3,
        tiled=True,
    )
    outer_sums = jnp.einsum("ikns,jkms->kinjm", turned, turned, preferred_element_type=jnp.float32)
    snapshots = turned.shape[3]
    covariance_real = (outer_sums[:, 0, :, 0, :] + outer_sums[:, 1, :, 1, :]) / snapshots
    covariance_imag = (outer_sums[:, 1, :, 0, :] - outer_sums[:, 0, :, 1, :]) / snapshots
    weight_pair = weights_stacked(covariance_real, covariance_imag, steer_real, steer_imag)
    local_beams = apply_beams(weight_pair, turned)
    return lax.all_to_all(local_beams, "tm", split_axis=3, concat_axis=1, tiled=True)


def taper_table(channels_all):
    offset = (C - channels_all) // 2
    channel = np.arange(channels_all) + offset
    sample = np.arange(C)
    angle = 2.0 * math.pi / C * (channel[None, :] * sample[:, None] % C)
    taper = (0.5 - 0.5 * np.cos(2.0 * math.pi / C * sample)) / math.sqrt(C)
    both = np.concatenate([taper[:, None] * np.cos(angle), taper[:, None] * np.sin(angle)], 1)
    return both.astype(np.float32).astype(BF16)


def iota(shape, axis):
    return lax.broadcasted_iota(jnp.int32, shape, axis)


def dot(a, b, dims=(((1,), (0,)), ((), ()))):
    return lax.dot_general(a, b, dims, preferred_element_type=F32)


def split(x):
    high = x.astype(BF16)
    return high, (x - high.astype(F32)).astype(BF16)


def exchange_blocks(rows, count, width):
    place = iota(rows[0].shape, 1) // width
    turned = [rows[0]] + [pltpu.roll(rows[t], t * width, 1) for t in range(1, count)]
    rows = [turned[-i % count] for i in range(count)]
    step = 1
    while step < count:
        take = place & step != 0
        rows = [jnp.where(take, rows[i - step], rows[i]) for i in range(count)]
        step *= 2
    return rows


def steering_parts(index):
    turn = index & (PHASES - 1)
    quarter = PHASES // 4
    quadrant = (turn + quarter // 2) // quarter
    x = (turn - quarter * quadrant).astype(F32) * (2.0 * math.pi / PHASES)
    y = x * x
    s = x * (1.0 + y * (-1.0 / 6 + y * (1.0 / 120 + y * (-1.0 / 5040 + y * (1.0 / 362880)))))
    c = 1.0 + y * (-0.5 + y * (1.0 / 24 + y * (-1.0 / 720 + y * (1.0 / 40320 - y * (1.0 / 3628800)))))
    odd = quadrant & 1 == 1
    flip_c = (quadrant + 1) & 2 == 2
    flip_s = quadrant & 2 == 2
    cosine = jnp.where(odd, s, c)
    sine = jnp.where(odd, c, s)
    return jnp.where(flip_c, -cosine, cosine), jnp.where(flip_s, -sine, sine)


def fused(ni, nj, samples_hbm, table_hbm, index_hbm, out_ref, samples_ref, table_ref, index_ref, re_ref,
          im_ref, send_ref, recv_ref, steer_ref, load_sem, send_sem, recv_sem, told):
    nl, t_loc, q = 16, 16, 2 * CH_DEV
    antennas = ni * nl
    size = q * t_loc
    my_i, my_j = lax.axis_index("chan"), lax.axis_index("tm")
    other_j = 1 - my_j

    loads = [pltpu.make_async_copy(src, dst, load_sem.at[i]) for i, (src, dst) in enumerate(
        [(table_hbm, table_ref), (samples_hbm.at[0], samples_ref.at[0]),
         (samples_hbm.at[1], samples_ref.at[1]), (index_hbm, index_ref)])]
    for load in loads[:3]:
        load.start()

    barrier = pltpu.get_barrier_semaphore()

    def after(step):
        ahead = my_i + step
        return jnp.where(ahead >= ni, ahead - ni, ahead)

    def around(body):
        lax.fori_loop(1, ni, lambda step, carry: (body(step), carry)[1], 0)

    def greet(peer_i, peer_j):
        pl.semaphore_signal(barrier, inc=1, device_id=(peer_i, peer_j),
                            device_id_type=pl.DeviceIdType.MESH)

    greet(my_i, other_j)

    level = ni // 4
    my_level = my_i // level

    def greet_both(step):
        peer = after(step)
        near = (peer >= 2 * level) | (my_level <= peer // level + 1)

        @pl.when(near)
        def _():
            greet(peer, my_j)
            greet(peer, other_j)

    around(greet_both)

    loads[0].wait()
    loads[1].wait()
    loads[2].wait()
    loads[3].start()
    table = table_ref[...]
    half = table.shape[1] // 2
    first = dot(samples_ref[0], table)
    second = dot(samples_ref[1], table)
    re_ref[...] = first[:, :half] + second[:, half:]
    im_ref[...] = second[:, :half] - first[:, half:]
    parts = []
    for ref in (re_ref, im_ref):
        rows = [ref[pl.ds(t, nl, stride=t_loc), :].astype(BF16) for t in range(t_loc)]
        parts.append(exchange_blocks(rows, ni, CH_DEV))
    send_ref[...] = jnp.concatenate([jnp.concatenate([a, b], 1) for a, b in zip(*parts)], 0)

    pl.semaphore_wait(barrier, jnp.minimum(my_level + 2, 4) * (level * nj) - 1)

    def tell(distance, which):
        pl.semaphore_signal(told.at[which], inc=1, device_id=(my_i - distance * level, my_j),
                            device_id_type=pl.DeviceIdType.MESH)

    @pl.when(my_level == 1)
    def _():
        tell(1, 0)

    @pl.when(my_level == 2)
    def _():
        tell(2, 1)
        tell(1, 1)

    rows_of = lambda i: pl.ds(pl.multiple_of(i * nl, nl), nl)
    mine = rows_of(my_i)

    def peer_of(step):
        if isinstance(step, int) and step == 0:
            return my_i
        begin = jnp.where(my_level == 2, 2, jnp.where(my_level == 1, 11, jnp.where(my_level == 0, 0, 3)))
        usual = lax.rem(step - 3 + begin, 13) + 1
        usual = jnp.where(usual >= ni - my_i, usual + 2, usual)
        moved = jnp.where(step <= 2, step - 1, lax.rem(my_i + usual, ni))
        return jnp.where((my_i >= 2) & (my_i < 16), moved, after(step))

    def block_copy(step, origin, plane):
        peer = peer_of(step)
        return pltpu.make_async_remote_copy(
            src_ref=send_ref.at[rows_of(peer), :],
            dst_ref=recv_ref.at[plane, rows_of(origin), :],
            send_sem=send_sem,
            recv_sem=recv_sem.at[plane],
            device_id=(peer, other_j if plane else my_j),
            device_id_type=pl.DeviceIdType.MESH,
        )

    def send(step):
        peer = peer_of(step)

        @pl.when((my_level == 0) & (peer == 2 * level))
        def _():
            pl.semaphore_wait(told.at[0], 1)

        @pl.when((my_level <= 1) & (peer == 3 * level))
        def _():
            pl.semaphore_wait(told.at[1], 1)

        block_copy(step, my_i, 1).start()
        block_copy(step, my_i, 0).start()

    block_copy(0, my_i, 1).start()
    around(send)
    recv_ref[0, mine, :] = send_ref[mine, :]

    loads[3].wait()
    cosine, sine = steering_parts(index_ref[...])
    steer_ref[0] = cosine.astype(BF16)
    steer_ref[1] = sine.astype(BF16)

    span = 2 * t_loc
    row_id, col_id = iota((size, size), 0), iota((size, size), 1)

    def source(column):
        shift = (column % t_loc + my_i) % t_loc
        return column // t_loc % 2 * (t_loc * CH_DEV) + shift * CH_DEV + column // span

    order = jnp.where(row_id == source(col_id), 1.0, 0.0).astype(BF16)
    order_t = jnp.where(col_id == source(row_id), 1.0, 0.0).astype(BF16)
    order_j = jnp.where(row_id == source(col_id ^ t_loc), jnp.where(col_id & t_loc == 0, 1.0, -1.0), 0.0).astype(BF16)

    def sized(ref, plane):
        return pltpu.make_async_remote_copy(
            src_ref=ref, dst_ref=ref, send_sem=send_sem, recv_sem=recv_sem.at[plane],
            device_id=(my_i, other_j), device_id_type=pl.DeviceIdType.MESH)

    sized(recv_ref.at[0, : antennas - nl], 0).wait_recv()
    sized(recv_ref.at[1], 1).wait_recv()
    held = jnp.concatenate([recv_ref[j] for j in range(nj)], 0)
    both = dot(held, jnp.concatenate([order, order_j], 1)).astype(BF16)
    planes = []
    for j in range(nj):
        part = both[j * antennas : (j + 1) * antennas]
        zt = dot(order_t, recv_ref[j], NT).astype(BF16)
        zjt = jnp.concatenate(
            [b for i in range(size // span) for b in
             (zt[i * span + t_loc : (i + 1) * span], -zt[i * span : i * span + t_loc])], 0)
        planes.append((part[:, :size], zt, part[:, size:], zjt))

    groups = size // LANES
    per = CH_DEV // groups
    cols = nj * LANES
    wide = nj * span
    chan_of = lambda x: x // span % per
    lane_chan = chan_of(iota((1, cols), 1))
    half_ants = antennas // 2
    blocks = range(cols // span)
    rows_at = lambda i: slice(i * span, (i + 1) * span)
    lane = iota((span, LANES), 1)
    slot = lane // span
    packed_slot = iota((span, LANES), 1) // span
    first = iota((cols, LANES), 1) < wide

    def shifted(x, amount):
        return x if amount % LANES == 0 else pltpu.roll(x, amount % LANES, 1)

    def pack(grams):
        done = []
        for i in blocks:
            kept = None
            for g in range(groups):
                for j in range(nj):
                    to = g * nj + j
                    moved = shifted(grams[g][rows_at(i), j * LANES : (j + 1) * LANES], (to - i % per) * span)
                    kept = moved if kept is None else jnp.where(slot == to, moved, kept)
            done.append(kept)
        return jnp.concatenate(done, 0)

    def spread(x, g):
        x = x.astype(BF16)
        done = []
        for i in range(x.shape[0] // span):
            k = i % per
            done.append(jnp.concatenate(
                [jnp.where(packed_slot == k, shifted(x[rows_at(i)], (k - g * nj - j) * span), jnp.zeros((), BF16))
                 for j in range(nj)], 1))
        return jnp.concatenate(done, 0)

    def spread_all(x):
        return jnp.concatenate([spread(x, g) for g in range(groups)], 0)

    def pick(out):
        return jnp.where(first, out[:cols], out[cols:])

    def only(x, k):
        none = jnp.zeros((span, antennas), BF16)
        return jnp.concatenate([x[rows_at(i)] if i % per == k else none for i in blocks], 0)

    def magnitude(re, im):
        power = re * re + im * im
        return power * lax.rsqrt(jnp.maximum(power, 1e-37))

    def group_steps(g, keepers):
        cut = slice(g * LANES, (g + 1) * LANES)
        z = jnp.concatenate([p[0][:, cut] for p in planes], 1)
        zj = jnp.concatenate([p[2][:, cut] for p in planes], 1)
        zt, zjt = (jnp.concatenate([p[i][cut] for p in planes], 0) for i in (1, 3))
        keepers["gram"][g] = dot(zt, z) + dot(zjt, zj)
        keepers["pt"][g] = zt, zjt
        low_t = jnp.concatenate([zt[:, half_ants:], zjt[:, half_ants:]], 1)
        upper = jnp.concatenate([z[:half_ants], zj[:half_ants]], 0)
        yield
        for k in range(per):
            yield
            top = dot(upper, only(zt, k))
            top = magnitude(top[:half_ants], top[half_ants:])
            low = dot(z[half_ants:], only(low_t, k))
            low = magnitude(low[:, :half_ants], low[:, half_ants:])
            rows = jnp.max(jnp.sum(top, axis=1, keepdims=True), axis=0, keepdims=True)
            columns = jnp.sum(top[:, half_ants:], axis=0, keepdims=True) + jnp.sum(low, axis=0, keepdims=True)
            keepers["largest"][g][k] = jnp.maximum(rows, jnp.max(columns, axis=1, keepdims=True))

    kept = {"gram": {}, "pt": {}, "largest": [{}, {}]}
    for _ in itertools.zip_longest(*[group_steps(g, kept) for g in range(groups)]):
        pass

    gram = pack(kept["gram"])
    gram_b = gram.astype(BF16)
    square = pick(dot(spread_all(gram), gram_b))

    lane_row = iota((1, LANES), 1)
    on_diag = iota((cols, LANES), 1) % wide == iota((cols, LANES), 0) // LANES * span + iota((cols, LANES), 0) % span
    diagonal = jnp.where(on_diag, gram, 0.0)
    loads_of, largest_of = [], []
    for k in range(per):
        both = jnp.sum(diagonal[rows_at(k)] + diagonal[rows_at(per + k)], axis=0, keepdims=True)
        traces = [jnp.sum(jnp.where(lane_row // wide == g, both, 0.0), axis=1, keepdims=True) for g in range(groups)]
        loads_of.append(jnp.where(lane_row < wide, traces[0], traces[1]))
        largest_of.append(jnp.where(lane_row < wide, kept["largest"][0][k], kept["largest"][1][k]))
    load = (0.1 / antennas * 0.5) * jnp.concatenate(loads_of * nj, 0)
    bound = jnp.concatenate(largest_of * nj, 0) + load
    inv = 1.0 / bound
    r = 1.0 - load * inv
    r2 = r * r
    r4 = r2 * r2
    s = [1.0 + 0.0 * r]
    for _ in range(TERMS - 1):
        s.append(1.0 + r * s[-1])
    c = [s[TERMS - 2 - m] for m in range(TERMS - 1)]
    t0 = c[4] + r * (c[5] + r * c[6])
    p0 = c[0] + r * (c[1] + r * (c[2] + r * c[3])) + r4 * t0

    def by(v, count=cols):
        return jnp.concatenate([jnp.broadcast_to(v[i : i + 1], (span, LANES)) for i in range(count // span)], 0)

    x1 = by(inv) * gram
    x2 = by(2.0 * r) * x1 - by(inv * inv) * square
    out = dot(spread_all(x2), jnp.concatenate([x1.astype(BF16), x2.astype(BF16)], 1))
    x3 = by(r) * x2 + by(r2) * x1 - pick(out[:, :LANES])
    x4 = by(2.0 * r2) * x2 - pick(out[:, LANES:])
    tail = by(c[5]) * x1 + by(c[6]) * x2
    head = x1 + x2 + x3
    out = dot(spread_all(x4), jnp.concatenate([tail.astype(BF16), head.astype(BF16)], 1))
    poly = (by(c[1] + r4 * c[5]) * x1 + by(c[2] + r4 * c[6]) * x2 + by(c[3]) * x3 + by(t0) * x4
            - pick(out[:, :LANES]))
    own = (by(1.0 + r4, LANES) * head[:LANES] + by(s[3], LANES) * x4[:LANES]
           - jnp.where(first[:LANES], out[:LANES, LANES:], out[cols : cols + LANES, LANES:]))
    own_low = own - own.astype(BF16).astype(F32)

    for g in range(groups):
        zt, zjt = kept["pt"][g]
        pt = dot(zt, steer_ref[0], NT) + dot(zjt, steer_ref[1], NT)
        pth, ptl = split(pt)
        oh = spread(own, g)
        ends = dot(jnp.concatenate([spread(poly, g), oh, spread(own_low, g)], 0), pth)
        back = (ends[cols : cols + LANES] + ends[cols + LANES :]) + dot(oh, ptl)
        for k in range(per):
            energy = 0.0
            at = slice(k, k + 1), slice(g * wide, g * wide + 1)
            for j in range(nj):
                low = rows_at(j * per + k)
                energy += jnp.sum(pt[low] * (p0[at] * pt[low] - ends[low]), axis=0, keepdims=True)
            whole = s[TERMS - 1][at]
            response = antennas * whole - energy * inv[at]
            factor = lax.rsqrt(response * (bound[at] * (1.0 / (nj * t_loc))))
            beam = (whole * pt[rows_at(k)] - back[rows_at(k)]) * factor
            beam = beam.astype(BF16)
            out_ref[0, g * per + k] = beam[:t_loc]
            out_ref[1, g * per + k] = beam[t_loc:]

    sized(send_ref.at[: antennas - nl], 0).wait_send()
    sized(send_ref, 1).wait_send()


def fused_local(ni, nj, samples, steer_index):
    _, nl, t_loc, _ = samples.shape
    beams, antennas = steer_index.shape
    size = 2 * CH_DEV * t_loc
    vmem = pl.BlockSpec(memory_space=pltpu.VMEM)
    table = jnp.asarray(taper_table(CH_DEV * ni))
    out = pl.pallas_call(
        functools.partial(fused, ni, nj),
        out_shape=pltpu.VMEM((2, CH_DEV, t_loc, beams), BF16),
        in_specs=[pl.BlockSpec(memory_space=pl.ANY)] * 3,
        out_specs=vmem,
        scratch_shapes=[
            pltpu.VMEM((2, nl * t_loc, C), BF16),
            pltpu.VMEM(table.shape, BF16),
            pltpu.VMEM((beams, antennas), jnp.int32),
            pltpu.VMEM((nl * t_loc, CH_DEV * ni), F32),
            pltpu.VMEM((nl * t_loc, CH_DEV * ni), F32),
            pltpu.VMEM((antennas, size), BF16),
            pltpu.VMEM((nj, antennas, size), BF16),
            pltpu.VMEM((2, beams, antennas), BF16),
            pltpu.SemaphoreType.DMA((4,)),
            pltpu.SemaphoreType.DMA,
            pltpu.SemaphoreType.DMA((nj,)),
            pltpu.SemaphoreType.REGULAR((2,)),
        ],
        compiler_params=pltpu.CompilerParams(collective_id=0, has_side_effects=True),
    )(samples.reshape(2, nl * t_loc, C), table, steer_index)
    return jnp.transpose(out, (0, 1, 3, 2))


def choose(ni, nj, samples, steer_index):
    _, nl, t_loc, _ = samples.shape
    beams, antennas = steer_index.shape
    tiled = nl == 16 and t_loc == 16 and CH_DEV * ni == LANES and antennas == nl * ni
    if tiled and nj == 2:
        return fused_local(ni, nj, samples, steer_index)
    return local(samples, steer_index)


def solution(mesh):
    return jax.shard_map(
        functools.partial(choose, mesh.shape["chan"], mesh.shape["tm"]),
        mesh=mesh,
        in_specs=(P(None, "chan", "tm", None), P()),
        out_specs=P(None, "chan", None, "tm"),
        check_vma=False,
    )
```
